32 devices in a mesh: row: 8 (over y, x, core), col: 4 (over z).
Axes of the slice: x: 2, y: 2, z: 4, core: 2. Of those that a mesh axis runs over, the one named last changes fastest.
Arguments:
- classes: int32 [128, 64], P('row', 'col'), may hold values from 0 to 15
- features: bfloat16 [128, 64, 128], P('row', 'col'), may hold values from -6 to 6
- cotangent: bfloat16 [128, 64, 128], P('row', 'col'), may hold values from -6 to 6
- table: float32 [16, 128], replicated, may hold values from -6 to 6
- norm_gain: float32 [128], replicated, may hold values from 0.5 to 1.5
- in_weight: bfloat16 [128, 512], replicated, may hold values from -0.5 to 0.5
- scan_weight: bfloat16 [256, 160], replicated, may hold values from -0.375 to 0.375
- step_weight: float32 [4, 8, 256], replicated, may hold values from -2 to 2
- step_bias: float32 [4, 256], replicated, may hold values from -6 to -2.5
- decay_log: float32 [4, 16, 256], replicated, may hold values from -4 to 2
- skip_gain: float32 [4, 256], replicated, may hold values from 0.5 to 1.5
- output_gain: float32 [256], replicated, may hold values from 0.5 to 1.5
- output_weight: bfloat16 [256, 128], replicated, may hold values from -0.375 to 0.375
Outputs:
- feature_grad: bfloat16 [128, 64, 128], P('row', 'col')
- in_weight_grad: float32 [128, 512], replicated
- scan_weight_grad: float32 [256, 160], replicated
- step_weight_grad: float32 [4, 8, 256], replicated
- step_bias_grad: float32 [4, 256], replicated
- decay_log_grad: float32 [4, 16, 256], replicated
- skip_gain_grad: float32 [4, 256], replicated
- norm_gain_grad: float32 [128], replicated
- output_gain_grad: float32 [256], replicated
- output_weight_grad: float32 [256, 128], replicated
The draws below stay inside these ranges and needn't reach their ends.
All inputs are finite; a program needn't handle non-finite values.
Results may differ from the reference program's by a relative error of at most 0.0076.
Values sent between devices are 32-bit elements; how exact they have to be, the bound alone decides.
A program may use at most 320 MiB of HBM per device.

```python
import math
import jax
import jax.numpy as jnp
import numpy as np
from jax import lax

D = 128
E = 256
STATE = 16
RANK = 8
CLASSES = 16
TILE = 16
HEIGHT = 128
WIDTH = 64
TOKENS = 8192


def touch_ends(drawn, rng, least, high):
    index_at = [jax.random.randint(jax.random.fold_in(rng, axis), (), 0, length) for axis, length in enumerate(drawn.shape)]
    widest = drawn.shape.index(max(drawn.shape))
    beside = index_at[:widest] + [(index_at[widest] + 1) % drawn.shape[widest]] + index_at[widest + 1:]
    return drawn.at[tuple(index_at)].set(least).at[tuple(beside)].set(high)


def shard_levels(rng, shape, shards, low, largest):
    def one(position, parts):
        steps = jax.random.uniform(jax.random.fold_in(jax.random.fold_in(rng, 6), position), (parts,), jnp.float32, low / len(shards), largest / len(shards))
        return jnp.repeat(jnp.exp(steps), shape[position] // parts).reshape((-1,) + (1,) * (len(shape) - position - 1))

    level = one(*shards[0])
    for cut in shards[1:]:
        level = level * one(*cut)
    return level


def cumulative_ranks(amount, skew):
    portions = [(1 << 20) // math.isqrt(rank ** skew) + 1 for rank in range(1, amount + 1)]
    scale = 1 + sum(portions) // (1 << 30)
    return np.cumsum(np.array([max(1, weight // scale) for weight in portions]))


def skewed_ids(own_key, shape, count, lean):
    table = cumulative_ranks(count, lean)
    lot = jax.random.randint(jax.random.fold_in(own_key, 1), shape, 0, int(table[count - 1]))
    grade = jnp.searchsorted(jnp.asarray(table, jnp.int32), lot, side="right")
    return jax.random.permutation(jax.random.fold_in(own_key, 2), count)[grade].astype(jnp.int32)


def normal_values(stream_key, extent, scale, limit, split=(), held_as=jnp.bfloat16):
    values = jax.random.normal(stream_key, extent, jnp.float32) * scale
    if len(split) > 0:
        values = shard_levels(stream_key, extent, split, -0.22, 0.18) * values
    return jnp.clip(values, min=-limit, max=limit).astype(held_as)


def setup_inputs(seed: int = 0) -> dict:
    arg_keys = jax.random.split(jax.random.key(seed), 14)
    classes = touch_ends(skewed_ids(arg_keys[0], (HEIGHT, WIDTH), CLASSES, 2), jax.random.fold_in(arg_keys[0], 3), 0, CLASSES - 1).astype(jnp.int32)
    features = normal_values(arg_keys[1], (HEIGHT, WIDTH, D), 1.0, 6.0, ((0, 8), (1, 4)))
    cotangent = normal_values(arg_keys[2], (HEIGHT, WIDTH, D), 1.0, 6.0, ((0, 8), (1, 4)))
    table = normal_values(arg_keys[3], (CLASSES, D), 1.0, 6.0, (), jnp.float32)
    norm_gain = jnp.clip(1.0 + 0.1 * jax.random.normal(arg_keys[4], (D,), jnp.float32), 0.5, 1.5)
    in_weight = normal_values(arg_keys[5], (D, 2 * E), D ** -0.5, 0.5)
    scan_weight = normal_values(arg_keys[6], (E, 4 * (RANK + 2 * STATE)), E ** -0.5, 0.375)
    step_weight = normal_values(arg_keys[7], (4, RANK, E), RANK ** -0.5, 2.0, (), jnp.float32)
    step_bias = jnp.clip(jax.random.uniform(arg_keys[8], (4, E), jnp.float32, -6.0, -2.5), -6.0, -2.5)
    decay_log = jnp.clip(jax.random.uniform(arg_keys[9], (4, STATE, E), jnp.float32, -4.0, 2.0), -4.0, 2.0)
    skip_gain = jnp.clip(jax.random.uniform(arg_keys[10], (4, E), jnp.float32, 0.5, 1.5), 0.5, 1.5)
    output_gain = jnp.clip(1.0 + 0.1 * jax.random.normal(arg_keys[11], (E,), jnp.float32), 0.5, 1.5)
    output_weight = normal_values(arg_keys[12], (E, D), E ** -0.5, 0.375)
    return {"classes": classes, "features": features, "cotangent": cotangent, "table": table, "norm_gain": norm_gain, "in_weight": in_weight, "scan_weight": scan_weight, "step_weight": step_weight, "step_bias": step_bias, "decay_log": decay_log, "skip_gain": skip_gain, "output_gain": output_gain, "output_weight": output_weight}


EPS = 1e-05
HIGHEST = lax.Precision.HIGHEST

def layer_norm(rows, gain):
    average = lax.optimization_barrier(jnp.mean(rows, axis=-1, keepdims=True))
    centred = rows - average
    spread = lax.optimization_barrier(jnp.mean(centred * centred, axis=-1, keepdims=True))
    return centred * lax.rsqrt(spread + EPS) * gain

def silu_slope(before):
    sigma = jax.nn.sigmoid(before)
    return sigma * (1.0 + before * (1.0 - sigma))

def embed(features, classes, table):
    labels = jnp.arange(table.shape[0], dtype=jnp.int32)
    onehot = (classes[..., None] == labels).astype(jnp.float32)
    lookup = jnp.einsum('hwk,kd->hwd', onehot, table.astype(jnp.float32), precision=HIGHEST)
    return features.astype(jnp.float32) + lookup

def direction_inputs(projected, step_weight, step_bias):
    rank = step_weight.shape[1]
    group = projected.shape[1] // 4
    states = (group - rank) // 2
    steps, inflow, readout = ([], [], [])
    for direction in range(4):
        first = direction * group
        lowrank = projected[:, first:first + rank]
        before = jnp.dot(lowrank, step_weight[direction], precision=HIGHEST) + step_bias[direction]
        steps.append(jax.nn.softplus(before))
        inflow.append(projected[:, first + rank:first + rank + states])
        readout.append(projected[:, first + rank + states:first + group])
    return (jnp.stack(steps), jnp.stack(inflow), jnp.stack(readout))

def gate_output(total, gate_in, output_gain):
    return layer_norm(total, output_gain) * jax.nn.silu(gate_in)

def to_sequence(grid, direction):
    if direction < 2:
        grid = jnp.transpose(grid, (1, 0, 2))
    if direction % 2 == 1:
        grid = grid[::-1]
    return grid

def from_sequence(lines, direction):
    if direction % 2 == 1:
        lines = lines[::-1]
    if direction < 2:
        lines = jnp.transpose(lines, (1, 0, 2))
    return lines

def scan_lines(values, steps, inflow, readout, rate, skip, start):

    def advance(state, slab):
        value, step, source, probe = slab
        decay = jnp.exp(step[:, None, :] * rate)
        state = decay * state + source[:, :, None] * (step * value)[:, None, :]
        output = jnp.einsum('bn,bne->be', probe, state, precision=HIGHEST) + skip * value
        return (state, output)
    final, outputs = lax.scan(advance, start, (values, steps, inflow, readout))
    return (outputs, final)

def reference(classes, features, cotangent, table, norm_gain, in_weight, scan_weight, step_weight, step_bias, decay_log, skip_gain, output_gain, output_weight):
    height, width, model_width = features.shape
    inner = output_weight.shape[0]
    count = height * width
    grad_scale = float(TOKENS) ** (-0.5)
    embedded = embed(features, classes, table).reshape(count, model_width)
    normed = layer_norm(embedded, norm_gain).astype(jnp.bfloat16)
    mixed = jnp.dot(normed, in_weight, preferred_element_type=jnp.float32)
    values = jax.nn.silu(mixed[:, :inner]).astype(jnp.bfloat16)
    gate_in = mixed[:, inner:]
    projected = jnp.dot(values, scan_weight, preferred_element_type=jnp.float32)
    steps, inflow, readout = direction_inputs(projected, step_weight, step_bias)
    values_wide = values.astype(jnp.float32)

    def lines_of(flat, direction):
        return to_sequence(flat.reshape(height, width, flat.shape[-1]), direction)

    def flat_of(lines, direction):
        return from_sequence(lines, direction).reshape(count, lines.shape[-1])

    def run_lines(line_values, line_steps, line_inflow, line_readout, log_rate, skip):
        rate = -jnp.exp(log_rate)
        blocks = line_values.shape[0] // TILE

        def regroup(array):
            return array.reshape((blocks, TILE) + array.shape[1:])

        def block(state, slab):
            outputs, state = scan_lines(slab[0], slab[1], slab[2], slab[3], rate, skip, state)
            return (state, outputs)
        start = jnp.zeros((line_values.shape[1], rate.shape[0], rate.shape[1]), jnp.float32)
        unused, outputs = lax.scan(jax.checkpoint(block), start, (regroup(line_values), regroup(line_steps), regroup(line_inflow), regroup(line_readout)))
        return outputs.reshape(line_values.shape)
    total = jnp.zeros((count, inner), jnp.float32)
    pulls = []
    for direction in range(4):
        outputs, pull = jax.vjp(run_lines, lines_of(values_wide, direction), lines_of(steps[direction], direction), lines_of(inflow[direction], direction), lines_of(readout[direction], direction), decay_log[direction], skip_gain[direction])
        pulls.append(pull)
        total = total + flat_of(outputs, direction)
    gated = gate_output(total, gate_in, output_gain).astype(jnp.bfloat16)
    upstream = cotangent.reshape(count, model_width)
    output_weight_grad = jnp.dot(gated.T, upstream, preferred_element_type=jnp.float32)
    d_gated = jnp.dot(upstream, output_weight.T, preferred_element_type=jnp.float32)
    unused, gate_pull = jax.vjp(gate_output, total, gate_in, output_gain)
    d_total, d_gate_in, output_gain_grad = gate_pull(d_gated)
    d_values_scan = jnp.zeros((count, inner), jnp.float32)
    d_steps, d_inflow, d_readout, decay_grads, skip_grads = ([], [], [], [], [])
    for direction in range(4):
        grads = pulls[direction](lines_of(d_total, direction))
        d_values_scan = d_values_scan + flat_of(grads[0], direction)
        d_steps.append(flat_of(grads[1], direction))
        d_inflow.append(flat_of(grads[2], direction))
        d_readout.append(flat_of(grads[3], direction))
        decay_grads.append(grads[4])
        skip_grads.append(grads[5])
    unused, input_pull = jax.vjp(direction_inputs, projected, step_weight, step_bias)
    d_projected, step_weight_grad, step_bias_grad = input_pull((jnp.stack(d_steps), jnp.stack(d_inflow), jnp.stack(d_readout)))
    d_projected = d_projected.astype(jnp.bfloat16)
    scan_weight_grad = jnp.dot(values.T, d_projected, preferred_element_type=jnp.float32)
    d_values = jnp.dot(d_projected, scan_weight.T, preferred_element_type=jnp.float32) + d_values_scan
    d_mixed = jnp.concatenate([d_values * silu_slope(mixed[:, :inner]), d_gate_in], axis=1).astype(jnp.bfloat16)
    in_weight_grad = jnp.dot(normed.T, d_mixed, preferred_element_type=jnp.float32)
    d_normed = jnp.dot(d_mixed, in_weight.T, preferred_element_type=jnp.float32)
    unused, norm_pull = jax.vjp(layer_norm, embedded, norm_gain)
    d_embedded, norm_gain_grad = norm_pull(d_normed)
    feature_grad = (upstream.astype(jnp.float32) + d_embedded).astype(jnp.bfloat16).reshape(height, width, model_width)
    return (feature_grad, in_weight_grad * grad_scale, scan_weight_grad * grad_scale, step_weight_grad * grad_scale, step_bias_grad * grad_scale, jnp.stack(decay_grads) * grad_scale, jnp.stack(skip_grads) * grad_scale, norm_gain_grad * grad_scale, output_gain_grad * grad_scale, output_weight_grad * grad_scale)
```

```python
import functools
import math

import jax
import jax.numpy as jnp
from jax import lax
from jax.experimental import pallas as pl
from jax.experimental.pallas import tpu as pltpu
from jax.sharding import PartitionSpec as P

EPS = 1e-05
HIGHEST = lax.Precision.HIGHEST
MESH = pl.DeviceIdType.MESH
LANES = 128
SUB = 8
LOG2E = math.log2(math.e)
VMEM = pl.BlockSpec(memory_space=pltpu.VMEM)
BIG = 60 * 1024 * 1024


def layer_norm(rows, gain):
    average = jnp.mean(rows, axis=-1, keepdims=True)
    centred = rows - average
    spread = jnp.mean(centred * centred, axis=-1, keepdims=True)
    return centred * lax.rsqrt(spread + EPS) * gain


def silu_slope(before):
    sigma = jax.nn.sigmoid(before)
    return sigma * (1.0 + before * (1.0 - sigma))


def embed(features, classes, table):
    labels = jnp.arange(table.shape[0], dtype=jnp.int32)
    onehot = (classes[..., None] == labels).astype(jnp.float32)
    lookup = jnp.einsum("hwk,kd->hwd", onehot, table, precision=HIGHEST)
    return features.astype(jnp.float32) + lookup


def gate_output(total, gate_in, output_gain):
    return layer_norm(total, output_gain) * jax.nn.silu(gate_in)


def greet(axes):
    barrier = pltpu.get_barrier_semaphore()
    partners = 0
    for axis in axes:
        count = lax.axis_size(axis)
        me = lax.axis_index(axis)
        for d in range(1, count):
            pl.semaphore_signal(
                barrier, inc=1, device_id={axis: lax.rem(me + d, count)}, device_id_type=MESH
            )
            partners += 1
    pl.semaphore_wait(barrier, partners)


def half(ref, k, h, t):
    return ref[k, h, pl.ds(t, 1), :]


def walk(lines, tile, blocks, group, start, step):
    def outer(b, carry):
        def inner(j, carry):
            time = b * tile + j
            rising = b * (tile * lines) + j
            falling = (blocks - 1 - b) * (tile * lines) + (tile - 1 - j)
            tokens = [[base + line * tile for line in group] for base in (rising, falling)]
            return step(carry, tokens, time)

        return lax.fori_loop(0, tile, inner, carry, unroll=2)

    return lax.fori_loop(0, blocks, outer, start)


def groups_of(lines):
    size = 2 if lines % 2 == 0 else 1
    return [tuple(range(g, g + size)) for g in range(0, lines, size)]


def fold(ref, k, h, count):
    total = ref[k, h, pl.ds(0, count, stride=SUB), :]
    for s in range(1, SUB):
        total = total + ref[k, h, pl.ds(s, count, stride=SUB), :]
    return total


def softplus(x):
    return jnp.maximum(x, 0.0) + jnp.log1p(jnp.exp(-jnp.abs(x)))


def cross(a, b):
    return lax.dot_general(a, b, (((0,), (0,)), ((), ())), preferred_element_type=jnp.float32)


def back(a, b):
    return lax.dot_general(a, b, (((1,), (1,)), ((), ())), preferred_element_type=jnp.float32)


def general_kernel(
    tile_rows, tile_cols, states, rank, grad_scale, tiles,
    embedded_ref, upstream_ref, norm_gain_ref, in_weight_ref, scan_weight_ref, step_weight_ref,
    step_bias_ref, rate_ref, skip_ref, output_gain_ref, output_weight_ref,
    feature_ref, in_grad_ref, scan_grad_ref, stepw_ref, stepb_ref, dr_ref, skip_grad_ref,
    norm_grad_ref, gain_grad_ref, out_grad_ref,
    mixed, gate_grad, turn, along, down, wide, sv, steps, slope, low, hist, eight, pace8, up, dproj, dr_acc,
    mine0, from0, side0, all0, mine1, from1, side1, all1, sems, sumsems,
):
    count, inner = tile_rows * tile_cols, output_weight_ref.shape[0]
    rows, cols = lax.axis_size("row"), lax.axis_size("col")
    eh, nh = inner // LANES, states // SUB
    group = rank + 2 * states
    shapes = ((tile_rows // cols, tile_cols), (tile_cols // rows, tile_rows))
    boxes = (along, down)
    axes = ("col", "row")
    greet(("row", "col"))

    def post(turn_number, pair):
        axis, box = axes[pair], boxes[pair]
        size = lax.axis_size(axis)
        me = lax.axis_index(axis)
        copies = []
        for d in range(1, size):
            target = lax.rem(me + d, size)
            copy = pltpu.make_async_remote_copy(
                src_ref=box.at[2 * turn_number, target],
                dst_ref=box.at[2 * turn_number + 1, me],
                send_sem=sems.at[turn_number, pair, 0, d],
                recv_sem=sems.at[turn_number, pair, 1, d],
                device_id={axis: target},
                device_id_type=MESH,
            )
            copy.start()
            copies.append(copy)
        box[2 * turn_number + 1, me] = box[2 * turn_number, me]
        return copies

    def finish(copies):
        for copy in copies:
            copy.wait()

    def put_home(turn_number, x):
        along[2 * turn_number] = x.reshape(along.shape[1:])
        first = post(turn_number, 0)
        for h in range(eh):
            turn[h] = x[:, h * LANES : (h + 1) * LANES]
        per = tile_cols // rows
        for c in range(tile_cols):
            for h in range(eh):
                down[
                    2 * turn_number, c // per,
                    (c % per) * tile_rows : (c % per + 1) * tile_rows,
                    h * LANES : (h + 1) * LANES,
                ] = turn[h, pl.ds(c, tile_rows, stride=tile_cols), :]
        return first, post(turn_number, 1)

    def take_home(turn_number):
        per = tile_cols // rows
        for c in range(tile_cols):
            for h in range(eh):
                turn[h, pl.ds(c, tile_rows, stride=tile_cols), :] = down[
                    2 * turn_number + 1, c // per,
                    (c % per) * tile_rows : (c % per + 1) * tile_rows,
                    h * LANES : (h + 1) * LANES,
                ]
        here = along[2 * turn_number + 1].reshape(count, inner)
        return here + jnp.concatenate([turn[h] for h in range(eh)], axis=1)

    def lines_in(turn_number, pair):
        return boxes[pair][2 * turn_number + 1].reshape(count, inner)

    def lines_out(turn_number, pair, x):
        boxes[pair][2 * turn_number] = x.reshape(boxes[pair].shape[1:])
        return post(turn_number, pair)

    def rate_of(d, m, h):
        return rate_ref[d, m * SUB : (m + 1) * SUB, h * LANES : (h + 1) * LANES]

    def part(h):
        return slice(h * LANES, (h + 1) * LANES)

    zero = jnp.zeros((SUB, LANES), jnp.float32)

    sums = ((mine0, from0, side0, all0), (mine1, from1, side1, all1))
    fill = [0, 0]

    def put(lot, x):
        mine = sums[lot][0]
        per = mine.shape[1] // SUB
        for i in range(x.shape[0] // SUB):
            tile = fill[lot]
            at = (tile % per) * SUB
            mine[tile // per, at : at + SUB, :] = x[i * SUB : (i + 1) * SUB]
            fill[lot] += 1

    def put_wide(lot, x):
        for h in range(x.shape[1] // LANES):
            put(lot, x[:, h * LANES : (h + 1) * LANES])

    taken = [0, 0]

    def take(lot, height):
        full = sums[lot][3]
        per = full.shape[1] // SUB
        out = []
        for i in range(height // SUB):
            tile = taken[lot]
            at = (tile % per) * SUB
            out.append(full[tile // per, at : at + SUB, :])
            taken[lot] += 1
        return jnp.concatenate(out, axis=0) * grad_scale

    def take_wide(lot, height, width):
        return jnp.concatenate([take(lot, height) for h in range(width // LANES)], axis=1)

    def pad_rows(*rows_in):
        missing = -len(rows_in) % SUB
        return jnp.concatenate(list(rows_in) + [jnp.zeros((missing, LANES), jnp.float32)], axis=0)

    def pad_lot(lot):
        while fill[lot] < tiles[lot]:
            put(lot, zero)

    def spread(lot, phase, axis, source, result):
        size = lax.axis_size(axis)
        me = lax.axis_index(axis)
        copies = []
        for d in range(1, size):
            target = lax.rem(me + d, size)
            copy = pltpu.make_async_remote_copy(
                src_ref=source(target),
                dst_ref=result(me, d),
                send_sem=sumsems.at[lot, phase, 0, d],
                recv_sem=sumsems.at[lot, phase, 1, d],
                device_id={axis: target},
                device_id_type=MESH,
            )
            copy.start()
            copies.append(copy)
        return copies

    def sum_scatter(lot):
        mine, other, side, full = sums[lot]
        pad_lot(lot)
        return spread(lot, 0, "row", lambda t: mine.at[t], lambda me, d: other.at[d - 1])

    def sum_across(lot, copies):
        mine, other, side, full = sums[lot]
        finish(copies)
        acc = mine[lax.axis_index("row")]
        for d in range(rows - 1):
            acc = acc + other[d]
        me = lax.axis_index("col")
        side[me] = acc
        return spread(lot, 1, "col", lambda t: side.at[me], lambda m, d: side.at[m])

    def sum_gather(lot, copies):
        mine, other, side, full = sums[lot]
        finish(copies)
        acc = side[0]
        for d in range(1, cols):
            acc = acc + side[d]
        me = lax.axis_index("row")
        full[me] = acc
        return spread(lot, 2, "row", lambda t: full.at[me], lambda m, d: full.at[m])

    embedded = embedded_ref[...]
    normed = layer_norm(embedded, norm_gain_ref[...]).astype(jnp.bfloat16)
    mixed[...] = jnp.dot(normed, in_weight_ref[...], preferred_element_type=jnp.float32)
    values = jax.nn.silu(mixed[:, :inner]).astype(jnp.bfloat16).astype(jnp.float32)
    arriving = put_home(0, values)

    leaving = []
    for pair in range(2):
        lines, tile = shapes[pair]
        length = count // lines
        blocks = length // tile
        finish(arriving[pair])
        value = lines_in(0, pair)
        wide_p, sv_p, steps_p, hist_p = wide.at[pair], sv.at[pair], steps.at[pair], hist.at[pair]
        weight = scan_weight_ref[:, 2 * pair * group : 2 * (pair + 1) * group]
        projected = jnp.dot(
            value.astype(jnp.bfloat16), weight, preferred_element_type=jnp.float32
        )
        for k in range(2):
            d = 2 * pair + k
            lowrank = projected[:, k * group : k * group + rank]
            low[d] = lowrank
            before = (
                jnp.dot(
                    lowrank, step_weight_ref[d], precision=HIGHEST,
                    preferred_element_type=jnp.float32,
                )
                + step_bias_ref[d : d + 1, :]
            )
            slope[d] = jax.nn.sigmoid(before)
            pace = softplus(before)
            for h in range(eh):
                steps_p[k, h] = pace[:, part(h)]
                sv_p[k, h] = pace[:, part(h)] * value[:, part(h)]
            for which in range(2):
                for n in range(states):
                    col = k * group + rank + which * states + n
                    wide_p[k, which, pl.ds(n, count, stride=states), :] = jnp.broadcast_to(
                        projected[:, col : col + 1], (count, LANES)
                    )
            for h in range(eh):
                for line in range(lines):
                    at = line * (length + 1) * states
                    hist_p[k, h, at : at + states, :] = jnp.zeros((states, LANES), jnp.float32)
        for lot in groups_of(lines):

            def advance(carry, tokens, time):
                new = []
                i = 0
                for k in range(2):
                    for line, t in zip(lot, tokens[k]):
                        drive = [half(sv_p, k, h, t) for h in range(eh)]
                        pace = [half(steps_p, k, h, t) for h in range(eh)]
                        sums = [None] * eh
                        for m in range(nh):
                            at = pl.ds(pl.multiple_of(t * states + m * SUB, SUB), SUB)
                            slot = (line * (length + 1) + time + 1) * states + m * SUB
                            source = wide_p[k, 0, at, :]
                            probe = wide_p[k, 1, at, :]
                            for h in range(eh):
                                a = jnp.exp2(pace[h] * rate_of(2 * pair + k, m, h))
                                state = a * carry[i] + source * drive[h]
                                i += 1
                                hist_p[k, h, pl.ds(pl.multiple_of(slot, SUB), SUB), :] = state
                                new.append(state)
                                term = probe * state
                                sums[h] = term if sums[h] is None else sums[h] + term
                        for h in range(eh):
                            eight[k, h, pl.ds(pl.multiple_of(t * SUB, SUB), SUB), :] = sums[h]
                return tuple(new)

            walk(lines, tile, blocks, lot, (zero,) * (2 * len(lot) * eh * nh), advance)
        skip = skip_ref[2 * pair : 2 * pair + 1, :] + skip_ref[2 * pair + 1 : 2 * pair + 2, :]
        y = skip * value + jnp.concatenate(
            [fold(eight, 0, h, count) + fold(eight, 1, h, count) for h in range(eh)], axis=1
        )
        leaving.append(lines_out(1, pair, y))
    finish(leaving[0])
    finish(leaving[1])
    total = take_home(1)

    upstream = upstream_ref[...]
    gated, gate_pull = jax.vjp(gate_output, total, mixed[:, inner:], output_gain_ref[...])
    d_gated = back(upstream, output_weight_ref[...])
    d_total, d_gate_in, gain_grad = gate_pull(d_gated)
    arriving = put_home(2, d_total)
    gate_grad[...] = d_gate_in
    put(0, pad_rows(*[gain_grad[:, part(h)] for h in range(eh)]))
    put_wide(0, cross(gated.astype(jnp.bfloat16), upstream))

    leaving = []
    for pair in range(2):
        lines, tile = shapes[pair]
        length = count // lines
        blocks = length // tile
        finish(arriving[pair])
        g_all = lines_in(2, pair)
        wide_p, sv_p, steps_p, hist_p = wide.at[pair], sv.at[pair], steps.at[pair], hist.at[pair]
        for h in range(eh):
            up[0, h] = g_all[:, part(h)]
        for lot in groups_of(lines):

            def retreat(carry, tokens, time):
                grads, rates = carry
                rates = list(rates)
                new = []
                i = 0
                for k in range(2):
                    for line, t in zip(lot, tokens[1 - k]):
                        drive = [half(sv_p, k, h, t) for h in range(eh)]
                        pace = [half(steps_p, k, h, t) for h in range(eh)]
                        g = [half(up, 0, h, t) for h in range(eh)]
                        dd = [None] * eh
                        dp = [None] * eh
                        for m in range(nh):
                            at = pl.ds(pl.multiple_of(t * states + m * SUB, SUB), SUB)
                            slot = (line * (length + 1) + length - 1 - time) * states + m * SUB
                            earlier = pl.ds(pl.multiple_of(slot, SUB), SUB)
                            current = pl.ds(pl.multiple_of(slot + states, SUB), SUB)
                            source = wide_p[k, 0, at, :]
                            probe = wide_p[k, 1, at, :]
                            flow = None
                            read = None
                            for h in range(eh):
                                rate = rate_of(2 * pair + k, m, h)
                                grad = grads[i] + probe * g[h]
                                i += 1
                                term = grad * drive[h]
                                flow = term if flow is None else flow + term
                                term = g[h] * hist_p[k, h, current, :]
                                read = term if read is None else read + term
                                term = grad * source
                                dd[h] = term if dd[h] is None else dd[h] + term
                                carried = jnp.exp2(pace[h] * rate) * grad
                                q = carried * hist_p[k, h, earlier, :]
                                term = q * rate
                                dp[h] = term if dp[h] is None else dp[h] + term
                                j = (k * nh + m) * eh + h
                                rates[j] = rates[j] + q * pace[h]
                                new.append(carried)
                            wide_p[k, 0, at, :] = flow
                            wide_p[k, 1, at, :] = read
                        for h in range(eh):
                            at8 = pl.ds(pl.multiple_of(t * SUB, SUB), SUB)
                            eight[k, h, at8, :] = dd[h]
                            pace8[k, h, at8, :] = dp[h]
                return (tuple(new), tuple(rates))

            chains = 2 * len(lot) * eh * nh
            unused, rates = walk(
                lines, tile, blocks, lot, ((zero,) * chains, (zero,) * (2 * eh * nh)), retreat
            )
            for k in range(2):
                for m in range(nh):
                    for h in range(eh):
                        place = (2 * pair + k, slice(m * SUB, (m + 1) * SUB), part(h))
                        add = rates[(k * nh + m) * eh + h] * rate_ref[place] * (1.0 / LOG2E)
                        if lot[0] == 0:
                            dr_acc[place] = add
                        else:
                            dr_acc[place] += add
        value = lines_in(0, pair)
        g_all = lines_in(2, pair)
        skip = skip_ref[2 * pair : 2 * pair + 1, :] + skip_ref[2 * pair + 1 : 2 * pair + 2, :]
        dv = skip * g_all
        direct = jnp.sum(g_all * value, axis=0, keepdims=True)
        small = [direct[:, part(h)] for h in range(eh)]
        for k in range(2):
            d = 2 * pair + k
            drive = jnp.concatenate([fold(eight, k, h, count) for h in range(eh)], axis=1)
            pace = jnp.concatenate([fold(pace8, k, h, count) for h in range(eh)], axis=1)
            dv = dv + drive * jnp.concatenate([steps_p[k, h] for h in range(eh)], axis=1)
            d_before = (drive * value + pace * (1.0 / LOG2E)) * slope[d]
            bias_sum = jnp.sum(d_before, axis=0, keepdims=True)
            small += [bias_sum[:, part(h)] for h in range(eh)]
            put_wide(
                pair,
                lax.dot_general(
                    low[d], d_before, (((0,), (0,)), ((), ())), precision=HIGHEST,
                    preferred_element_type=jnp.float32,
                ),
            )
            put_wide(pair, dr_acc[d])
            dproj[:, k * group : k * group + rank] = lax.dot_general(
                d_before, step_weight_ref[d], (((1,), (1,)), ((), ())), precision=HIGHEST,
                preferred_element_type=jnp.float32,
            )
            lane = lax.broadcasted_iota(jnp.int32, (LANES, 2 * states), 1)
            flow = None
            for j in range(2 * states):
                x = wide_p[k, j // states, pl.ds(j % states, count, stride=states), :]
                pick = (lane == j).astype(jnp.bfloat16)
                term = jnp.dot(x.astype(jnp.bfloat16), pick, preferred_element_type=jnp.float32)
                flow = term if flow is None else flow + term
            dproj[:, k * group + rank : (k + 1) * group] = flow
        d_projected = dproj[...].astype(jnp.bfloat16)
        span = slice(2 * pair * group, 2 * (pair + 1) * group)
        leaving.append(lines_out(3, pair, back(d_projected, scan_weight_ref[:, span]) + dv))
        put(pair, pad_rows(*small))
        put_wide(pair, cross(d_projected, value.astype(jnp.bfloat16)))
        if pair == 0:
            early = sum_scatter(0)
        else:
            early = sum_across(0, early)
    finish(leaving[0])
    finish(leaving[1])
    d_values = take_home(3)
    early = sum_gather(0, early)

    d_mixed = jnp.concatenate(
        [d_values * silu_slope(mixed[:, :inner]), gate_grad[...]], axis=1
    ).astype(jnp.bfloat16)
    normed, norm_pull = jax.vjp(layer_norm, embedded_ref[...], norm_gain_ref[...])
    put_wide(1, cross(normed.astype(jnp.bfloat16), d_mixed))
    d_embedded, norm_grad = norm_pull(back(d_mixed, in_weight_ref[...]))
    put(1, pad_rows(norm_grad))
    late = sum_scatter(1)
    feature_ref[...] = (upstream_ref[...].astype(jnp.float32) + d_embedded).astype(jnp.bfloat16)
    late = sum_across(1, late)
    finish(early)
    late = sum_gather(1, late)

    def take_pair(pair):
        for d in (2 * pair, 2 * pair + 1):
            stepw_ref[d] = take_wide(pair, rank, inner)
            dr_ref[d] = take_wide(pair, states, inner)
        small = take(pair, -(-3 * eh // SUB) * SUB)
        for h in range(eh):
            for k in range(2):
                d = 2 * pair + k
                skip_grad_ref[d : d + 1, part(h)] = small[h : h + 1]
                stepb_ref[d : d + 1, part(h)] = small[(k + 1) * eh + h : (k + 1) * eh + h + 1]
        span = slice(2 * pair * group, 2 * (pair + 1) * group)
        scan_grad_ref[:, span] = take_wide(pair, 2 * group, inner).T

    small = take(0, SUB)
    for h in range(eh):
        gain_grad_ref[:, part(h)] = small[h : h + 1]
    out_grad_ref[...] = take_wide(0, inner, out_grad_ref.shape[1])
    take_pair(0)
    finish(late)
    take_pair(1)
    in_grad_ref[...] = take_wide(1, in_grad_ref.shape[0], in_grad_ref.shape[1])
    norm_grad_ref[...] = take(1, SUB)[0:1]


def general(
    classes, features, cotangent, table, norm_gain, in_weight, scan_weight, step_weight,
    step_bias, decay_log, skip_gain, output_gain, output_weight,
):
    tile_rows, tile_cols, model_width = features.shape
    inner = output_weight.shape[0]
    count = tile_rows * tile_cols
    rows, cols = lax.axis_size("row"), lax.axis_size("col")
    rank = step_weight.shape[1]
    states = decay_log.shape[1]
    group = rank + 2 * states
    eh = inner // LANES
    lines = max(tile_rows // cols, tile_cols // rows)
    grad_scale = float(count * rows * cols) ** (-0.5)
    rate2 = -jnp.exp(decay_log) * LOG2E
    embedded = embed(features, classes, table).reshape(count, model_width)
    f32 = jnp.float32
    shapes = [
        ((count, model_width), jnp.bfloat16),
        (in_weight.shape, f32),
        (scan_weight.shape, f32),
        (step_weight.shape, f32),
        (step_bias.shape, f32),
        (decay_log.shape, f32),
        (skip_gain.shape, f32),
        ((1, model_width), f32),
        ((1, inner), f32),
        (output_weight.shape, f32),
    ]
    scratch = [
        ((count, 2 * inner), f32),
        ((count, inner), f32),
        ((eh, count, LANES), f32),
        ((8, cols, count // cols, inner), f32),
        ((8, rows, count // rows, inner), f32),
        ((2, 2, 2, count * states, LANES), f32),
        ((2, 2, eh, count, LANES), f32),
        ((2, 2, eh, count, LANES), f32),
        ((4, count, inner), f32),
        ((4, count, rank), f32),
        ((2, 2, eh, (count + lines) * states, LANES), f32),
        ((2, eh, count * SUB, LANES), f32),
        ((2, eh, count * SUB, LANES), f32),
        ((1, eh, count, LANES), f32),
        ((count, 2 * group), f32),
        (decay_log.shape, f32),
    ]
    pair_tiles = eh * (2 * rank + 2 * states + 2 * group) // SUB + -(-3 * eh // SUB)
    least = (
        1 + inner * model_width // (LANES * SUB) + pair_tiles,
        1 + in_weight.size // (LANES * SUB) + pair_tiles,
    )
    tiles = tuple(-(-t // rows) * rows for t in least)
    for lot in range(2):
        chunk = (tiles[lot] // rows * SUB, LANES)
        scratch += [((rows,) + chunk, f32), ((rows - 1,) + chunk, f32), ((cols,) + chunk, f32), ((rows,) + chunk, f32)]
    feature_grad, *grads = pl.pallas_call(
        functools.partial(general_kernel, tile_rows, tile_cols, states, rank, grad_scale, tiles),
        out_shape=[jax.ShapeDtypeStruct(*s) for s in shapes],
        in_specs=[VMEM] * 11,
        out_specs=[VMEM] * 10,
        scratch_shapes=[pltpu.VMEM(*s) for s in scratch]
        + [
            pltpu.SemaphoreType.DMA((4, 2, 2, max(rows, cols))),
            pltpu.SemaphoreType.DMA((2, 3, 2, max(rows, cols))),
        ],
        compiler_params=pltpu.CompilerParams(
            vmem_limit_bytes=BIG, collective_id=1, has_side_effects=True
        ),
    )(
        embedded, cotangent.reshape(count, model_width), norm_gain[None], in_weight, scan_weight,
        step_weight, step_bias, rate2, skip_gain, output_gain[None], output_weight,
    )
    feature_grad = feature_grad.reshape(tile_rows, tile_cols, model_width)
    grads[6], grads[7] = grads[6][0], grads[7][0]
    return (feature_grad, *grads)


def split2(x):
    high = x.astype(jnp.bfloat16)
    return high, (x - high.astype(jnp.float32)).astype(jnp.bfloat16)


def dot(a, b):
    return jnp.dot(a, b, preferred_element_type=jnp.float32)


def greet_all():
    barrier = pltpu.get_barrier_semaphore()
    rows, cols = lax.axis_size("row"), lax.axis_size("col")
    r, c = lax.axis_index("row"), lax.axis_index("col")
    for dr in range(rows):
        for dc in range(cols):
            if dr or dc:
                there = {"row": lax.rem(r + dr, rows), "col": lax.rem(c + dc, cols)}
                pl.semaphore_signal(barrier, inc=1, device_id=there, device_id_type=MESH)
    pl.semaphore_wait(barrier, rows * cols - 1)


def lots_of(rows, inner, model_width, states, rank, group, eh):
    small = -(-5 * eh // SUB) * SUB
    pair = 2 * (rank + states) * eh + small + 2 * group * eh
    early = inner * model_width // LANES + model_width * eh + SUB + pair
    late = model_width * eh + SUB + pair
    per = SUB * rows
    return tuple(-(-n // per) * per for n in (early, late))


def fast_kernel(
    tile_rows, tile_cols, states, rank,
    embedded_ref, upstream_ref, norm_gain_ref, in_weight_ref, sw_ref, step_weight_ref,
    step_bias_ref, decay_ref, skip_ref, output_gain_ref, output_weight_ref,
    feature_ref, early_ref, late_ref,
    home, emb_s0, emb_s1, emb_r0, emb_r1, cot_s0, cot_s1, cot_r0, cot_r1,
    back_s0, back_s1, back_r0, back_r1, y_s0, y_s1, y_r0, y_r1,
    spread0, spread1, wpk, swp, cmat, rate_s, normed_s, mixed_s, value_s, proj_s, tok, slope,
    wide, hist, pace_t, drive_t, bufs, bufs_tok, probe_t, lhs, dval, dr_s, in_acc, norm_acc,
    mine0, from0, side0, mine1, from1, side1, sems, ysems, sumsems,
):
    f32, bf16 = jnp.float32, jnp.bfloat16
    count, inner = tile_rows * tile_cols, output_weight_ref.shape[0]
    model = embedded_ref.shape[1]
    rows, cols = lax.axis_size("row"), lax.axis_size("col")
    me_r, me_c = lax.axis_index("row"), lax.axis_index("col")
    eh = inner // LANES
    group = rank + 2 * states
    lines = (tile_rows // cols, tile_cols // rows)
    length = (count // lines[0], count // lines[1])
    copies_m = tuple(SUB // (2 * n) for n in lines)
    per_n = tuple(states // m for m in copies_m)
    tall = tuple(SUB * n for n in length)
    blocks = count // SUB
    axes = ("col", "row")
    sizes = (cols, rows)
    zero = jnp.zeros((SUB, LANES), f32)
    sub = lax.broadcasted_iota(jnp.int32, (SUB, LANES), 0)
    even = lax.rem(sub, 2) == 0
    pos = sub // 2
    pos_even = lax.rem(pos, 2) == 0
    pos_edge = (pos == 0) | (pos == 3)
    low_half = sub < 4

    def part(h):
        return slice(h * LANES, (h + 1) * LANES)

    def tile(b):
        return pl.ds(pl.multiple_of(b * SUB, SUB), SUB)

    greet_all()

    def pack(src, dst, p):
        if p == 0:
            for rho in range(tile_rows):
                c, i = rho // lines[0], rho % lines[0]
                for j in range(2):
                    dst[c, pl.ds(2 * i + j, tile_cols // 2, stride=SUB), :] = src[
                        pl.ds(rho * tile_cols + j, tile_cols // 2, stride=2), :
                    ]
        else:
            for r in range(rows):
                for j in range(2):
                    dst[r, pl.ds(j, tile_rows, stride=2), :] = src[
                        pl.ds(2 * r + j, tile_rows, stride=tile_cols), :
                    ]

    def unpack(src, dst, p):
        if p == 0:
            for rho in range(tile_rows):
                c, i = rho // lines[0], rho % lines[0]
                for j in range(2):
                    dst[pl.ds(rho * tile_cols + j, tile_cols // 2, stride=2), :] = src[
                        c, pl.ds(2 * i + j, tile_cols // 2, stride=SUB), :
                    ]
        else:
            for r in range(rows):
                for j in range(2):
                    dst[pl.ds(2 * r + j, tile_rows, stride=tile_cols), :] = src[
                        r, pl.ds(j, tile_rows, stride=2), :
                    ]

    def exchange(turn, p, src, dst):
        size, axis = sizes[p], axes[p]
        me = lax.axis_index(axis)
        out = []
        for d in range(1, size):
            target = lax.rem(me + d, size)
            copy = pltpu.make_async_remote_copy(
                src_ref=src.at[target],
                dst_ref=dst.at[me],
                send_sem=sems.at[turn, p, 0, d],
                recv_sem=sems.at[turn, p, 1, d],
                device_id={axis: target},
                device_id_type=MESH,
            )
            copy.start()
            out.append(copy)
        dst[me] = src[me]
        return out

    def swap(p, src, dst):
        out = []
        for dr in range(rows):
            for dc in range(cols):
                r, c = lax.rem(me_r + dr, rows), lax.rem(me_c + dc, cols)
                if p == 0:
                    there, here = c * rows + r, me_r * cols + me_c
                else:
                    there, here = r * cols + c, me_c * rows + me_r
                if dr == 0 and dc == 0:
                    dst[here] = src[there]
                    continue
                copy = pltpu.make_async_remote_copy(
                    src_ref=src.at[there],
                    dst_ref=dst.at[here],
                    send_sem=ysems.at[p, 0, dr * cols + dc],
                    recv_sem=ysems.at[p, 1, dr * cols + dc],
                    device_id={"row": r, "col": c},
                    device_id_type=MESH,
                )
                copy.start()
                out.append(copy)
        return out

    def arrived(copies):
        for copy in copies:
            copy.wait_recv()

    def sent(copies):
        for copy in copies:
            copy.wait_send()

    emb_s, emb_r = (emb_s0, emb_s1), (emb_r0, emb_r1)
    cot_s, cot_r = (cot_s0, cot_s1), (cot_r0, cot_r1)
    back_s, back_r = (back_s0, back_s1), (back_r0, back_r1)
    y_s, y_r = (y_s0, y_s1), (y_r0, y_r1)
    spreads = (spread0, spread1)
    pending = []

    pack(embedded_ref, emb_s1, 1)
    emb1 = exchange(0, 1, emb_s1, emb_r1)
    pack(embedded_ref, emb_s0, 0)
    emb0 = exchange(0, 0, emb_s0, emb_r0)
    home[...] = upstream_ref[...].astype(f32)
    pack(home, cot_s0, 0)
    cot0 = exchange(1, 0, cot_s0, cot_r0)
    pack(home, cot_s1, 1)
    cot1 = exchange(1, 1, cot_s1, cot_r1)
    pending += emb1 + emb0 + cot0 + cot1

    key_row = lax.broadcasted_iota(jnp.int32, (LANES, 2 * LANES), 0)
    lane_tile = lax.broadcasted_iota(jnp.int32, (LANES, 2 * LANES), 1) // LANES
    for p in range(2):
        which = lax.rem(key_row, 2 * states) // states
        key = which * per_n[p] + lax.rem(key_row, per_n[p])
        key = jnp.where(key_row < 4 * states, key - lane_tile, -8 * states)
        for q in range(per_n[p]):
            spreads[p][:, 2 * q * LANES : 2 * (q + 1) * LANES] = jnp.where(
                key == 2 * q, 1.0, 0.0
            ).astype(bf16)
    sw32 = sw_ref[...].astype(f32)
    for d in range(4):
        off = d * group
        low_w = sw32[off : off + rank]
        wpk[d] = jnp.concatenate(
            [sw32[off + rank : off + group], low_w,
             jnp.zeros((LANES - group, inner), f32)], axis=0
        ).astype(bf16)
        step_w = step_weight_ref[d]
        w1, w2 = split2(step_w)
        w3 = (step_w - w1.astype(f32) - w2.astype(f32)).astype(bf16)
        blank = jnp.zeros((rank, inner), f32)
        left = jnp.concatenate([low_w, low_w, low_w, blank], axis=0).astype(bf16)
        right = jnp.concatenate(
            [w1.astype(f32), w2.astype(f32), w3.astype(f32), blank], axis=0
        ).astype(bf16)
        c_high, c_low = split2(cross(left, right))
        cmat[d, 0] = c_high
        cmat[d, 1] = c_low
        for i, w in enumerate((w1, w2)):
            swp[d, i] = jnp.concatenate(
                [jnp.zeros((2 * states, inner), f32), w.astype(f32),
                 jnp.zeros((LANES - group, inner), f32)], axis=0
            ).astype(bf16)
        rate = -jnp.exp(decay_ref[d]) * LOG2E
        p, k = d // 2, d % 2
        for n in range(states):
            m, n1 = n // per_n[p], n % per_n[p]
            for h in range(eh):
                row = jnp.broadcast_to(rate[n : n + 1, part(h)], (SUB, LANES))
                if p == 0:
                    mask = lax.rem(sub, 2) == k
                else:
                    mask = pos == 2 * m + k
                at = slice(n1 * SUB, (n1 + 1) * SUB)
                if k == 0 and m == 0:
                    rate_s[p, h, at, :] = row
                else:
                    rate_s[p, h, at, :] = jnp.where(mask, row, rate_s[p, h, at, :])

    def to_scan(p, first, second, store):
        def one(b, carry):
            mirror = blocks - 1 - b
            x0, x1 = first(tile(b)), second(tile(mirror))
            if p == 0:
                z = jnp.where(even, x1, x0)
                store(tile(2 * b), jnp.where(even, x0, x1))
                store(
                    tile(2 * b + 1),
                    jnp.where(even, pltpu.roll(z, SUB - 1, 0), pltpu.roll(z, 1, 0)),
                )
            else:
                u = jnp.where(pos_even, x0, x1)
                v = pltpu.roll(u, 4, 0)
                u2 = pltpu.roll(jnp.where(pos_even, x1, x0), 2, 0)
                v2 = pltpu.roll(u2, 4, 0)
                store(tile(4 * b), jnp.where(pos_edge, u, v))
                store(tile(4 * b + 1), jnp.where(low_half, v2, u2))
                store(tile(4 * b + 2), jnp.where(pos_edge, v, u))
                store(tile(4 * b + 3), jnp.where(low_half, u2, v2))
            return carry

        lax.fori_loop(0, blocks, one, 0, unroll=4)

    def from_scan(p, load, store):
        def one(b, carry):
            mirror = blocks - 1 - b
            if p == 0:
                s0, s1 = load(tile(2 * b)), load(tile(2 * b + 1))
                store(0, tile(b), jnp.where(even, s0, pltpu.roll(s1, 1, 0)))
                store(1, tile(mirror), jnp.where(even, pltpu.roll(s1, SUB - 1, 0), s0))
            else:
                a = []
                for i in range(4):
                    s = load(tile(4 * b + i))
                    s = s + pltpu.roll(s, 4, 0)
                    a.append(pltpu.roll(s, 2, 0) if i % 2 else s)
                store(
                    0, tile(b),
                    jnp.where(low_half, jnp.where(pos == 0, a[0], a[1]), jnp.where(pos == 2, a[2], a[3])),
                )
                store(
                    1, tile(mirror),
                    jnp.where(low_half, jnp.where(pos == 0, a[3], a[2]), jnp.where(pos == 2, a[1], a[0])),
                )
            return carry

        lax.fori_loop(0, blocks, one, 0, unroll=4)

    def prologue(p):
        embedded = emb_r[p][...].reshape(count, model)
        normed = layer_norm(embedded, norm_gain_ref[...]).astype(bf16)
        normed_s[p] = normed
        mixed_s[p] = dot(normed, in_weight_ref[...])
        value = jax.nn.silu(mixed_s[p, :, :inner]).astype(bf16)
        value_s[p] = value
        value32 = value.astype(f32)
        for k in range(2):
            d = 2 * p + k
            proj_s[p, k] = back(value, wpk[d])
            before = dot(value, cmat[d, 0]) + dot(value, cmat[d, 1]) + step_bias_ref[d : d + 1, :]
            slope[p, k] = jax.nn.sigmoid(before)
            pace = softplus(before)
            for h in range(eh):
                tok[p, k, h] = pace[:, part(h)]
        for h in range(eh):
            for k in range(2):
                bufs[k, :count, :] = tok[p, k, h] * value32[:, part(h)]

            def put_pace(at, x, h=h):
                pace_t[p, h, at, :] = x

            def put_drive(at, x, h=h):
                drive_t[p, h, at, :] = x

            to_scan(p, lambda at, h=h: tok[p, 0, h, at, :], lambda at, h=h: tok[p, 1, h, at, :], put_pace)
            to_scan(p, lambda at: bufs[0, at, :], lambda at: bufs[1, at, :], put_drive)

        def put_probe(at, x):
            probe_t[at, :] = x

        to_scan(p, lambda at: proj_s[p, 0, at, :], lambda at: proj_s[p, 1, at, :], put_probe)
        size_of = tall[p]
        x = jnp.where(keep_lanes(p, size_of), probe_t[:size_of, :], 0.0)
        high = x.astype(bf16).astype(f32)
        lhs[:size_of, :] = (high + pltpu.roll(x - high, 2 * states, 1)).astype(bf16)
        chunk = count
        for q in range(per_n[p]):
            w, n1 = 2 * q // per_n[p], 2 * q % per_n[p]
            for s in range(size_of // chunk):
                out = dot(
                    lhs[s * chunk : (s + 1) * chunk, :],
                    spreads[p][:, 2 * q * LANES : 2 * (q + 1) * LANES],
                )
                for j in range(2):
                    at = (n1 + j) * size_of + s * chunk
                    wide[p, w, at : at + chunk, :] = out[:, part(j)]

    def keep_lanes(p, height):
        lane = lax.broadcasted_iota(jnp.int32, (height, LANES), 1)
        keep = lane < 2 * states
        if copies_m[p] > 1:
            row = lax.broadcasted_iota(jnp.int32, (height, LANES), 0)
            m = lax.rem(row, SUB) // (SUB // copies_m[p])
            keep = keep & (lax.rem(lane, states) // per_n[p] == m)
        return keep

    def forward(p):
        high, stride = tall[p], tall[p] + SUB
        half_n = 8
        for h in range(eh):
            for n in range(per_n[p]):
                hist[p, h, n * stride : n * stride + SUB, :] = zero
        for g in range(per_n[p] // half_n):
            ns = range(g * half_n, (g + 1) * half_n)
            rates = [[rate_s[p, h, n * SUB : (n + 1) * SUB, :] for h in range(eh)] for n in ns]

            def step(t, carry, g=g, ns=ns, rates=rates):
                at = tile(t)
                pace = [pace_t[p, h, at, :] for h in range(eh)]
                drive = [drive_t[p, h, at, :] for h in range(eh)]
                y = [bufs[h, at, :] if g else None for h in range(eh)]
                new = []
                for i, n in enumerate(ns):
                    row = tile(n * (high // SUB) + t)
                    slot = tile(n * (stride // SUB) + t + 1)
                    source, probe = wide[p, 0, row, :], wide[p, 1, row, :]
                    for h in range(eh):
                        a = jnp.exp2(pace[h] * rates[i][h])
                        state = a * carry[i * eh + h] + source * drive[h]
                        hist[p, h, slot, :] = state
                        new.append(state)
                        term = probe * state
                        y[h] = term if y[h] is None else y[h] + term
                for h in range(eh):
                    bufs[h, at, :] = y[h]
                return tuple(new)

            lax.fori_loop(0, length[p], step, (zero,) * (half_n * eh), unroll=2)
        for h in range(eh):

            def put_y(k, at, x, h=h):
                bufs[2 + k, at, :] = x

            from_scan(p, lambda at, h=h: bufs[h, at, :], put_y)
            y_s[p][:, :, part(h)] = (bufs[2, :count, :] + bufs[3, :count, :]).reshape(blocks, SUB, LANES)

    def gate(p):
        value = value_s[p].astype(f32)
        skips = jnp.sum(skip_ref[...], axis=0, keepdims=True)
        total = (
            y_s[p][...].reshape(count, inner) + y_r[p][...].reshape(count, inner) + skips * value
        )
        upstream = cot_r[p][...].reshape(count, model).astype(bf16)
        d_gated = back(upstream, output_weight_ref[...])
        gated, pull = jax.vjp(gate_output, total, mixed_s[p, :, inner:], output_gain_ref[...])
        d_total, d_gate_in, gain_grad = pull(d_gated)
        dval[p] = d_total
        if p == 0:
            put(0, pad_rows(*[gain_grad[:, part(h)] for h in range(eh)]))
            put_wide(0, cross(gated.astype(bf16), upstream))
            d_gate = d_gate_in.astype(bf16)
            gate16 = d_gate
            put_wide(0, cross(normed_s[p], d_gate))
        else:
            gate16 = None

        for h in range(eh):

            def put_g(at, x, h=h):
                bufs[h, at, :] = x

            to_scan(
                p, lambda at, h=h: dval[p, at, part(h)], lambda at, h=h: dval[p, at, part(h)], put_g
            )
        return gate16

    sums = ((mine0, from0, side0, early_ref), (mine1, from1, side1, late_ref))
    fill = [0, 0]

    def put(lot, x):
        mine = sums[lot][0]
        per = mine.shape[1] // SUB
        for i in range(x.shape[0] // SUB):
            n = fill[lot]
            at = (n % per) * SUB
            mine[n // per, at : at + SUB, :] = x[i * SUB : (i + 1) * SUB]
            fill[lot] += 1

    def put_wide(lot, x):
        for h in range(x.shape[1] // LANES):
            put(lot, x[:, h * LANES : (h + 1) * LANES])

    def pad_rows(*rows_in):
        missing = -len(rows_in) % SUB
        return jnp.concatenate(list(rows_in) + [jnp.zeros((missing, LANES), f32)], axis=0)

    def pad_lot(lot):
        mine = sums[lot][0]
        while fill[lot] < rows * mine.shape[1] // SUB:
            put(lot, zero)

    def spread(lot, phase, axis, source, result):
        size = lax.axis_size(axis)
        me = lax.axis_index(axis)
        out = []
        for d in range(1, size):
            target = lax.rem(me + d, size)
            copy = pltpu.make_async_remote_copy(
                src_ref=source(target),
                dst_ref=result(me, d),
                send_sem=sumsems.at[lot, phase, 0, d],
                recv_sem=sumsems.at[lot, phase, 1, d],
                device_id={axis: target},
                device_id_type=MESH,
            )
            copy.start()
            out.append(copy)
        pending.extend(out)
        return out

    def sum_scatter(lot):
        mine, other, side, full = sums[lot]
        pad_lot(lot)
        return spread(lot, 0, "row", lambda t: mine.at[t], lambda me, d: other.at[d - 1])

    def sum_across(lot, copies):
        mine, other, side, full = sums[lot]
        arrived(copies)
        acc = mine[me_r]
        for d in range(rows - 1):
            acc = acc + other[d]
        side[me_c] = acc
        return spread(lot, 1, "col", lambda t: side.at[me_c], lambda m, d: side.at[m])

    def sum_gather(lot, copies):
        mine, other, side, full = sums[lot]
        arrived(copies)
        acc = side[0]
        for d in range(1, cols):
            acc = acc + side[d]
        full[me_r] = acc
        return spread(lot, 2, "row", lambda t: full.at[me_r], lambda m, d: full.at[m])

    def backward(p):
        high, stride = tall[p], tall[p] + SUB
        half_n = 8
        for g in range(per_n[p] // half_n):
            ns = range(g * half_n, (g + 1) * half_n)

            def step(i, carry, g=g, ns=ns):
                grads, rates = carry
                t = length[p] - 1 - i
                at = tile(t)
                pace = [pace_t[p, h, at, :] for h in range(eh)]
                drive = [drive_t[p, h, at, :] for h in range(eh)]
                gs = [bufs[h, at, :] for h in range(eh)]
                dd = [bufs[2 + h, at, :] if g else None for h in range(eh)]
                dp = [bufs[4 + h, at, :] if g else None for h in range(eh)]
                new, new_rates = [], []
                for i, n in enumerate(ns):
                    row = tile(n * (high // SUB) + t)
                    earlier = tile(n * (stride // SUB) + t)
                    current = tile(n * (stride // SUB) + t + 1)
                    source, probe = wide[p, 0, row, :], wide[p, 1, row, :]
                    flow = read = None
                    for h in range(eh):
                        j = i * eh + h
                        rate = rate_s[p, h, n * SUB : (n + 1) * SUB, :]
                        grad = grads[j] + probe * gs[h]
                        term = grad * drive[h]
                        flow = term if flow is None else flow + term
                        term = gs[h] * hist[p, h, current, :]
                        read = term if read is None else read + term
                        term = grad * source
                        dd[h] = term if dd[h] is None else dd[h] + term
                        carried = jnp.exp2(pace[h] * rate) * grad
                        q = carried * hist[p, h, earlier, :]
                        term = q * rate
                        dp[h] = term if dp[h] is None else dp[h] + term
                        new_rates.append(rates[j] + q * pace[h])
                        new.append(carried)
                    wide[p, 0, row, :] = flow
                    wide[p, 1, row, :] = read
                for h in range(eh):
                    bufs[2 + h, at, :] = dd[h]
                    bufs[4 + h, at, :] = dp[h]
                return tuple(new), tuple(new_rates)

            chains = (zero,) * (half_n * eh)
            unused, rates = lax.fori_loop(0, length[p], step, (chains, chains), unroll=2)
            for i, n in enumerate(ns):
                for h in range(eh):
                    place = slice(n * SUB, (n + 1) * SUB)
                    dr_s[h, place, :] = rates[i * eh + h] * rate_s[p, h, place, :] * (1.0 / LOG2E)

    def finish_pair(p, gate16):
        lot = p
        high = tall[p]
        chunk = count
        for s in range(high // chunk):
            flow = jnp.zeros((chunk, LANES), f32)
            for q in range(per_n[p]):
                w, n1 = 2 * q // per_n[p], 2 * q % per_n[p]
                at = n1 * high + s * chunk
                left = jnp.concatenate(
                    [wide[p, w, at : at + chunk, :].astype(bf16),
                     wide[p, w, at + high : at + high + chunk, :].astype(bf16)], axis=1
                )
                flow = flow + back(left, spreads[p][:, 2 * q * LANES : 2 * (q + 1) * LANES])
            probe_t[s * chunk : (s + 1) * chunk, :] = jnp.where(keep_lanes(p, chunk), flow, 0.0)

        def put_flow(k, at, x):
            bufs[k, at, :] = x

        from_scan(p, lambda at: probe_t[at, :], put_flow)
        value16 = value_s[p]
        value = value16.astype(f32)
        d_total = dval[p]
        direct = jnp.sum(d_total * value, axis=0, keepdims=True)
        small = [direct[:, part(h)] for h in range(eh)]
        skip = skip_ref[2 * p : 2 * p + 1, :] + skip_ref[2 * p + 1 : 2 * p + 2, :]
        dv = skip * d_total
        ddt, dpt = [[None] * eh for k in range(2)], [[None] * eh for k in range(2)]
        for h in range(eh):
            for which, out in ((2, ddt), (4, dpt)):

                def put_tok(k, at, x, which=which, h=h):
                    bufs_tok[k, which // 2 - 1, h, at, :] = x

                from_scan(p, lambda at, which=which, h=h: bufs[which + h, at, :], put_tok)
        for k in range(2):
            d = 2 * p + k
            drive = jnp.concatenate([bufs_tok[k, 0, h] for h in range(eh)], axis=1)
            pull = jnp.concatenate([bufs_tok[k, 1, h] for h in range(eh)], axis=1)
            pace = jnp.concatenate([tok[p, k, h] for h in range(eh)], axis=1)
            dv = dv + drive * pace
            d_before = (drive * value + pull * (1.0 / LOG2E)) * slope[p, k]
            b_high, b_low = split2(d_before)
            bias_sum = jnp.sum(d_before, axis=0, keepdims=True)
            small += [bias_sum[:, part(h)] for h in range(eh)]
            d_proj = (
                bufs[k, :count, :] + back(b_high, swp[d, 0]) + back(b_low, swp[d, 0])
                + back(b_high, swp[d, 1])
            ).astype(bf16)
            dv = dv + dot(d_proj, wpk[d])
            put_wide(lot, cross(proj_s[p, k].astype(bf16), b_high)[2 * states : group])
            grad = cross(d_proj, value16)
            put_wide(lot, grad[2 * states : group])
            put_wide(lot, grad[: 2 * states])
            for h in range(eh):
                for m in range(copies_m[p]):
                    acc = None
                    for line in range(lines[p]):
                        s = 2 * line + k if p == 0 else 4 * m + 2 * k + line
                        term = dr_s[h, pl.ds(s, per_n[p], stride=SUB), :]
                        acc = term if acc is None else acc + term
                    put(lot, acc)
        put(lot, pad_rows(*small))
        d_val = (dv * silu_slope(mixed_s[p, :, :inner])).astype(bf16)
        grad = cross(normed_s[p], d_val)
        if p == 0:
            in_acc[...] = grad
            d_mixed = jnp.concatenate([d_val, gate16], axis=1)
            d_normed = back(d_mixed, in_weight_ref[...])
        else:
            put_wide(1, in_acc[...] + grad)
            d_normed = back(d_val, in_weight_ref[:, :inner])
        unused, pull = jax.vjp(layer_norm, emb_r[p][...].reshape(count, model), norm_gain_ref[...])
        d_embedded, norm_grad = pull(d_normed)
        if p == 0:
            norm_acc[...] = norm_grad
        else:
            put(1, pad_rows(norm_acc[...] + norm_grad))
        back_s[p][...] = d_embedded.reshape(back_s[p].shape)
        out = exchange(2, p, back_s[p], back_r[p])
        pending.extend(out)
        return out

    arrived(emb1)
    prologue(1)
    forward(1)
    y1 = swap(1, y_s1, y_r0)
    pending += y1
    arrived(emb0)
    prologue(0)
    forward(0)
    y0 = swap(0, y_s0, y_r1)
    pending += y0
    arrived(y1)
    arrived(cot0)
    gate16 = gate(0)
    backward(0)
    home0 = finish_pair(0, gate16)
    early = sum_scatter(0)
    arrived(y0)
    arrived(cot1)
    gate(1)
    early = sum_across(0, early)
    backward(1)
    early = sum_gather(0, early)
    home1 = finish_pair(1, None)
    late = sum_scatter(1)
    arrived(home0)
    unpack(back_r0, bufs.at[0], 0)
    home[...] = home[...] + bufs[0, :count, :]
    late = sum_across(1, late)
    arrived(home1)
    unpack(back_r1, bufs.at[1], 1)
    feature_ref[...] = (home[...] + bufs[1, :count, :]).astype(bf16)
    arrived(early)
    late = sum_gather(1, late)
    arrived(late)
    sent(pending)


def unpack_kernel(
    states, rank, grad_scale,
    feature_in, early_ref, late_ref,
    feature_ref, in_grad_ref, scan_grad_ref, stepw_ref, stepb_ref, dr_ref, skip_grad_ref,
    norm_grad_ref, gain_grad_ref, out_grad_ref,
):
    feature_ref[...] = feature_in[...]
    inner = out_grad_ref.shape[0]
    eh = inner // LANES
    group = rank + 2 * states
    taken = [0, 0]
    lots = (early_ref, late_ref)

    def take(lot, height):
        at = taken[lot]
        taken[lot] += height
        return lots[lot][at : at + height, :] * grad_scale

    def take_wide(lot, out, at, height, width):
        for h in range(width // LANES):
            out[at : at + height, h * LANES : (h + 1) * LANES] = take(lot, height)

    def part(h):
        return slice(h * LANES, (h + 1) * LANES)

    for p in range(2):
        if p == 0:
            small = take(0, -(-eh // SUB) * SUB)
            for h in range(eh):
                gain_grad_ref[:, part(h)] = small[h : h + 1]
            take_wide(0, out_grad_ref, 0, inner, out_grad_ref.shape[1])
            for h in range(eh):
                in_grad_ref[:, inner + h * LANES : inner + (h + 1) * LANES] = take(
                    0, in_grad_ref.shape[0]
                )
        for k in range(2):
            d = 2 * p + k
            take_wide(p, stepw_ref.at[d], 0, rank, inner)
            take_wide(p, scan_grad_ref, d * group, rank, inner)
            take_wide(p, scan_grad_ref, d * group + rank, 2 * states, inner)
            take_wide(p, dr_ref.at[d], 0, states, inner)
        small = take(p, -(-3 * eh // SUB) * SUB)
        for h in range(eh):
            for k in range(2):
                d = 2 * p + k
                skip_grad_ref[d : d + 1, part(h)] = small[h : h + 1]
                stepb_ref[d : d + 1, part(h)] = small[(k + 1) * eh + h : (k + 1) * eh + h + 1]
        if p == 1:
            take_wide(1, in_grad_ref, 0, in_grad_ref.shape[0], inner)
            norm_grad_ref[...] = take(1, SUB)[0:1]


def fast(
    classes, features, cotangent, table, norm_gain, in_weight, scan_weight, step_weight,
    step_bias, decay_log, skip_gain, output_gain, output_weight,
):
    tile_rows, tile_cols, model = features.shape
    inner = output_weight.shape[0]
    count = tile_rows * tile_cols
    rows, cols = lax.axis_size("row"), lax.axis_size("col")
    rank, states = step_weight.shape[1], decay_log.shape[1]
    group = rank + 2 * states
    eh = inner // LANES
    grad_scale = float(count * rows * cols) ** (-0.5)
    embedded = embed(features, classes, table).reshape(count, model)
    f32, bf16 = jnp.float32, jnp.bfloat16
    tall = max(SUB * count // (tile_rows // cols), SUB * count // (tile_cols // rows))
    blocks = count // SUB
    early, late = lots_of(rows, inner, model, states, rank, group, eh)
    per_row = ((cols, count // cols, model), (rows, count // rows, model))
    scratch = [((count, model), f32)]
    for name in range(6):
        scratch += [(per_row[0], f32), (per_row[1], f32)]
    scratch += [((blocks, SUB, inner), f32)] * 4
    scratch += [
        ((LANES, 2 * states * LANES), bf16),
        ((LANES, 2 * states * LANES // 2), bf16),
        ((4, LANES, inner), bf16),
        ((4, 2, LANES, inner), bf16),
        ((4, 2, inner, inner), bf16),
        ((2, eh, states * SUB, LANES), f32),
        ((2, count, model), bf16),
        ((2, count, 2 * inner), f32),
        ((2, count, inner), bf16),
        ((2, 2, count, LANES), f32),
        ((2, 2, eh, count, LANES), f32),
        ((2, 2, count, inner), f32),
        ((2, 2, 2 * count * states, LANES), f32),
        ((2, eh, 2 * count * states + states * SUB, LANES), f32),
        ((2, eh, tall, LANES), f32),
        ((2, eh, tall, LANES), f32),
        ((6, tall, LANES), f32),
        ((2, 2, eh, count, LANES), f32),
        ((tall, LANES), f32),
        ((tall, LANES), bf16),
        ((2, count, inner), f32),
        ((eh, states * SUB, LANES), f32),
        ((model, inner), f32),
        ((1, model), f32),
    ]
    for lot in (early, late):
        chunk = (lot // rows, LANES)
        scratch += [((rows,) + chunk, f32), ((rows - 1,) + chunk, f32), ((cols,) + chunk, f32)]
    feature, early_sum, late_sum = pl.pallas_call(
        functools.partial(fast_kernel, tile_rows, tile_cols, states, rank),
        out_shape=[
            jax.ShapeDtypeStruct((count, model), bf16),
            jax.ShapeDtypeStruct((rows, early // rows, LANES), f32),
            jax.ShapeDtypeStruct((rows, late // rows, LANES), f32),
        ],
        in_specs=[VMEM] * 11,
        out_specs=[VMEM] * 3,
        scratch_shapes=[pltpu.VMEM(*s) for s in scratch]
        + [
            pltpu.SemaphoreType.DMA((3, 2, 2, max(rows, cols))),
            pltpu.SemaphoreType.DMA((2, 2, rows * cols)),
            pltpu.SemaphoreType.DMA((2, 3, 2, max(rows, cols))),
        ],
        compiler_params=pltpu.CompilerParams(
            vmem_limit_bytes=BIG, collective_id=1, has_side_effects=True
        ),
    )(
        embedded, cotangent.reshape(count, model), norm_gain[None], in_weight, scan_weight.T,
        step_weight, step_bias, decay_log, skip_gain, output_gain[None], output_weight,
    )
    shapes = [
        ((count, model), bf16),
        (in_weight.shape, f32),
        (scan_weight.shape[::-1], f32),
        (step_weight.shape, f32),
        (step_bias.shape, f32),
        (decay_log.shape, f32),
        (skip_gain.shape, f32),
        ((1, model), f32),
        ((1, inner), f32),
        (output_weight.shape, f32),
    ]
    feature_grad, *grads = pl.pallas_call(
        functools.partial(unpack_kernel, states, rank, grad_scale),
        out_shape=[jax.ShapeDtypeStruct(*s) for s in shapes],
        in_specs=[VMEM] * 3,
        out_specs=[VMEM] * 10,
    )(feature, early_sum.reshape(early, LANES), late_sum.reshape(late, LANES))
    feature_grad = feature_grad.reshape(tile_rows, tile_cols, model)
    grads[1] = grads[1].T
    grads[6], grads[7] = grads[6][0], grads[7][0]
    return (feature_grad, *grads)


def local(*args):
    tile_rows, tile_cols, model = args[1].shape
    rows, cols = lax.axis_size("row"), lax.axis_size("col")
    rank, states, inner = args[7].shape[1], args[9].shape[1], args[12].shape[0]
    fits = (
        tile_rows == 4 * cols and tile_cols == 2 * rows and model == LANES and inner == 2 * LANES
        and states == 2 * SUB and rank == SUB
    )
    return (fast if fits else general)(*args)


def solution(mesh):
    in_specs = (P("row", "col"), P("row", "col", None), P("row", "col", None)) + (P(),) * 10
    out_specs = (P("row", "col", None),) + (P(),) * 9
    return jax.shard_map(local, mesh=mesh, in_specs=in_specs, out_specs=out_specs, check_vma=False)
```

```python
import functools
import math

import jax
import jax.numpy as jnp
from jax import lax
from jax.experimental import pallas as pl
from jax.experimental.pallas import tpu as pltpu
from jax.sharding import PartitionSpec as P

EPS = 1e-05
HIGHEST = lax.Precision.HIGHEST
MESH = pl.DeviceIdType.MESH
LANES = 128
SUB = 8
LOG2E = math.log2(math.e)
VMEM = pl.BlockSpec(memory_space=pltpu.VMEM)
BIG = 60 * 1024 * 1024


def layer_norm(rows, gain):
    average = jnp.mean(rows, axis=-1, keepdims=True)
    centred = rows - average
    spread = jnp.mean(centred * centred, axis=-1, keepdims=True)
    return centred * lax.rsqrt(spread + EPS) * gain


def silu_slope(before):
    sigma = jax.nn.sigmoid(before)
    return sigma * (1.0 + before * (1.0 - sigma))


def embed(features, classes, table):
    labels = jnp.arange(table.shape[0], dtype=jnp.int32)
    onehot = (classes[..., None] == labels).astype(jnp.float32)
    lookup = jnp.einsum("hwk,kd->hwd", onehot, table, precision=HIGHEST)
    return features.astype(jnp.float32) + lookup


def gate_output(total, gate_in, output_gain):
    return layer_norm(total, output_gain) * jax.nn.silu(gate_in)


def greet(axes):
    barrier = pltpu.get_barrier_semaphore()
    partners = 0
    for axis in axes:
        count = lax.axis_size(axis)
        me = lax.axis_index(axis)
        for d in range(1, count):
            pl.semaphore_signal(
                barrier, inc=1, device_id={axis: lax.rem(me + d, count)}, device_id_type=MESH
            )
            partners += 1
    pl.semaphore_wait(barrier, partners)


def half(ref, k, h, t):
    return ref[k, h, pl.ds(t, 1), :]


def walk(lines, tile, blocks, group, start, step):
    def outer(b, carry):
        def inner(j, carry):
            time = b * tile + j
            rising = b * (tile * lines) + j
            falling = (blocks - 1 - b) * (tile * lines) + (tile - 1 - j)
            tokens = [[base + line * tile for line in group] for base in (rising, falling)]
            return step(carry, tokens, time)

        return lax.fori_loop(0, tile, inner, carry, unroll=2)

    return lax.fori_loop(0, blocks, outer, start)


def groups_of(lines):
    size = 2 if lines % 2 == 0 else 1
    return [tuple(range(g, g + size)) for g in range(0, lines, size)]


def fold(ref, k, h, count):
    total = ref[k, h, pl.ds(0, count, stride=SUB), :]
    for s in range(1, SUB):
        total = total + ref[k, h, pl.ds(s, count, stride=SUB), :]
    return total


def softplus(x):
    return jnp.maximum(x, 0.0) + jnp.log1p(jnp.exp(-jnp.abs(x)))


def cross(a, b):
    return lax.dot_general(a, b, (((0,), (0,)), ((), ())), preferred_element_type=jnp.float32)


def back(a, b):
    return lax.dot_general(a, b, (((1,), (1,)), ((), ())), preferred_element_type=jnp.float32)


def general_kernel(
    tile_rows, tile_cols, states, rank, grad_scale, tiles,
    embedded_ref, upstream_ref, norm_gain_ref, in_weight_ref, scan_weight_ref, step_weight_ref,
    step_bias_ref, rate_ref, skip_ref, output_gain_ref, output_weight_ref,
    feature_ref, in_grad_ref, scan_grad_ref, stepw_ref, stepb_ref, dr_ref, skip_grad_ref,
    norm_grad_ref, gain_grad_ref, out_grad_ref,
    mixed, gate_grad, turn, along, down, wide, sv, steps, slope, low, hist, eight, pace8, up, dproj, dr_acc,
    mine0, from0, side0, all0, mine1, from1, side1, all1, sems, sumsems,
):
    count, inner = tile_rows * tile_cols, output_weight_ref.shape[0]
    rows, cols = lax.axis_size("row"), lax.axis_size("col")
    eh, nh = inner // LANES, states // SUB
    group = rank + 2 * states
    shapes = ((tile_rows // cols, tile_cols), (tile_cols // rows, tile_rows))
    boxes = (along, down)
    axes = ("col", "row")
    greet(("row", "col"))

    def post(turn_number, pair):
        axis, box = axes[pair], boxes[pair]
        size = lax.axis_size(axis)
        me = lax.axis_index(axis)
        copies = []
        for d in range(1, size):
            target = lax.rem(me + d, size)
            copy = pltpu.make_async_remote_copy(
                src_ref=box.at[2 * turn_number, target],
                dst_ref=box.at[2 * turn_number + 1, me],
                send_sem=sems.at[turn_number, pair, 0, d],
                recv_sem=sems.at[turn_number, pair, 1, d],
                device_id={axis: target},
                device_id_type=MESH,
            )
            copy.start()
            copies.append(copy)
        box[2 * turn_number + 1, me] = box[2 * turn_number, me]
        return copies

    def finish(copies):
        for copy in copies:
            copy.wait()

    def put_home(turn_number, x):
        along[2 * turn_number] = x.reshape(along.shape[1:])
        first = post(turn_number, 0)
        for h in range(eh):
            turn[h] = x[:, h * LANES : (h + 1) * LANES]
        per = tile_cols // rows
        for c in range(tile_cols):
            for h in range(eh):
                down[
                    2 * turn_number, c // per,
                    (c % per) * tile_rows : (c % per + 1) * tile_rows,
                    h * LANES : (h + 1) * LANES,
                ] = turn[h, pl.ds(c, tile_rows, stride=tile_cols), :]
        return first, post(turn_number, 1)

    def take_home(turn_number):
        per = tile_cols // rows
        for c in range(tile_cols):
            for h in range(eh):
                turn[h, pl.ds(c, tile_rows, stride=tile_cols), :] = down[
                    2 * turn_number + 1, c // per,
                    (c % per) * tile_rows : (c % per + 1) * tile_rows,
                    h * LANES : (h + 1) * LANES,
                ]
        here = along[2 * turn_number + 1].reshape(count, inner)
        return here + jnp.concatenate([turn[h] for h in range(eh)], axis=1)

    def lines_in(turn_number, pair):
        return boxes[pair][2 * turn_number + 1].reshape(count, inner)

    def lines_out(turn_number, pair, x):
        boxes[pair][2 * turn_number] = x.reshape(boxes[pair].shape[1:])
        return post(turn_number, pair)

    def rate_of(d, m, h):
        return rate_ref[d, m * SUB : (m + 1) * SUB, h * LANES : (h + 1) * LANES]

    def part(h):
        return slice(h * LANES, (h + 1) * LANES)

    zero = jnp.zeros((SUB, LANES), jnp.float32)

    sums = ((mine0, from0, side0, all0), (mine1, from1, side1, all1))
    fill = [0, 0]

    def put(lot, x):
        mine = sums[lot][0]
        per = mine.shape[1] // SUB
        for i in range(x.shape[0] // SUB):
            tile = fill[lot]
            at = (tile % per) * SUB
            mine[tile // per, at : at + SUB, :] = x[i * SUB : (i + 1) * SUB]
            fill[lot] += 1

    def put_wide(lot, x):
        for h in range(x.shape[1] // LANES):
            put(lot, x[:, h * LANES : (h + 1) * LANES])

    taken = [0, 0]

    def take(lot, height):
        full = sums[lot][3]
        per = full.shape[1] // SUB
        out = []
        for i in range(height // SUB):
            tile = taken[lot]
            at = (tile % per) * SUB
            out.append(full[tile // per, at : at + SUB, :])
            taken[lot] += 1
        return jnp.concatenate(out, axis=0) * grad_scale

    def take_wide(lot, height, width):
        return jnp.concatenate([take(lot, height) for h in range(width // LANES)], axis=1)

    def pad_rows(*rows_in):
        missing = -len(rows_in) % SUB
        return jnp.concatenate(list(rows_in) + [jnp.zeros((missing, LANES), jnp.float32)], axis=0)

    def pad_lot(lot):
        while fill[lot] < tiles[lot]:
            put(lot, zero)

    def spread(lot, phase, axis, source, result):
        size = lax.axis_size(axis)
        me = lax.axis_index(axis)
        copies = []
        for d in range(1, size):
            target = lax.rem(me + d, size)
            copy = pltpu.make_async_remote_copy(
                src_ref=source(target),
                dst_ref=result(me, d),
                send_sem=sumsems.at[lot, phase, 0, d],
                recv_sem=sumsems.at[lot, phase, 1, d],
                device_id={axis: target},
                device_id_type=MESH,
            )
            copy.start()
            copies.append(copy)
        return copies

    def sum_scatter(lot):
        mine, other, side, full = sums[lot]
        pad_lot(lot)
        return spread(lot, 0, "row", lambda t: mine.at[t], lambda me, d: other.at[d - 1])

    def sum_across(lot, copies):
        mine, other, side, full = sums[lot]
        finish(copies)
        acc = mine[lax.axis_index("row")]
        for d in range(rows - 1):
            acc = acc + other[d]
        me = lax.axis_index("col")
        side[me] = acc
        return spread(lot, 1, "col", lambda t: side.at[me], lambda m, d: side.at[m])

    def sum_gather(lot, copies):
        mine, other, side, full = sums[lot]
        finish(copies)
        acc = side[0]
        for d in range(1, cols):
            acc = acc + side[d]
        me = lax.axis_index("row")
        full[me] = acc
        return spread(lot, 2, "row", lambda t: full.at[me], lambda m, d: full.at[m])

    embedded = embedded_ref[...]
    normed = layer_norm(embedded, norm_gain_ref[...]).astype(jnp.bfloat16)
    mixed[...] = jnp.dot(normed, in_weight_ref[...], preferred_element_type=jnp.float32)
    values = jax.nn.silu(mixed[:, :inner]).astype(jnp.bfloat16).astype(jnp.float32)
    arriving = put_home(0, values)

    leaving = []
    for pair in range(2):
        lines, tile = shapes[pair]
        length = count // lines
        blocks = length // tile
        finish(arriving[pair])
        value = lines_in(0, pair)
        wide_p, sv_p, steps_p, hist_p = wide.at[pair], sv.at[pair], steps.at[pair], hist.at[pair]
        weight = scan_weight_ref[:, 2 * pair * group : 2 * (pair + 1) * group]
        projected = jnp.dot(
            value.astype(jnp.bfloat16), weight, preferred_element_type=jnp.float32
        )
        for k in range(2):
            d = 2 * pair + k
            lowrank = projected[:, k * group : k * group + rank]
            low[d] = lowrank
            before = (
                jnp.dot(
                    lowrank, step_weight_ref[d], precision=HIGHEST,
                    preferred_element_type=jnp.float32,
                )
                + step_bias_ref[d : d + 1, :]
            )
            slope[d] = jax.nn.sigmoid(before)
            pace = softplus(before)
            for h in range(eh):
                steps_p[k, h] = pace[:, part(h)]
                sv_p[k, h] = pace[:, part(h)] * value[:, part(h)]
            for which in range(2):
                for n in range(states):
                    col = k * group + rank + which * states + n
                    wide_p[k, which, pl.ds(n, count, stride=states), :] = jnp.broadcast_to(
                        projected[:, col : col + 1], (count, LANES)
                    )
            for h in range(eh):
                for line in range(lines):
                    at = line * (length + 1) * states
                    hist_p[k, h, at : at + states, :] = jnp.zeros((states, LANES), jnp.float32)
        for lot in groups_of(lines):

            def advance(carry, tokens, time):
                new = []
                i = 0
                for k in range(2):
                    for line, t in zip(lot, tokens[k]):
                        drive = [half(sv_p, k, h, t) for h in range(eh)]
                        pace = [half(steps_p, k, h, t) for h in range(eh)]
                        sums = [None] * eh
                        for m in range(nh):
                            at = pl.ds(pl.multiple_of(t * states + m * SUB, SUB), SUB)
                            slot = (line * (length + 1) + time + 1) * states + m * SUB
                            source = wide_p[k, 0, at, :]
                            probe = wide_p[k, 1, at, :]
                            for h in range(eh):
                                a = jnp.exp2(pace[h] * rate_of(2 * pair + k, m, h))
                                state = a * carry[i] + source * drive[h]
                                i += 1
                                hist_p[k, h, pl.ds(pl.multiple_of(slot, SUB), SUB), :] = state
                                new.append(state)
                                term = probe * state
                                sums[h] = term if sums[h] is None else sums[h] + term
                        for h in range(eh):
                            eight[k, h, pl.ds(pl.multiple_of(t * SUB, SUB), SUB), :] = sums[h]
                return tuple(new)

            walk(lines, tile, blocks, lot, (zero,) * (2 * len(lot) * eh * nh), advance)
        skip = skip_ref[2 * pair : 2 * pair + 1, :] + skip_ref[2 * pair + 1 : 2 * pair + 2, :]
        y = skip * value + jnp.concatenate(
            [fold(eight, 0, h, count) + fold(eight, 1, h, count) for h in range(eh)], axis=1
        )
        leaving.append(lines_out(1, pair, y))
    finish(leaving[0])
    finish(leaving[1])
    total = take_home(1)

    upstream = upstream_ref[...]
    gated, gate_pull = jax.vjp(gate_output, total, mixed[:, inner:], output_gain_ref[...])
    d_gated = back(upstream, output_weight_ref[...])
    d_total, d_gate_in, gain_grad = gate_pull(d_gated)
    arriving = put_home(2, d_total)
    gate_grad[...] = d_gate_in
    put(0, pad_rows(*[gain_grad[:, part(h)] for h in range(eh)]))
    put_wide(0, cross(gated.astype(jnp.bfloat16), upstream))

    leaving = []
    for pair in range(2):
        lines, tile = shapes[pair]
        length = count // lines
        blocks = length // tile
        finish(arriving[pair])
        g_all = lines_in(2, pair)
        wide_p, sv_p, steps_p, hist_p = wide.at[pair], sv.at[pair], steps.at[pair], hist.at[pair]
        for h in range(eh):
            up[0, h] = g_all[:, part(h)]
        for lot in groups_of(lines):

            def retreat(carry, tokens, time):
                grads, rates = carry
                rates = list(rates)
                new = []
                i = 0
                for k in range(2):
                    for line, t in zip(lot, tokens[1 - k]):
                        drive = [half(sv_p, k, h, t) for h in range(eh)]
                        pace = [half(steps_p, k, h, t) for h in range(eh)]
                        g = [half(up, 0, h, t) for h in range(eh)]
                        dd = [None] * eh
                        dp = [None] * eh
                        for m in range(nh):
                            at = pl.ds(pl.multiple_of(t * states + m * SUB, SUB), SUB)
                            slot = (line * (length + 1) + length - 1 - time) * states + m * SUB
                            earlier = pl.ds(pl.multiple_of(slot, SUB), SUB)
                            current = pl.ds(pl.multiple_of(slot + states, SUB), SUB)
                            source = wide_p[k, 0, at, :]
                            probe = wide_p[k, 1, at, :]
                            flow = None
                            read = None
                            for h in range(eh):
                                rate = rate_of(2 * pair + k, m, h)
                                grad = grads[i] + probe * g[h]
                                i += 1
                                term = grad * drive[h]
                                flow = term if flow is None else flow + term
                                term = g[h] * hist_p[k, h, current, :]
                                read = term if read is None else read + term
                                term = grad * source
                                dd[h] = term if dd[h] is None else dd[h] + term
                                carried = jnp.exp2(pace[h] * rate) * grad
                                q = carried * hist_p[k, h, earlier, :]
                                term = q * rate
                                dp[h] = term if dp[h] is None else dp[h] + term
                                j = (k * nh + m) * eh + h
                                rates[j] = rates[j] + q * pace[h]
                                new.append(carried)
                            wide_p[k, 0, at, :] = flow
                            wide_p[k, 1, at, :] = read
                        for h in range(eh):
                            at8 = pl.ds(pl.multiple_of(t * SUB, SUB), SUB)
                            eight[k, h, at8, :] = dd[h]
                            pace8[k, h, at8, :] = dp[h]
                return (tuple(new), tuple(rates))

            chains = 2 * len(lot) * eh * nh
            unused, rates = walk(
                lines, tile, blocks, lot, ((zero,) * chains, (zero,) * (2 * eh * nh)), retreat
            )
            for k in range(2):
                for m in range(nh):
                    for h in range(eh):
                        place = (2 * pair + k, slice(m * SUB, (m + 1) * SUB), part(h))
                        add = rates[(k * nh + m) * eh + h] * rate_ref[place] * (1.0 / LOG2E)
                        if lot[0] == 0:
                            dr_acc[place] = add
                        else:
                            dr_acc[place] += add
        value = lines_in(0, pair)
        g_all = lines_in(2, pair)
        skip = skip_ref[2 * pair : 2 * pair + 1, :] + skip_ref[2 * pair + 1 : 2 * pair + 2, :]
        dv = skip * g_all
        direct = jnp.sum(g_all * value, axis=0, keepdims=True)
        small = [direct[:, part(h)] for h in range(eh)]
        for k in range(2):
            d = 2 * pair + k
            drive = jnp.concatenate([fold(eight, k, h, count) for h in range(eh)], axis=1)
            pace = jnp.concatenate([fold(pace8, k, h, count) for h in range(eh)], axis=1)
            dv = dv + drive * jnp.concatenate([steps_p[k, h] for h in range(eh)], axis=1)
            d_before = (drive * value + pace * (1.0 / LOG2E)) * slope[d]
            bias_sum = jnp.sum(d_before, axis=0, keepdims=True)
            small += [bias_sum[:, part(h)] for h in range(eh)]
            put_wide(
                pair,
                lax.dot_general(
                    low[d], d_before, (((0,), (0,)), ((), ())), precision=HIGHEST,
                    preferred_element_type=jnp.float32,
                ),
            )
            put_wide(pair, dr_acc[d])
            dproj[:, k * group : k * group + rank] = lax.dot_general(
                d_before, step_weight_ref[d], (((1,), (1,)), ((), ())), precision=HIGHEST,
                preferred_element_type=jnp.float32,
            )
            lane = lax.broadcasted_iota(jnp.int32, (LANES, 2 * states), 1)
            flow = None
            for j in range(2 * states):
                x = wide_p[k, j // states, pl.ds(j % states, count, stride=states), :]
                pick = (lane == j).astype(jnp.bfloat16)
                term = jnp.dot(x.astype(jnp.bfloat16), pick, preferred_element_type=jnp.float32)
                flow = term if flow is None else flow + term
            dproj[:, k * group + rank : (k + 1) * group] = flow
        d_projected = dproj[...].astype(jnp.bfloat16)
        span = slice(2 * pair * group, 2 * (pair + 1) * group)
        leaving.append(lines_out(3, pair, back(d_projected, scan_weight_ref[:, span]) + dv))
        put(pair, pad_rows(*small))
        put_wide(pair, cross(d_projected, value.astype(jnp.bfloat16)))
        if pair == 0:
            early = sum_scatter(0)
        else:
            early = sum_across(0, early)
    finish(leaving[0])
    finish(leaving[1])
    d_values = take_home(3)
    early = sum_gather(0, early)

    d_mixed = jnp.concatenate(
        [d_values * silu_slope(mixed[:, :inner]), gate_grad[...]], axis=1
    ).astype(jnp.bfloat16)
    normed, norm_pull = jax.vjp(layer_norm, embedded_ref[...], norm_gain_ref[...])
    put_wide(1, cross(normed.astype(jnp.bfloat16), d_mixed))
    d_embedded, norm_grad = norm_pull(back(d_mixed, in_weight_ref[...]))
    put(1, pad_rows(norm_grad))
    late = sum_scatter(1)
    feature_ref[...] = (upstream_ref[...].astype(jnp.float32) + d_embedded).astype(jnp.bfloat16)
    late = sum_across(1, late)
    finish(early)
    late = sum_gather(1, late)

    def take_pair(pair):
        for d in (2 * pair, 2 * pair + 1):
            stepw_ref[d] = take_wide(pair, rank, inner)
            dr_ref[d] = take_wide(pair, states, inner)
        small = take(pair, -(-3 * eh // SUB) * SUB)
        for h in range(eh):
            for k in range(2):
                d = 2 * pair + k
                skip_grad_ref[d : d + 1, part(h)] = small[h : h + 1]
                stepb_ref[d : d + 1, part(h)] = small[(k + 1) * eh + h : (k + 1) * eh + h + 1]
        span = slice(2 * pair * group, 2 * (pair + 1) * group)
        scan_grad_ref[:, span] = take_wide(pair, 2 * group, inner).T

    small = take(0, SUB)
    for h in range(eh):
        gain_grad_ref[:, part(h)] = small[h : h + 1]
    out_grad_ref[...] = take_wide(0, inner, out_grad_ref.shape[1])
    take_pair(0)
    finish(late)
    take_pair(1)
    in_grad_ref[...] = take_wide(1, in_grad_ref.shape[0], in_grad_ref.shape[1])
    norm_grad_ref[...] = take(1, SUB)[0:1]


def general(
    classes, features, cotangent, table, norm_gain, in_weight, scan_weight, step_weight,
    step_bias, decay_log, skip_gain, output_gain, output_weight,
):
    tile_rows, tile_cols, model_width = features.shape
    inner = output_weight.shape[0]
    count = tile_rows * tile_cols
    rows, cols = lax.axis_size("row"), lax.axis_size("col")
    rank = step_weight.shape[1]
    states = decay_log.shape[1]
    group = rank + 2 * states
    eh = inner // LANES
    lines = max(tile_rows // cols, tile_cols // rows)
    grad_scale = float(count * rows * cols) ** (-0.5)
    rate2 = -jnp.exp(decay_log) * LOG2E
    embedded = embed(features, classes, table).reshape(count, model_width)
    f32 = jnp.float32
    shapes = [
        ((count, model_width), jnp.bfloat16),
        (in_weight.shape, f32),
        (scan_weight.shape, f32),
        (step_weight.shape, f32),
        (step_bias.shape, f32),
        (decay_log.shape, f32),
        (skip_gain.shape, f32),
        ((1, model_width), f32),
        ((1, inner), f32),
        (output_weight.shape, f32),
    ]
    scratch = [
        ((count, 2 * inner), f32),
        ((count, inner), f32),
        ((eh, count, LANES), f32),
        ((8, cols, count // cols, inner), f32),
        ((8, rows, count // rows, inner), f32),
        ((2, 2, 2, count * states, LANES), f32),
        ((2, 2, eh, count, LANES), f32),
        ((2, 2, eh, count, LANES), f32),
        ((4, count, inner), f32),
        ((4, count, rank), f32),
        ((2, 2, eh, (count + lines) * states, LANES), f32),
        ((2, eh, count * SUB, LANES), f32),
        ((2, eh, count * SUB, LANES), f32),
        ((1, eh, count, LANES), f32),
        ((count, 2 * group), f32),
        (decay_log.shape, f32),
    ]
    pair_tiles = eh * (2 * rank + 2 * states + 2 * group) // SUB + -(-3 * eh // SUB)
    least = (
        1 + inner * model_width // (LANES * SUB) + pair_tiles,
        1 + in_weight.size // (LANES * SUB) + pair_tiles,
    )
    tiles = tuple(-(-t // rows) * rows for t in least)
    for lot in range(2):
        chunk = (tiles[lot] // rows * SUB, LANES)
        scratch += [((rows,) + chunk, f32), ((rows - 1,) + chunk, f32), ((cols,) + chunk, f32), ((rows,) + chunk, f32)]
    feature_grad, *grads = pl.pallas_call(
        functools.partial(general_kernel, tile_rows, tile_cols, states, rank, grad_scale, tiles),
        out_shape=[jax.ShapeDtypeStruct(*s) for s in shapes],
        in_specs=[VMEM] * 11,
        out_specs=[VMEM] * 10,
        scratch_shapes=[pltpu.VMEM(*s) for s in scratch]
        + [
            pltpu.SemaphoreType.DMA((4, 2, 2, max(rows, cols))),
            pltpu.SemaphoreType.DMA((2, 3, 2, max(rows, cols))),
        ],
        compiler_params=pltpu.CompilerParams(
            vmem_limit_bytes=BIG, collective_id=1, has_side_effects=True
        ),
    )(
        embedded, cotangent.reshape(count, model_width), norm_gain[None], in_weight, scan_weight,
        step_weight, step_bias, rate2, skip_gain, output_gain[None], output_weight,
    )
    feature_grad = feature_grad.reshape(tile_rows, tile_cols, model_width)
    grads[6], grads[7] = grads[6][0], grads[7][0]
    return (feature_grad, *grads)


def split2(x):
    high = x.astype(jnp.bfloat16)
    return high, (x - high.astype(jnp.float32)).astype(jnp.bfloat16)


def dot(a, b):
    return jnp.dot(a, b, preferred_element_type=jnp.float32)


def greet_all():
    barrier = pltpu.get_barrier_semaphore()
    rows, cols = lax.axis_size("row"), lax.axis_size("col")
    r, c = lax.axis_index("row"), lax.axis_index("col")
    for dr in range(rows):
        for dc in range(cols):
            if dr or dc:
                there = {"row": lax.rem(r + dr, rows), "col": lax.rem(c + dc, cols)}
                pl.semaphore_signal(barrier, inc=1, device_id=there, device_id_type=MESH)
    pl.semaphore_wait(barrier, rows * cols - 1)


def lots_of(rows, inner, model_width, states, rank, group, eh):
    pair = (rank + states + group) * 2 * eh + -(-3 * eh // SUB) * SUB
    gated = SUB + inner * model_width // LANES + model_width * eh
    per = SUB * rows
    return tuple(-(-n // per) * per for n in (gated, pair, pair, model_width * eh + SUB))


def fast_kernel(
    tile_rows, tile_cols, states, rank,
    features_ref, classes_ref, table_ref, upstream_ref, norm_gain_ref, in_weight_ref, sw_ref,
    step_weight_ref, step_bias_ref, decay_ref, skip_ref, output_gain_ref, output_weight_ref,
    feature_ref, full0, full1, full2, full3,
    home, emb_s0, emb_s1, emb_r0, emb_r1, cot_s0, cot_s1, cot_r0, cot_r1,
    back_s0, back_s1, back_r0, back_r1, y_s0, y_s1, y_r0, y_r1,
    spread0, spread1, wpk, swp, cmat, rate_s, normed_s, mixed_s, value_s, proj_s, tok, slope,
    wide, flows, hist, pace_t, drive_t, g_t, dd_a, dd_b, dp_a, dp_b, bufs, bufs_tok, probe_t, lhs, dval, dr_s, in_acc, norm_acc,
    mine0, from0, side0, mine1, from1, side1, mine2, from2, side2, mine3, from3, side3,
    sems, ysems, sumsems,
):
    f32, bf16 = jnp.float32, jnp.bfloat16
    count, inner = tile_rows * tile_cols, output_weight_ref.shape[0]
    model = features_ref.shape[1]
    rows, cols = lax.axis_size("row"), lax.axis_size("col")
    me_r, me_c = lax.axis_index("row"), lax.axis_index("col")
    eh = inner // LANES
    group = rank + 2 * states
    lines = (tile_rows // cols, tile_cols // rows)
    length = (count // lines[0], count // lines[1])
    copies_m = tuple(SUB // (2 * n) for n in lines)
    per_n = tuple(states // m for m in copies_m)
    tall = tuple(SUB * n for n in length)
    blocks = count // SUB
    axes = ("col", "row")
    sizes = (cols, rows)
    zero = jnp.zeros((SUB, LANES), f32)
    sub = lax.broadcasted_iota(jnp.int32, (SUB, LANES), 0)
    even = lax.rem(sub, 2) == 0
    pos = sub // 2
    pos_even = lax.rem(pos, 2) == 0
    pos_edge = (pos == 0) | (pos == 3)
    low_half = sub < 4

    def part(h):
        return slice(h * LANES, (h + 1) * LANES)

    def tile(b):
        return pl.ds(pl.multiple_of(b * SUB, SUB), SUB)

    def tile2(b):
        return pl.ds(pl.multiple_of(b * 2 * SUB, 2 * SUB), 2 * SUB)

    greet_all()

    def pack(src, dst, p):
        if p == 0:
            for rho in range(tile_rows):
                c, i = rho // lines[0], rho % lines[0]
                for j in range(2):
                    dst[c, pl.ds(2 * i + j, tile_cols // 2, stride=SUB), :] = src[
                        pl.ds(rho * tile_cols + j, tile_cols // 2, stride=2), :
                    ]
        else:
            for r in range(rows):
                for j in range(2):
                    dst[r, pl.ds(j, tile_rows, stride=2), :] = src[
                        pl.ds(2 * r + j, tile_rows, stride=tile_cols), :
                    ]

    def unpack(src, dst, p):
        if p == 0:
            for rho in range(tile_rows):
                c, i = rho // lines[0], rho % lines[0]
                for j in range(2):
                    dst[pl.ds(rho * tile_cols + j, tile_cols // 2, stride=2), :] = src[
                        c, pl.ds(2 * i + j, tile_cols // 2, stride=SUB), :
                    ]
        else:
            for r in range(rows):
                for j in range(2):
                    dst[pl.ds(2 * r + j, tile_rows, stride=tile_cols), :] = src[
                        r, pl.ds(j, tile_rows, stride=2), :
                    ]

    def batch(src, dst, amount, send, recv):
        return pltpu.make_async_remote_copy(
            src_ref=src.at[pl.ds(0, amount)], dst_ref=dst.at[pl.ds(0, amount)], send_sem=send,
            recv_sem=recv, device_id={"row": me_r, "col": me_c}, device_id_type=MESH,
        )

    def exchange(turn, p, src, dst):
        size, axis = sizes[p], axes[p]
        me = lax.axis_index(axis)
        for d in range(1, size):
            target = lax.rem(me + d, size)
            copy = pltpu.make_async_remote_copy(
                src_ref=src.at[target],
                dst_ref=dst.at[me],
                send_sem=sems.at[turn, p, 0],
                recv_sem=sems.at[turn, p, 1],
                device_id={axis: target},
                device_id_type=MESH,
            )
            copy.start()
        dst[me] = src[me]
        return [batch(src, dst, size - 1, sems.at[turn, p, 0], sems.at[turn, p, 1])]

    def swap(p, src, dst):
        for dr in range(rows):
            for dc in range(cols):
                r, c = lax.rem(me_r + dr, rows), lax.rem(me_c + dc, cols)
                if p == 0:
                    there, here = c * rows + r, me_r * cols + me_c
                else:
                    there, here = r * cols + c, me_c * rows + me_r
                if dr == 0 and dc == 0:
                    dst[here] = src[there]
                    continue
                copy = pltpu.make_async_remote_copy(
                    src_ref=src.at[there],
                    dst_ref=dst.at[here],
                    send_sem=ysems.at[p, 0],
                    recv_sem=ysems.at[p, 1],
                    device_id={"row": r, "col": c},
                    device_id_type=MESH,
                )
                copy.start()
        return [batch(src, dst, rows * cols - 1, ysems.at[p, 0], ysems.at[p, 1])]

    def arrived(copies):
        for copy in copies:
            copy.wait_recv()

    def sent(copies):
        for copy in copies:
            copy.wait_send()

    emb_s, emb_r = (emb_s0, emb_s1), (emb_r0, emb_r1)
    cot_s, cot_r = (cot_s0, cot_s1), (cot_r0, cot_r1)
    back_s, back_r = (back_s0, back_s1), (back_r0, back_r1)
    y_s, y_r = (y_s0, y_s1), (y_r0, y_r1)
    spreads = (spread0, spread1)
    pending = []
    half_n = SUB
    dd_t, dp_t = (dd_a, dd_b), (dp_a, dp_b)
    y_t = dd_t

    def added(refs, p, h, at):
        total = refs[0][h, at, :]
        for g in range(1, per_n[p] // half_n):
            total = total + refs[g][h, at, :]
        return total

    token = lax.broadcasted_iota(jnp.int32, (count, tile_rows), 0)
    lane = lax.broadcasted_iota(jnp.int32, (count, tile_rows), 1)
    of_row = jnp.where(token // tile_cols == lane, 1.0, 0.0).astype(bf16)
    labels = dot(of_row, classes_ref[...].astype(f32).astype(bf16))
    token = lax.broadcasted_iota(jnp.int32, (count, tile_cols), 0)
    lane = lax.broadcasted_iota(jnp.int32, (count, tile_cols), 1)
    labels = jnp.where(lax.rem(token, tile_cols) == lane, labels, 0.0).astype(bf16)
    labels = dot(labels, jnp.ones((tile_cols, LANES), bf16))
    lane = lax.broadcasted_iota(jnp.int32, (count, LANES), 1).astype(f32)
    onehot = jnp.where(labels == lane, 1.0, 0.0).astype(bf16)
    entries = table_ref[...]
    lookup = None
    for i in range(3):
        rounded = entries.astype(bf16).astype(f32)
        rest = jnp.zeros((LANES - entries.shape[0], model), f32)
        term = dot(onehot, jnp.concatenate([rounded, rest], axis=0).astype(bf16))
        lookup = term if lookup is None else lookup + term
        entries = entries - rounded
    home[...] = features_ref[...].astype(f32) + lookup
    pack(home, emb_s1, 1)
    emb1 = exchange(0, 1, emb_s1, emb_r1)
    pack(home, emb_s0, 0)
    emb0 = exchange(0, 0, emb_s0, emb_r0)
    home[...] = upstream_ref[...].astype(f32)
    pack(home, cot_s0, 0)
    cot0 = exchange(1, 0, cot_s0, cot_r0)
    pack(home, cot_s1, 1)
    cot1 = exchange(1, 1, cot_s1, cot_r1)
    pending += emb1 + emb0 + cot0 + cot1

    key_row = lax.broadcasted_iota(jnp.int32, (LANES, 2 * LANES), 0)
    lane_tile = lax.broadcasted_iota(jnp.int32, (LANES, 2 * LANES), 1) // LANES
    for p in range(2):
        which = lax.rem(key_row, 2 * states) // states
        key = which * per_n[p] + lax.rem(key_row, per_n[p])
        key = jnp.where(key_row < 4 * states, key - lane_tile, -8 * states)
        for q in range(per_n[p]):
            spreads[p][:, 2 * q * LANES : 2 * (q + 1) * LANES] = jnp.where(
                key == 2 * q, 1.0, 0.0
            ).astype(bf16)
    sw32 = sw_ref[...].astype(f32)
    for d in range(4):
        off = d * group
        low_w = sw32[off : off + rank]
        wpk[d] = jnp.concatenate(
            [sw32[off + rank : off + group], low_w,
             jnp.zeros((LANES - group, inner), f32)], axis=0
        ).astype(bf16)
        step_w = step_weight_ref[d]
        w1, w2 = split2(step_w)
        w3 = (step_w - w1.astype(f32) - w2.astype(f32)).astype(bf16)
        blank = jnp.zeros((rank, inner), f32)
        left = jnp.concatenate([low_w, low_w, low_w, blank], axis=0).astype(bf16)
        right = jnp.concatenate(
            [w1.astype(f32), w2.astype(f32), w3.astype(f32), blank], axis=0
        ).astype(bf16)
        c_high, c_low = split2(cross(left, right))
        cmat[d, 0] = c_high
        cmat[d, 1] = c_low
        for i, w in enumerate((w1, w2)):
            swp[d, i] = jnp.concatenate(
                [jnp.zeros((2 * states, inner), f32), w.astype(f32),
                 jnp.zeros((LANES - group, inner), f32)], axis=0
            ).astype(bf16)
        rate = -jnp.exp(decay_ref[d]) * LOG2E
        p, k = d // 2, d % 2
        for n in range(states):
            m, n1 = n // per_n[p], n % per_n[p]
            for h in range(eh):
                row = jnp.broadcast_to(rate[n : n + 1, part(h)], (SUB, LANES))
                if p == 0:
                    mask = lax.rem(sub, 2) == k
                else:
                    mask = pos == 2 * m + k
                at = slice(n1 * SUB, (n1 + 1) * SUB)
                if k == 0 and m == 0:
                    rate_s[p, h, at, :] = row
                else:
                    rate_s[p, h, at, :] = jnp.where(mask, row, rate_s[p, h, at, :])

    def to_scan(p, *moves):
        def one(b, carry):
            for move in moves:
                one_of(b, *move)
            return carry

        def one_of(b, first, second, store):
            mirror = blocks - 1 - b
            x0, x1 = first(tile(b)), second(tile(mirror))
            if p == 0:
                z = jnp.where(even, x1, x0)
                store(tile(2 * b), jnp.where(even, x0, x1))
                store(
                    tile(2 * b + 1),
                    jnp.where(even, pltpu.roll(z, SUB - 1, 0), pltpu.roll(z, 1, 0)),
                )
            else:
                u = jnp.where(pos_even, x0, x1)
                v = pltpu.roll(u, 4, 0)
                u2 = pltpu.roll(jnp.where(pos_even, x1, x0), 2, 0)
                v2 = pltpu.roll(u2, 4, 0)
                store(tile(4 * b), jnp.where(pos_edge, u, v))
                store(tile(4 * b + 1), jnp.where(low_half, v2, u2))
                store(tile(4 * b + 2), jnp.where(pos_edge, v, u))
                store(tile(4 * b + 3), jnp.where(low_half, u2, v2))

        lax.fori_loop(0, blocks, one, 0, unroll=max(2, 4 // len(moves)))

    def from_scan(p, *moves):
        def one(b, carry):
            for move in moves:
                one_of(b, *move)
            return carry

        def one_of(b, load, store):
            mirror = blocks - 1 - b
            if p == 0:
                s0, s1 = load(tile(2 * b)), load(tile(2 * b + 1))
                store(0, tile(b), jnp.where(even, s0, pltpu.roll(s1, 1, 0)))
                store(1, tile(mirror), jnp.where(even, pltpu.roll(s1, SUB - 1, 0), s0))
            else:
                a = []
                for i in range(4):
                    s = load(tile(4 * b + i))
                    s = s + pltpu.roll(s, 4, 0)
                    a.append(pltpu.roll(s, 2, 0) if i % 2 else s)
                store(
                    0, tile(b),
                    jnp.where(low_half, jnp.where(pos == 0, a[0], a[1]), jnp.where(pos == 2, a[2], a[3])),
                )
                store(
                    1, tile(mirror),
                    jnp.where(low_half, jnp.where(pos == 0, a[3], a[2]), jnp.where(pos == 2, a[1], a[0])),
                )

        lax.fori_loop(0, blocks, one, 0, unroll=max(2, 4 // len(moves)))

    def put_at(ref, at, x):
        ref[at, :] = x

    def put_probe(at, x):
        probe_t[at, :] = x

    def prologue(p):
        embedded = emb_r[p][...].reshape(count, model)
        normed = layer_norm(embedded, norm_gain_ref[...]).astype(bf16)
        normed_s[p] = normed
        mixed_s[p] = dot(normed, in_weight_ref[...])
        value = jax.nn.silu(mixed_s[p, :, :inner]).astype(bf16)
        value_s[p] = value
        value32 = value.astype(f32)
        for k in range(2):
            d = 2 * p + k
            proj_s[p, k] = back(value, wpk[d])
            before = dot(value, cmat[d, 0]) + dot(value, cmat[d, 1]) + step_bias_ref[d : d + 1, :]
            slope[p, k] = jax.nn.sigmoid(before)
            pace = softplus(before)
            for h in range(eh):
                tok[p, k, h] = pace[:, part(h)]
        moves = [(lambda at: proj_s[p, 0, at, :], lambda at: proj_s[p, 1, at, :], put_probe)]
        for h in range(eh):
            bufs_tok[0, 0, h] = value32[:, part(h)]
            moves.append(
                (lambda at, h=h: tok[p, 0, h, at, :], lambda at, h=h: tok[p, 1, h, at, :],
                 functools.partial(put_at, pace_t.at[p, h]))
            )
            moves.append(
                (lambda at, h=h: tok[p, 0, h, at, :] * bufs_tok[0, 0, h, at, :],
                 lambda at, h=h: tok[p, 1, h, at, :] * bufs_tok[0, 0, h, at, :],
                 functools.partial(put_at, drive_t.at[p, h]))
            )
        to_scan(p, *moves)
        size_of = tall[p]
        x = jnp.where(keep_lanes(p, size_of), probe_t[:size_of, :], 0.0)
        high = x.astype(bf16).astype(f32)
        lhs[:size_of, :] = (high + pltpu.roll(x - high, 2 * states, 1)).astype(bf16)
        chunk = count
        for q in range(per_n[p]):
            w, n1 = 2 * q // per_n[p], 2 * q % per_n[p]
            for s in range(size_of // chunk):
                out = dot(
                    lhs[s * chunk : (s + 1) * chunk, :],
                    spreads[p][:, 2 * q * LANES : 2 * (q + 1) * LANES],
                )
                for j in range(2):
                    at = (n1 + j) * size_of + s * chunk
                    wide[p, w, at : at + chunk, :] = out[:, part(j)]

    def keep_lanes(p, height):
        lane = lax.broadcasted_iota(jnp.int32, (height, LANES), 1)
        keep = lane < 2 * states
        if copies_m[p] > 1:
            row = lax.broadcasted_iota(jnp.int32, (height, LANES), 0)
            m = lax.rem(row, SUB) // (SUB // copies_m[p])
            keep = keep & (lax.rem(lane, states) // per_n[p] == m)
        return keep

    def forward(p):
        high, stride = tall[p], tall[p] + SUB
        for h in range(eh):
            for n in range(per_n[p]):
                hist[p, h, n * stride : n * stride + SUB, :] = zero
        for g in range(per_n[p] // half_n):
            ns = range(g * half_n, (g + 1) * half_n)
            rates = [[rate_s[p, h, n * SUB : (n + 1) * SUB, :] for h in range(eh)] for n in ns]

            def step(t, carry, g=g, ns=ns, rates=rates):
                at = tile(t)
                pace = [pace_t[p, h, at, :] for h in range(eh)]
                drive = [drive_t[p, h, at, :] for h in range(eh)]
                y = [None] * eh
                new = []
                for i, n in enumerate(ns):
                    row = tile(n * (high // SUB) + t)
                    slot = tile(n * (stride // SUB) + t + 1)
                    source, probe = wide[p, 0, row, :], wide[p, 1, row, :]
                    for h in range(eh):
                        a = jnp.exp2(pace[h] * rates[i][h])
                        state = a * carry[i * eh + h] + source * drive[h]
                        hist[p, h, slot, :] = state
                        new.append(state)
                        term = probe * state
                        y[h] = term if y[h] is None else y[h] + term
                for h in range(eh):
                    y_t[g][h, at, :] = y[h]
                return tuple(new)

            lax.fori_loop(0, length[p], step, (zero,) * (half_n * eh), unroll=2)
        moves = []
        for h in range(eh):

            def put_y(k, at, x, h=h):
                bufs_tok[k, 0, h, at, :] = x

            moves.append((lambda at, h=h: added(y_t, p, h, at), put_y))
        from_scan(p, *moves)
        for h in range(eh):
            y_s[p][:, :, part(h)] = (bufs_tok[0, 0, h] + bufs_tok[1, 0, h]).reshape(blocks, SUB, LANES)

    def gate(p):
        value = value_s[p].astype(f32)
        skips = jnp.sum(skip_ref[...], axis=0, keepdims=True)
        total = (
            y_s[p][...].reshape(count, inner) + y_r[p][...].reshape(count, inner) + skips * value
        )
        upstream = cot_r[p][...].reshape(count, model).astype(bf16)
        d_gated = back(upstream, output_weight_ref[...])
        gated, pull = jax.vjp(gate_output, total, mixed_s[p, :, inner:], output_gain_ref[...])
        d_total, d_gate_in, gain_grad = pull(d_gated)
        dval[p] = d_total
        if p == 0:
            put(0, pad_rows(*[gain_grad[:, part(h)] for h in range(eh)]))
            put_wide(0, cross(gated.astype(bf16), upstream))
            d_gate = d_gate_in.astype(bf16)
            gate16 = d_gate
            put_wide(0, cross(normed_s[p], d_gate))
        else:
            gate16 = None

        moves = []
        for h in range(eh):
            load = lambda at, h=h: dval[p, at, part(h)]
            moves.append((load, load, functools.partial(put_at, g_t.at[h])))
        to_scan(p, *moves)
        return gate16

    sums = (
        (mine0, from0, side0, full0), (mine1, from1, side1, full1),
        (mine2, from2, side2, full2), (mine3, from3, side3, full3),
    )
    fill = [0] * 4

    def put(lot, x):
        mine = sums[lot][0]
        per = mine.shape[1] // SUB
        for i in range(x.shape[0] // SUB):
            n = fill[lot]
            at = (n % per) * SUB
            mine[n // per, at : at + SUB, :] = x[i * SUB : (i + 1) * SUB]
            fill[lot] += 1

    def put_wide(lot, x):
        for h in range(x.shape[1] // LANES):
            put(lot, x[:, h * LANES : (h + 1) * LANES])

    def pad_rows(*rows_in):
        missing = -len(rows_in) % SUB
        return jnp.concatenate(list(rows_in) + [jnp.zeros((missing, LANES), f32)], axis=0)

    def pad_lot(lot):
        mine = sums[lot][0]
        while fill[lot] < rows * mine.shape[1] // SUB:
            put(lot, zero)

    def spread(lot, phase, axis, source, result, whole):
        size = lax.axis_size(axis)
        me = lax.axis_index(axis)
        for d in range(1, size):
            target = lax.rem(me + d, size)
            copy = pltpu.make_async_remote_copy(
                src_ref=source(target),
                dst_ref=result(me, d),
                send_sem=sumsems.at[lot, phase, 0],
                recv_sem=sumsems.at[lot, phase, 1],
                device_id={axis: target},
                device_id_type=MESH,
            )
            copy.start()
        out = [batch(whole, whole, size - 1, sumsems.at[lot, phase, 0], sumsems.at[lot, phase, 1])]
        pending.extend(out)
        return out

    def sum_scatter(lot):
        mine, other, side, full = sums[lot]
        pad_lot(lot)
        return spread(lot, 0, "row", lambda t: mine.at[t], lambda me, d: other.at[d - 1], other)

    def sum_across(lot, copies):
        mine, other, side, full = sums[lot]
        arrived(copies)
        acc = mine[me_r]
        for d in range(rows - 1):
            acc = acc + other[d]
        side[me_c] = acc
        return spread(lot, 1, "col", lambda t: side.at[me_c], lambda m, d: side.at[m], side)

    def sum_gather(lot, copies):
        mine, other, side, full = sums[lot]
        arrived(copies)
        acc = side[0]
        for d in range(1, cols):
            acc = acc + side[d]
        full[me_r] = acc
        return spread(lot, 2, "row", lambda t: full.at[me_r], lambda m, d: full.at[m], full)

    def backward(p):
        high, stride = tall[p], tall[p] + SUB
        for g in range(per_n[p] // half_n):
            ns = range(g * half_n, (g + 1) * half_n)

            def step(i, carry, g=g, ns=ns):
                grads, rates, t = carry
                at = tile(t)
                pace = [pace_t[p, h, at, :] for h in range(eh)]
                drive = [drive_t[p, h, at, :] for h in range(eh)]
                gs = [g_t[h, at, :] for h in range(eh)]
                dd, dp = [None] * eh, [None] * eh
                new, new_rates = [], []
                for i, n in enumerate(ns):
                    row = tile(n * (high // SUB) + t)
                    earlier = tile(n * (stride // SUB) + t)
                    current = tile(n * (stride // SUB) + t + 1)
                    source, probe = wide[p, 0, row, :], wide[p, 1, row, :]
                    flow = read = None
                    for h in range(eh):
                        j = i * eh + h
                        rate = rate_s[p, h, n * SUB : (n + 1) * SUB, :]
                        grad = grads[j] + probe * gs[h]
                        term = grad * drive[h]
                        flow = term if flow is None else flow + term
                        term = gs[h] * hist[p, h, current, :]
                        read = term if read is None else read + term
                        term = grad * source
                        dd[h] = term if dd[h] is None else dd[h] + term
                        carried = jnp.exp2(pace[h] * rate) * grad
                        q = carried * hist[p, h, earlier, :]
                        term = q * rate
                        dp[h] = term if dp[h] is None else dp[h] + term
                        new_rates.append(rates[j] + q * pace[h])
                        new.append(carried)
                    if n % 2 == 0:
                        kept = (flow, read)
                        continue
                    place = tile2((n // 2) * (high // SUB) + t)
                    for w, x in enumerate((flow, read)):
                        both = jnp.concatenate([kept[w], x], axis=0)
                        flows[w, place, :] = both.astype(bf16)
                for h in range(eh):
                    dd_t[g][h, at, :] = dd[h]
                    dp_t[g][h, at, :] = dp[h]
                return tuple(new), tuple(new_rates), t - 1

            chains = (zero,) * (half_n * eh)
            unused, rates, end = lax.fori_loop(
                0, length[p], step, (chains, chains, jnp.int32(length[p] - 1)), unroll=2
            )
            for i, n in enumerate(ns):
                for h in range(eh):
                    place = slice(n * SUB, (n + 1) * SUB)
                    dr_s[h, place, :] = rates[i * eh + h] * rate_s[p, h, place, :] * (1.0 / LOG2E)

    def finish_pair(p, gate16):
        lot = p + 1
        high = tall[p]
        chunk = count
        wide_high = 2 * chunk
        lane = lax.broadcasted_iota(jnp.int32, (wide_high, LANES), 1)
        row = lax.broadcasted_iota(jnp.int32, (wide_high, LANES), 0)
        mine = lax.rem(lane, 2) == lax.rem(row // SUB, 2)
        keep = keep_lanes(p, wide_high) & mine

        def ones_of(w, a):
            at = (w * per_n[p] + 2 * a) * LANES
            return spreads[p][:, at : at + LANES] + spreads[p][:, at + LANES : at + 2 * LANES]

        for s in range(high // chunk):
            flow = None
            for w in range(2):
                for a in range(0, per_n[p] // 2, 2):
                    at = [(a + i) * 2 * high + s * wide_high for i in range(2)]
                    left = jnp.concatenate([flows[w, i : i + wide_high, :] for i in at], axis=1)
                    right = jnp.concatenate([ones_of(w, a), ones_of(w, a + 1)], axis=1)
                    term = back(left, right)
                    flow = term if flow is None else flow + term
            flow = jnp.where(keep, flow, 0.0).reshape(chunk // SUB, 2, SUB, LANES)
            probe_t[s * chunk : (s + 1) * chunk, :] = (flow[:, 0] + flow[:, 1]).reshape(chunk, LANES)

        def put_flow(k, at, x):
            bufs[k, at, :] = x

        moves = [(lambda at: probe_t[at, :], put_flow)]
        value16 = value_s[p]
        value = value16.astype(f32)
        d_total = dval[p]
        direct = jnp.sum(d_total * value, axis=0, keepdims=True)
        small = [direct[:, part(h)] for h in range(eh)]
        skip = skip_ref[2 * p : 2 * p + 1, :] + skip_ref[2 * p + 1 : 2 * p + 2, :]
        dv = skip * d_total
        for h in range(eh):
            for which, source in enumerate((dd_t, dp_t)):

                def put_tok(k, at, x, which=which, h=h):
                    bufs_tok[k, which, h, at, :] = x

                moves.append((lambda at, source=source, h=h: added(source, p, h, at), put_tok))
        from_scan(p, *moves)
        for k in range(2):
            d = 2 * p + k
            drive = jnp.concatenate([bufs_tok[k, 0, h] for h in range(eh)], axis=1)
            pull = jnp.concatenate([bufs_tok[k, 1, h] for h in range(eh)], axis=1)
            pace = jnp.concatenate([tok[p, k, h] for h in range(eh)], axis=1)
            dv = dv + drive * pace
            d_before = (drive * value + pull * (1.0 / LOG2E)) * slope[p, k]
            b_high, b_low = split2(d_before)
            bias_sum = jnp.sum(d_before, axis=0, keepdims=True)
            small += [bias_sum[:, part(h)] for h in range(eh)]
            d_proj = (
                bufs[k, :count, :] + back(b_high, swp[d, 0]) + back(b_low, swp[d, 0])
                + back(b_high, swp[d, 1])
            ).astype(bf16)
            dv = dv + dot(d_proj, wpk[d])
            put_wide(lot, cross(proj_s[p, k].astype(bf16), b_high)[2 * states : group])
            grad = cross(d_proj, value16)
            put_wide(lot, grad[2 * states : group])
            put_wide(lot, grad[: 2 * states])
            for h in range(eh):
                for m in range(copies_m[p]):
                    acc = None
                    for line in range(lines[p]):
                        s = 2 * line + k if p == 0 else 4 * m + 2 * k + line
                        term = dr_s[h, pl.ds(s, per_n[p], stride=SUB), :]
                        acc = term if acc is None else acc + term
                    put(lot, acc)
        put(lot, pad_rows(*small))
        steps = [sum_scatter(lot)]
        if p == 1:
            between()
        d_val = (dv * silu_slope(mixed_s[p, :, :inner])).astype(bf16)
        grad = cross(normed_s[p], d_val)
        if p == 0:
            in_acc[...] = grad
            d_mixed = jnp.concatenate([d_val, gate16], axis=1)
            d_normed = back(d_mixed, in_weight_ref[...])
        else:
            put_wide(3, in_acc[...] + grad)
            d_normed = back(d_val, in_weight_ref[:, :inner])
        unused, pull = jax.vjp(layer_norm, emb_r[p][...].reshape(count, model), norm_gain_ref[...])
        d_embedded, norm_grad = pull(d_normed)
        if p == 0:
            norm_acc[...] = norm_grad
        else:
            put(3, pad_rows(norm_acc[...] + norm_grad))
            steps.append(sum_scatter(3))
        back_s[p][...] = d_embedded.reshape(back_s[p].shape)
        out = exchange(2, p, back_s[p], back_r[p])
        pending.extend(out)
        return [out] + steps

    arrived(emb1)
    prologue(1)
    forward(1)
    y1 = swap(1, y_s1, y_r0)
    pending += y1
    arrived(emb0)
    prologue(0)
    forward(0)
    y0 = swap(0, y_s0, y_r1)
    pending += y0
    arrived(y1)
    arrived(cot0)
    gate16 = gate(0)
    first = sum_scatter(0)
    backward(0)
    first = sum_across(0, first)
    home0, second = finish_pair(0, gate16)
    first = sum_gather(0, first)
    arrived(y0)
    arrived(cot1)
    gate(1)
    backward(1)
    flying = [sum_across(1, second)]

    def between():
        flying.append(sum_gather(1, flying[0]))

    home1, third, fourth = finish_pair(1, None)
    sent(pending[:-3])
    del pending[:-3]
    third = sum_across(2, third)
    home[...] = upstream_ref[...].astype(f32)
    arrived(home0)
    unpack(back_r0, bufs.at[0], 0)
    home[...] = home[...] + bufs[0, :count, :]
    fourth = sum_across(3, fourth)
    third = sum_gather(2, third)
    arrived(home1)
    unpack(back_r1, bufs.at[1], 1)
    feature_ref[...] = (home[...] + bufs[1, :count, :]).astype(bf16)
    fourth = sum_gather(3, fourth)
    for copies in (first, flying[1], third, fourth):
        arrived(copies)
    sent(pending)


def unpack_kernel(
    states, rank, grad_scale,
    feature_in, full0, full1, full2, full3,
    feature_ref, in_grad_ref, scan_grad_ref, stepw_ref, stepb_ref, dr_ref, skip_grad_ref,
    norm_grad_ref, gain_grad_ref, out_grad_ref,
):
    feature_ref[...] = feature_in[...]
    inner = out_grad_ref.shape[0]
    eh = inner // LANES
    group = rank + 2 * states
    taken = [0] * 4
    lots = (full0, full1, full2, full3)

    def take(lot, height):
        at = taken[lot]
        taken[lot] += height
        return lots[lot][at : at + height, :] * grad_scale

    def take_wide(lot, out, at, height, width):
        for h in range(width // LANES):
            out[at : at + height, h * LANES : (h + 1) * LANES] = take(lot, height)

    def part(h):
        return slice(h * LANES, (h + 1) * LANES)

    small = take(0, SUB)
    for h in range(eh):
        gain_grad_ref[:, part(h)] = small[h : h + 1]
    take_wide(0, out_grad_ref, 0, inner, out_grad_ref.shape[1])
    model = in_grad_ref.shape[0]
    for h in range(eh):
        in_grad_ref[:, inner + h * LANES : inner + (h + 1) * LANES] = take(0, model)
    for p in range(2):
        lot = p + 1
        for k in range(2):
            d = 2 * p + k
            take_wide(lot, stepw_ref.at[d], 0, rank, inner)
            take_wide(lot, scan_grad_ref, d * group, rank, inner)
            take_wide(lot, scan_grad_ref, d * group + rank, 2 * states, inner)
            take_wide(lot, dr_ref.at[d], 0, states, inner)
        small = take(lot, -(-3 * eh // SUB) * SUB)
        for h in range(eh):
            for k in range(2):
                d = 2 * p + k
                skip_grad_ref[d : d + 1, part(h)] = small[h : h + 1]
                stepb_ref[d : d + 1, part(h)] = small[(k + 1) * eh + h : (k + 1) * eh + h + 1]
    take_wide(3, in_grad_ref, 0, model, inner)
    norm_grad_ref[...] = take(3, SUB)[0:1]


def fast(
    classes, features, cotangent, table, norm_gain, in_weight, scan_weight, step_weight,
    step_bias, decay_log, skip_gain, output_gain, output_weight,
):
    tile_rows, tile_cols, model = features.shape
    inner = output_weight.shape[0]
    count = tile_rows * tile_cols
    rows, cols = lax.axis_size("row"), lax.axis_size("col")
    rank, states = step_weight.shape[1], decay_log.shape[1]
    group = rank + 2 * states
    eh = inner // LANES
    grad_scale = float(count * rows * cols) ** (-0.5)
    f32, bf16 = jnp.float32, jnp.bfloat16
    tall = max(SUB * count // (tile_rows // cols), SUB * count // (tile_cols // rows))
    blocks = count // SUB
    lots = lots_of(rows, inner, model, states, rank, group, eh)
    per_row = ((cols, count // cols, model), (rows, count // rows, model))
    scratch = [((count, model), f32)]
    for name in range(6):
        scratch += [(per_row[0], f32), (per_row[1], f32)]
    scratch += [((blocks, SUB, inner), f32)] * 4
    scratch += [
        ((LANES, 2 * states * LANES), bf16),
        ((LANES, 2 * states * LANES // 2), bf16),
        ((4, LANES, inner), bf16),
        ((4, 2, LANES, inner), bf16),
        ((4, 2, inner, inner), bf16),
        ((2, eh, states * SUB, LANES), f32),
        ((2, count, model), bf16),
        ((2, count, 2 * inner), f32),
        ((2, count, inner), bf16),
        ((2, 2, count, LANES), f32),
        ((2, 2, eh, count, LANES), f32),
        ((2, 2, count, inner), f32),
        ((2, 2, 2 * count * states, LANES), f32),
        ((2, 2 * count * states, LANES), bf16),
        ((2, eh, 2 * count * states + states * SUB, LANES), f32),
        ((2, eh, tall, LANES), f32),
        ((2, eh, tall, LANES), f32),
        ((eh, tall, LANES), f32),
        ((eh, tall, LANES), f32),
        ((eh, tall // 2, LANES), f32),
        ((eh, tall, LANES), f32),
        ((eh, tall // 2, LANES), f32),
        ((2, count, LANES), f32),
        ((2, 2, eh, count, LANES), f32),
        ((tall, LANES), f32),
        ((tall, LANES), bf16),
        ((2, count, inner), f32),
        ((eh, states * SUB, LANES), f32),
        ((model, inner), f32),
        ((1, model), f32),
    ]
    for lot in lots:
        chunk = (lot // rows, LANES)
        scratch += [((rows,) + chunk, f32), ((rows - 1,) + chunk, f32), ((cols,) + chunk, f32)]
    feature, *full = pl.pallas_call(
        functools.partial(fast_kernel, tile_rows, tile_cols, states, rank),
        out_shape=[
            jax.ShapeDtypeStruct((count, model), bf16),
        ]
        + [jax.ShapeDtypeStruct((rows, lot // rows, LANES), f32) for lot in lots],
        in_specs=[VMEM] * 13,
        out_specs=[VMEM] * 5,
        scratch_shapes=[pltpu.VMEM(*s) for s in scratch]
        + [
            pltpu.SemaphoreType.DMA((3, 2, 2)),
            pltpu.SemaphoreType.DMA((2, 2)),
            pltpu.SemaphoreType.DMA((4, 3, 2)),
        ],
        compiler_params=pltpu.CompilerParams(
            vmem_limit_bytes=BIG + 3 * 1024 * 1024, collective_id=1, has_side_effects=True
        ),
    )(
        features.reshape(count, model), classes, table, cotangent.reshape(count, model),
        norm_gain[None], in_weight, scan_weight.T,
        step_weight, step_bias, decay_log, skip_gain, output_gain[None], output_weight,
    )
    shapes = [
        ((count, model), bf16),
        (in_weight.shape, f32),
        (scan_weight.shape[::-1], f32),
        (step_weight.shape, f32),
        (step_bias.shape, f32),
        (decay_log.shape, f32),
        (skip_gain.shape, f32),
        ((1, model), f32),
        ((1, inner), f32),
        (output_weight.shape, f32),
    ]
    feature_grad, *grads = pl.pallas_call(
        functools.partial(unpack_kernel, states, rank, grad_scale),
        out_shape=[jax.ShapeDtypeStruct(*s) for s in shapes],
        in_specs=[VMEM] * 5,
        out_specs=[VMEM] * 10,
    )(feature, *[x.reshape(lot, LANES) for x, lot in zip(full, lots)])
    feature_grad = feature_grad.reshape(tile_rows, tile_cols, model)
    grads[1] = grads[1].T
    grads[6], grads[7] = grads[6][0], grads[7][0]
    return (feature_grad, *grads)


def local(*args):
    tile_rows, tile_cols, model = args[1].shape
    rows, cols = lax.axis_size("row"), lax.axis_size("col")
    rank, states, inner = args[7].shape[1], args[9].shape[1], args[12].shape[0]
    fits = (
        tile_rows == 4 * cols and tile_cols == 2 * rows and model == LANES and inner == 2 * LANES
        and states == 2 * SUB and rank == SUB and args[3].shape[0] <= LANES
    )
    return (fast if fits else general)(*args)


def solution(mesh):
    in_specs = (P("row", "col"), P("row", "col", None), P("row", "col", None)) + (P(),) * 10
    out_specs = (P("row", "col", None),) + (P(),) * 9
    return jax.shard_map(local, mesh=mesh, in_specs=in_specs, out_specs=out_specs, check_vma=False)
```

```python
import functools
import math

import jax
import jax.numpy as jnp
from jax import lax
from jax.experimental import pallas as pl
from jax.experimental.pallas import tpu as pltpu
from jax.sharding import PartitionSpec as P

EPS = 1e-05
HIGHEST = lax.Precision.HIGHEST
MESH = pl.DeviceIdType.MESH
LANES = 128
SUB = 8
LOG2E = math.log2(math.e)
VMEM = pl.BlockSpec(memory_space=pltpu.VMEM)
BIG = 60 * 1024 * 1024


def layer_norm(rows, gain):
    average = jnp.mean(rows, axis=-1, keepdims=True)
    centred = rows - average
    spread = jnp.mean(centred * centred, axis=-1, keepdims=True)
    return centred * lax.rsqrt(spread + EPS) * gain


def silu_slope(before):
    sigma = jax.nn.sigmoid(before)
    return sigma * (1.0 + before * (1.0 - sigma))


def embed(features, classes, table):
    labels = jnp.arange(table.shape[0], dtype=jnp.int32)
    onehot = (classes[..., None] == labels).astype(jnp.float32)
    lookup = jnp.einsum("hwk,kd->hwd", onehot, table, precision=HIGHEST)
    return features.astype(jnp.float32) + lookup


def gate_output(total, gate_in, output_gain):
    return layer_norm(total, output_gain) * jax.nn.silu(gate_in)


def greet(axes):
    barrier = pltpu.get_barrier_semaphore()
    partners = 0
    for axis in axes:
        count = lax.axis_size(axis)
        me = lax.axis_index(axis)
        for d in range(1, count):
            pl.semaphore_signal(
                barrier, inc=1, device_id={axis: lax.rem(me + d, count)}, device_id_type=MESH
            )
            partners += 1
    pl.semaphore_wait(barrier, partners)


def half(ref, k, h, t):
    return ref[k, h, pl.ds(t, 1), :]


def walk(lines, tile, blocks, group, start, step):
    def outer(b, carry):
        def inner(j, carry):
            time = b * tile + j
            rising = b * (tile * lines) + j
            falling = (blocks - 1 - b) * (tile * lines) + (tile - 1 - j)
            tokens = [[base + line * tile for line in group] for base in (rising, falling)]
            return step(carry, tokens, time)

        return lax.fori_loop(0, tile, inner, carry, unroll=2)

    return lax.fori_loop(0, blocks, outer, start)


def groups_of(lines):
    size = 2 if lines % 2 == 0 else 1
    return [tuple(range(g, g + size)) for g in range(0, lines, size)]


def fold(ref, k, h, count):
    total = ref[k, h, pl.ds(0, count, stride=SUB), :]
    for s in range(1, SUB):
        total = total + ref[k, h, pl.ds(s, count, stride=SUB), :]
    return total


def softplus(x):
    return jnp.maximum(x, 0.0) + jnp.log1p(jnp.exp(-jnp.abs(x)))


def cross(a, b):
    return lax.dot_general(a, b, (((0,), (0,)), ((), ())), preferred_element_type=jnp.float32)


def back(a, b):
    return lax.dot_general(a, b, (((1,), (1,)), ((), ())), preferred_element_type=jnp.float32)


def general_kernel(
    tile_rows, tile_cols, states, rank, grad_scale, tiles,
    embedded_ref, upstream_ref, norm_gain_ref, in_weight_ref, scan_weight_ref, step_weight_ref,
    step_bias_ref, rate_ref, skip_ref, output_gain_ref, output_weight_ref,
    feature_ref, in_grad_ref, scan_grad_ref, stepw_ref, stepb_ref, dr_ref, skip_grad_ref,
    norm_grad_ref, gain_grad_ref, out_grad_ref,
    mixed, gate_grad, turn, along, down, wide, sv, steps, slope, low, hist, eight, pace8, up, dproj, dr_acc,
    mine0, from0, side0, all0, mine1, from1, side1, all1, sems, sumsems,
):
    count, inner = tile_rows * tile_cols, output_weight_ref.shape[0]
    rows, cols = lax.axis_size("row"), lax.axis_size("col")
    eh, nh = inner // LANES, states // SUB
    group = rank + 2 * states
    shapes = ((tile_rows // cols, tile_cols), (tile_cols // rows, tile_rows))
    boxes = (along, down)
    axes = ("col", "row")
    greet(("row", "col"))

    def post(turn_number, pair):
        axis, box = axes[pair], boxes[pair]
        size = lax.axis_size(axis)
        me = lax.axis_index(axis)
        copies = []
        for d in range(1, size):
            target = lax.rem(me + d, size)
            copy = pltpu.make_async_remote_copy(
                src_ref=box.at[2 * turn_number, target],
                dst_ref=box.at[2 * turn_number + 1, me],
                send_sem=sems.at[turn_number, pair, 0, d],
                recv_sem=sems.at[turn_number, pair, 1, d],
                device_id={axis: target},
                device_id_type=MESH,
            )
            copy.start()
            copies.append(copy)
        box[2 * turn_number + 1, me] = box[2 * turn_number, me]
        return copies

    def finish(copies):
        for copy in copies:
            copy.wait()

    def put_home(turn_number, x):
        along[2 * turn_number] = x.reshape(along.shape[1:])
        first = post(turn_number, 0)
        for h in range(eh):
            turn[h] = x[:, h * LANES : (h + 1) * LANES]
        per = tile_cols // rows
        for c in range(tile_cols):
            for h in range(eh):
                down[
                    2 * turn_number, c // per,
                    (c % per) * tile_rows : (c % per + 1) * tile_rows,
                    h * LANES : (h + 1) * LANES,
                ] = turn[h, pl.ds(c, tile_rows, stride=tile_cols), :]
        return first, post(turn_number, 1)

    def take_home(turn_number):
        per = tile_cols // rows
        for c in range(tile_cols):
            for h in range(eh):
                turn[h, pl.ds(c, tile_rows, stride=tile_cols), :] = down[
                    2 * turn_number + 1, c // per,
                    (c % per) * tile_rows : (c % per + 1) * tile_rows,
                    h * LANES : (h + 1) * LANES,
                ]
        here = along[2 * turn_number + 1].reshape(count, inner)
        return here + jnp.concatenate([turn[h] for h in range(eh)], axis=1)

    def lines_in(turn_number, pair):
        return boxes[pair][2 * turn_number + 1].reshape(count, inner)

    def lines_out(turn_number, pair, x):
        boxes[pair][2 * turn_number] = x.reshape(boxes[pair].shape[1:])
        return post(turn_number, pair)

    def rate_of(d, m, h):
        return rate_ref[d, m * SUB : (m + 1) * SUB, h * LANES : (h + 1) * LANES]

    def part(h):
        return slice(h * LANES, (h + 1) * LANES)

    zero = jnp.zeros((SUB, LANES), jnp.float32)

    sums = ((mine0, from0, side0, all0), (mine1, from1, side1, all1))
    fill = [0, 0]

    def put(lot, x):
        mine = sums[lot][0]
        per = mine.shape[1] // SUB
        for i in range(x.shape[0] // SUB):
            tile = fill[lot]
            at = (tile % per) * SUB
            mine[tile // per, at : at + SUB, :] = x[i * SUB : (i + 1) * SUB]
            fill[lot] += 1

    def put_wide(lot, x):
        for h in range(x.shape[1] // LANES):
            put(lot, x[:, h * LANES : (h + 1) * LANES])

    taken = [0, 0]

    def take(lot, height):
        full = sums[lot][3]
        per = full.shape[1] // SUB
        out = []
        for i in range(height // SUB):
            tile = taken[lot]
            at = (tile % per) * SUB
            out.append(full[tile // per, at : at + SUB, :])
            taken[lot] += 1
        return jnp.concatenate(out, axis=0) * grad_scale

    def take_wide(lot, height, width):
        return jnp.concatenate([take(lot, height) for h in range(width // LANES)], axis=1)

    def pad_rows(*rows_in):
        missing = -len(rows_in) % SUB
        return jnp.concatenate(list(rows_in) + [jnp.zeros((missing, LANES), jnp.float32)], axis=0)

    def pad_lot(lot):
        while fill[lot] < tiles[lot]:
            put(lot, zero)

    def spread(lot, phase, axis, source, result):
        size = lax.axis_size(axis)
        me = lax.axis_index(axis)
        copies = []
        for d in range(1, size):
            target = lax.rem(me + d, size)
            copy = pltpu.make_async_remote_copy(
                src_ref=source(target),
                dst_ref=result(me, d),
                send_sem=sumsems.at[lot, phase, 0, d],
                recv_sem=sumsems.at[lot, phase, 1, d],
                device_id={axis: target},
                device_id_type=MESH,
            )
            copy.start()
            copies.append(copy)
        return copies

    def sum_scatter(lot):
        mine, other, side, full = sums[lot]
        pad_lot(lot)
        return spread(lot, 0, "row", lambda t: mine.at[t], lambda me, d: other.at[d - 1])

    def sum_across(lot, copies):
        mine, other, side, full = sums[lot]
        finish(copies)
        acc = mine[lax.axis_index("row")]
        for d in range(rows - 1):
            acc = acc + other[d]
        me = lax.axis_index("col")
        side[me] = acc
        return spread(lot, 1, "col", lambda t: side.at[me], lambda m, d: side.at[m])

    def sum_gather(lot, copies):
        mine, other, side, full = sums[lot]
        finish(copies)
        acc = side[0]
        for d in range(1, cols):
            acc = acc + side[d]
        me = lax.axis_index("row")
        full[me] = acc
        return spread(lot, 2, "row", lambda t: full.at[me], lambda m, d: full.at[m])

    embedded = embedded_ref[...]
    normed = layer_norm(embedded, norm_gain_ref[...]).astype(jnp.bfloat16)
    mixed[...] = jnp.dot(normed, in_weight_ref[...], preferred_element_type=jnp.float32)
    values = jax.nn.silu(mixed[:, :inner]).astype(jnp.bfloat16).astype(jnp.float32)
    arriving = put_home(0, values)

    leaving = []
    for pair in range(2):
        lines, tile = shapes[pair]
        length = count // lines
        blocks = length // tile
        finish(arriving[pair])
        value = lines_in(0, pair)
        wide_p, sv_p, steps_p, hist_p = wide.at[pair], sv.at[pair], steps.at[pair], hist.at[pair]
        weight = scan_weight_ref[:, 2 * pair * group : 2 * (pair + 1) * group]
        projected = jnp.dot(
            value.astype(jnp.bfloat16), weight, preferred_element_type=jnp.float32
        )
        for k in range(2):
            d = 2 * pair + k
            lowrank = projected[:, k * group : k * group + rank]
            low[d] = lowrank
            before = (
                jnp.dot(
                    lowrank, step_weight_ref[d], precision=HIGHEST,
                    preferred_element_type=jnp.float32,
                )
                + step_bias_ref[d : d + 1, :]
            )
            slope[d] = jax.nn.sigmoid(before)
            pace = softplus(before)
            for h in range(eh):
                steps_p[k, h] = pace[:, part(h)]
                sv_p[k, h] = pace[:, part(h)] * value[:, part(h)]
            for which in range(2):
                for n in range(states):
                    col = k * group + rank + which * states + n
                    wide_p[k, which, pl.ds(n, count, stride=states), :] = jnp.broadcast_to(
                        projected[:, col : col + 1], (count, LANES)
                    )
            for h in range(eh):
                for line in range(lines):
                    at = line * (length + 1) * states
                    hist_p[k, h, at : at + states, :] = jnp.zeros((states, LANES), jnp.float32)
        for lot in groups_of(lines):

            def advance(carry, tokens, time):
                new = []
                i = 0
                for k in range(2):
                    for line, t in zip(lot, tokens[k]):
                        drive = [half(sv_p, k, h, t) for h in range(eh)]
                        pace = [half(steps_p, k, h, t) for h in range(eh)]
                        sums = [None] * eh
                        for m in range(nh):
                            at = pl.ds(pl.multiple_of(t * states + m * SUB, SUB), SUB)
                            slot = (line * (length + 1) + time + 1) * states + m * SUB
                            source = wide_p[k, 0, at, :]
                            probe = wide_p[k, 1, at, :]
                            for h in range(eh):
                                a = jnp.exp2(pace[h] * rate_of(2 * pair + k, m, h))
                                state = a * carry[i] + source * drive[h]
                                i += 1
                                hist_p[k, h, pl.ds(pl.multiple_of(slot, SUB), SUB), :] = state
                                new.append(state)
                                term = probe * state
                                sums[h] = term if sums[h] is None else sums[h] + term
                        for h in range(eh):
                            eight[k, h, pl.ds(pl.multiple_of(t * SUB, SUB), SUB), :] = sums[h]
                return tuple(new)

            walk(lines, tile, blocks, lot, (zero,) * (2 * len(lot) * eh * nh), advance)
        skip = skip_ref[2 * pair : 2 * pair + 1, :] + skip_ref[2 * pair + 1 : 2 * pair + 2, :]
        y = skip * value + jnp.concatenate(
            [fold(eight, 0, h, count) + fold(eight, 1, h, count) for h in range(eh)], axis=1
        )
        leaving.append(lines_out(1, pair, y))
    finish(leaving[0])
    finish(leaving[1])
    total = take_home(1)

    upstream = upstream_ref[...]
    gated, gate_pull = jax.vjp(gate_output, total, mixed[:, inner:], output_gain_ref[...])
    d_gated = back(upstream, output_weight_ref[...])
    d_total, d_gate_in, gain_grad = gate_pull(d_gated)
    arriving = put_home(2, d_total)
    gate_grad[...] = d_gate_in
    put(0, pad_rows(*[gain_grad[:, part(h)] for h in range(eh)]))
    put_wide(0, cross(gated.astype(jnp.bfloat16), upstream))

    leaving = []
    for pair in range(2):
        lines, tile = shapes[pair]
        length = count // lines
        blocks = length // tile
        finish(arriving[pair])
        g_all = lines_in(2, pair)
        wide_p, sv_p, steps_p, hist_p = wide.at[pair], sv.at[pair], steps.at[pair], hist.at[pair]
        for h in range(eh):
            up[0, h] = g_all[:, part(h)]
        for lot in groups_of(lines):

            def retreat(carry, tokens, time):
                grads, rates = carry
                rates = list(rates)
                new = []
                i = 0
                for k in range(2):
                    for line, t in zip(lot, tokens[1 - k]):
                        drive = [half(sv_p, k, h, t) for h in range(eh)]
                        pace = [half(steps_p, k, h, t) for h in range(eh)]
                        g = [half(up, 0, h, t) for h in range(eh)]
                        dd = [None] * eh
                        dp = [None] * eh
                        for m in range(nh):
                            at = pl.ds(pl.multiple_of(t * states + m * SUB, SUB), SUB)
                            slot = (line * (length + 1) + length - 1 - time) * states + m * SUB
                            earlier = pl.ds(pl.multiple_of(slot, SUB), SUB)
                            current = pl.ds(pl.multiple_of(slot + states, SUB), SUB)
                            source = wide_p[k, 0, at, :]
                            probe = wide_p[k, 1, at, :]
                            flow = None
                            read = None
                            for h in range(eh):
                                rate = rate_of(2 * pair + k, m, h)
                                grad = grads[i] + probe * g[h]
                                i += 1
                                term = grad * drive[h]
                                flow = term if flow is None else flow + term
                                term = g[h] * hist_p[k, h, current, :]
                                read = term if read is None else read + term
                                term = grad * source
                                dd[h] = term if dd[h] is None else dd[h] + term
                                carried = jnp.exp2(pace[h] * rate) * grad
                                q = carried * hist_p[k, h, earlier, :]
                                term = q * rate
                                dp[h] = term if dp[h] is None else dp[h] + term
                                j = (k * nh + m) * eh + h
                                rates[j] = rates[j] + q * pace[h]
                                new.append(carried)
                            wide_p[k, 0, at, :] = flow
                            wide_p[k, 1, at, :] = read
                        for h in range(eh):
                            at8 = pl.ds(pl.multiple_of(t * SUB, SUB), SUB)
                            eight[k, h, at8, :] = dd[h]
                            pace8[k, h, at8, :] = dp[h]
                return (tuple(new), tuple(rates))

            chains = 2 * len(lot) * eh * nh
            unused, rates = walk(
                lines, tile, blocks, lot, ((zero,) * chains, (zero,) * (2 * eh * nh)), retreat
            )
            for k in range(2):
                for m in range(nh):
                    for h in range(eh):
                        place = (2 * pair + k, slice(m * SUB, (m + 1) * SUB), part(h))
                        add = rates[(k * nh + m) * eh + h] * rate_ref[place] * (1.0 / LOG2E)
                        if lot[0] == 0:
                            dr_acc[place] = add
                        else:
                            dr_acc[place] += add
        value = lines_in(0, pair)
        g_all = lines_in(2, pair)
        skip = skip_ref[2 * pair : 2 * pair + 1, :] + skip_ref[2 * pair + 1 : 2 * pair + 2, :]
        dv = skip * g_all
        direct = jnp.sum(g_all * value, axis=0, keepdims=True)
        small = [direct[:, part(h)] for h in range(eh)]
        for k in range(2):
            d = 2 * pair + k
            drive = jnp.concatenate([fold(eight, k, h, count) for h in range(eh)], axis=1)
            pace = jnp.concatenate([fold(pace8, k, h, count) for h in range(eh)], axis=1)
            dv = dv + drive * jnp.concatenate([steps_p[k, h] for h in range(eh)], axis=1)
            d_before = (drive * value + pace * (1.0 / LOG2E)) * slope[d]
            bias_sum = jnp.sum(d_before, axis=0, keepdims=True)
            small += [bias_sum[:, part(h)] for h in range(eh)]
            put_wide(
                pair,
                lax.dot_general(
                    low[d], d_before, (((0,), (0,)), ((), ())), precision=HIGHEST,
                    preferred_element_type=jnp.float32,
                ),
            )
            put_wide(pair, dr_acc[d])
            dproj[:, k * group : k * group + rank] = lax.dot_general(
                d_before, step_weight_ref[d], (((1,), (1,)), ((), ())), precision=HIGHEST,
                preferred_element_type=jnp.float32,
            )
            lane = lax.broadcasted_iota(jnp.int32, (LANES, 2 * states), 1)
            flow = None
            for j in range(2 * states):
                x = wide_p[k, j // states, pl.ds(j % states, count, stride=states), :]
                pick = (lane == j).astype(jnp.bfloat16)
                term = jnp.dot(x.astype(jnp.bfloat16), pick, preferred_element_type=jnp.float32)
                flow = term if flow is None else flow + term
            dproj[:, k * group + rank : (k + 1) * group] = flow
        d_projected = dproj[...].astype(jnp.bfloat16)
        span = slice(2 * pair * group, 2 * (pair + 1) * group)
        leaving.append(lines_out(3, pair, back(d_projected, scan_weight_ref[:, span]) + dv))
        put(pair, pad_rows(*small))
        put_wide(pair, cross(d_projected, value.astype(jnp.bfloat16)))
        if pair == 0:
            early = sum_scatter(0)
        else:
            early = sum_across(0, early)
    finish(leaving[0])
    finish(leaving[1])
    d_values = take_home(3)
    early = sum_gather(0, early)

    d_mixed = jnp.concatenate(
        [d_values * silu_slope(mixed[:, :inner]), gate_grad[...]], axis=1
    ).astype(jnp.bfloat16)
    normed, norm_pull = jax.vjp(layer_norm, embedded_ref[...], norm_gain_ref[...])
    put_wide(1, cross(normed.astype(jnp.bfloat16), d_mixed))
    d_embedded, norm_grad = norm_pull(back(d_mixed, in_weight_ref[...]))
    put(1, pad_rows(norm_grad))
    late = sum_scatter(1)
    feature_ref[...] = (upstream_ref[...].astype(jnp.float32) + d_embedded).astype(jnp.bfloat16)
    late = sum_across(1, late)
    finish(early)
    late = sum_gather(1, late)

    def take_pair(pair):
        for d in (2 * pair, 2 * pair + 1):
            stepw_ref[d] = take_wide(pair, rank, inner)
            dr_ref[d] = take_wide(pair, states, inner)
        small = take(pair, -(-3 * eh // SUB) * SUB)
        for h in range(eh):
            for k in range(2):
                d = 2 * pair + k
                skip_grad_ref[d : d + 1, part(h)] = small[h : h + 1]
                stepb_ref[d : d + 1, part(h)] = small[(k + 1) * eh + h : (k + 1) * eh + h + 1]
        span = slice(2 * pair * group, 2 * (pair + 1) * group)
        scan_grad_ref[:, span] = take_wide(pair, 2 * group, inner).T

    small = take(0, SUB)
    for h in range(eh):
        gain_grad_ref[:, part(h)] = small[h : h + 1]
    out_grad_ref[...] = take_wide(0, inner, out_grad_ref.shape[1])
    take_pair(0)
    finish(late)
    take_pair(1)
    in_grad_ref[...] = take_wide(1, in_grad_ref.shape[0], in_grad_ref.shape[1])
    norm_grad_ref[...] = take(1, SUB)[0:1]


def general(
    classes, features, cotangent, table, norm_gain, in_weight, scan_weight, step_weight,
    step_bias, decay_log, skip_gain, output_gain, output_weight,
):
    tile_rows, tile_cols, model_width = features.shape
    inner = output_weight.shape[0]
    count = tile_rows * tile_cols
    rows, cols = lax.axis_size("row"), lax.axis_size("col")
    rank = step_weight.shape[1]
    states = decay_log.shape[1]
    group = rank + 2 * states
    eh = inner // LANES
    lines = max(tile_rows // cols, tile_cols // rows)
    grad_scale = float(count * rows * cols) ** (-0.5)
    rate2 = -jnp.exp(decay_log) * LOG2E
    embedded = embed(features, classes, table).reshape(count, model_width)
    f32 = jnp.float32
    shapes = [
        ((count, model_width), jnp.bfloat16),
        (in_weight.shape, f32),
        (scan_weight.shape, f32),
        (step_weight.shape, f32),
        (step_bias.shape, f32),
        (decay_log.shape, f32),
        (skip_gain.shape, f32),
        ((1, model_width), f32),
        ((1, inner), f32),
        (output_weight.shape, f32),
    ]
    scratch = [
        ((count, 2 * inner), f32),
        ((count, inner), f32),
        ((eh, count, LANES), f32),
        ((8, cols, count // cols, inner), f32),
        ((8, rows, count // rows, inner), f32),
        ((2, 2, 2, count * states, LANES), f32),
        ((2, 2, eh, count, LANES), f32),
        ((2, 2, eh, count, LANES), f32),
        ((4, count, inner), f32),
        ((4, count, rank), f32),
        ((2, 2, eh, (count + lines) * states, LANES), f32),
        ((2, eh, count * SUB, LANES), f32),
        ((2, eh, count * SUB, LANES), f32),
        ((1, eh, count, LANES), f32),
        ((count, 2 * group), f32),
        (decay_log.shape, f32),
    ]
    pair_tiles = eh * (2 * rank + 2 * states + 2 * group) // SUB + -(-3 * eh // SUB)
    least = (
        1 + inner * model_width // (LANES * SUB) + pair_tiles,
        1 + in_weight.size // (LANES * SUB) + pair_tiles,
    )
    tiles = tuple(-(-t // rows) * rows for t in least)
    for lot in range(2):
        chunk = (tiles[lot] // rows * SUB, LANES)
        scratch += [((rows,) + chunk, f32), ((rows - 1,) + chunk, f32), ((cols,) + chunk, f32), ((rows,) + chunk, f32)]
    feature_grad, *grads = pl.pallas_call(
        functools.partial(general_kernel, tile_rows, tile_cols, states, rank, grad_scale, tiles),
        out_shape=[jax.ShapeDtypeStruct(*s) for s in shapes],
        in_specs=[VMEM] * 11,
        out_specs=[VMEM] * 10,
        scratch_shapes=[pltpu.VMEM(*s) for s in scratch]
        + [
            pltpu.SemaphoreType.DMA((4, 2, 2, max(rows, cols))),
            pltpu.SemaphoreType.DMA((2, 3, 2, max(rows, cols))),
        ],
        compiler_params=pltpu.CompilerParams(
            vmem_limit_bytes=BIG, collective_id=1, has_side_effects=True
        ),
    )(
        embedded, cotangent.reshape(count, model_width), norm_gain[None], in_weight, scan_weight,
        step_weight, step_bias, rate2, skip_gain, output_gain[None], output_weight,
    )
    feature_grad = feature_grad.reshape(tile_rows, tile_cols, model_width)
    grads[6], grads[7] = grads[6][0], grads[7][0]
    return (feature_grad, *grads)


def split2(x):
    high = x.astype(jnp.bfloat16)
    return high, (x - high.astype(jnp.float32)).astype(jnp.bfloat16)


def dot(a, b):
    return jnp.dot(a, b, preferred_element_type=jnp.float32)


def greet_all():
    barrier = pltpu.get_barrier_semaphore()
    rows, cols = lax.axis_size("row"), lax.axis_size("col")
    r, c = lax.axis_index("row"), lax.axis_index("col")
    for dr in range(rows):
        for dc in range(cols):
            if dr or dc:
                there = {"row": lax.rem(r + dr, rows), "col": lax.rem(c + dc, cols)}
                pl.semaphore_signal(barrier, inc=1, device_id=there, device_id_type=MESH)
    pl.semaphore_wait(barrier, rows * cols - 1)


def lots_of(rows, inner, model_width, states, rank, group, eh):
    pair = (rank + states + group) * 2 * eh + -(-3 * eh // SUB) * SUB
    gated = SUB + inner * model_width // LANES + model_width * eh
    per = SUB * rows
    return tuple(-(-n // per) * per for n in (gated, pair, pair, model_width * eh))


def fast_kernel(
    tile_rows, tile_cols, states, rank,
    features_ref, classes_ref, table_ref, upstream_ref, norm_gain_ref, in_weight_ref, sw_ref,
    step_weight_ref, step_bias_ref, decay_ref, skip_ref, output_gain_ref, output_weight_ref,
    feature_ref, full0, full1, full2, full3,
    home, emb_s0, emb_s1, emb_r0, emb_r1, cot_s0, cot_s1, cot_r0, cot_r1,
    back_s0, back_s1, back_r0, back_r1, y_s0, y_s1, y_r0, y_r1,
    spread0, spread1, wpk, swp, cmat, rate_s, normed_s, mixed_s, value_s, proj_s, tok, slope,
    wide, flows, hist, pace_t, drive_t, g_t, dd_t, dp_t, bufs, bufs_tok, probe_t, lhs, dval, dr_s, in_acc,
    mine0, from0, side0, mine1, from1, side1, mine2, from2, side2, mine3, from3, side3,
    sems, ysems, sumsems,
):
    f32, bf16 = jnp.float32, jnp.bfloat16
    count, inner = tile_rows * tile_cols, output_weight_ref.shape[0]
    model = features_ref.shape[1]
    rows, cols = lax.axis_size("row"), lax.axis_size("col")
    me_r, me_c = lax.axis_index("row"), lax.axis_index("col")
    eh = inner // LANES
    group = rank + 2 * states
    lines = (tile_rows // cols, tile_cols // rows)
    length = (count // lines[0], count // lines[1])
    copies_m = tuple(SUB // (2 * n) for n in lines)
    per_n = tuple(states // m for m in copies_m)
    tall = tuple(SUB * n for n in length)
    blocks = count // SUB
    axes = ("col", "row")
    sizes = (cols, rows)
    zero = jnp.zeros((SUB, LANES), f32)
    sub = lax.broadcasted_iota(jnp.int32, (SUB, LANES), 0)
    even = lax.rem(sub, 2) == 0
    pos = sub // 2
    pos_even = lax.rem(pos, 2) == 0
    pos_edge = (pos == 0) | (pos == 3)
    low_half = sub < 4

    def part(h):
        return slice(h * LANES, (h + 1) * LANES)

    def tile(b):
        return pl.ds(pl.multiple_of(b * SUB, SUB), SUB)

    def step_tile(p, b):
        return tile(b + (length[0] if p else 0))

    def tile2(b):
        return pl.ds(pl.multiple_of(b * 2 * SUB, 2 * SUB), 2 * SUB)

    greet_all()

    def pack(src, dst, p):
        if p == 0:
            for rho in range(tile_rows):
                c, i = rho // lines[0], rho % lines[0]
                for j in range(2):
                    dst[c, pl.ds(2 * i + j, tile_cols // 2, stride=SUB), :] = src[
                        pl.ds(rho * tile_cols + j, tile_cols // 2, stride=2), :
                    ]
        else:
            for r in range(rows):
                for j in range(2):
                    dst[r, pl.ds(j, tile_rows, stride=2), :] = src[
                        pl.ds(2 * r + j, tile_rows, stride=tile_cols), :
                    ]

    def unpack(src, dst, p):
        if p == 0:
            for rho in range(tile_rows):
                c, i = rho // lines[0], rho % lines[0]
                for j in range(2):
                    dst[pl.ds(rho * tile_cols + j, tile_cols // 2, stride=2), :] = src[
                        c, pl.ds(2 * i + j, tile_cols // 2, stride=SUB), :
                    ]
        else:
            for r in range(rows):
                for j in range(2):
                    dst[pl.ds(2 * r + j, tile_rows, stride=tile_cols), :] = src[
                        r, pl.ds(j, tile_rows, stride=2), :
                    ]

    def batch(src, dst, amount, send, recv):
        return pltpu.make_async_remote_copy(
            src_ref=src.at[pl.ds(0, amount)], dst_ref=dst.at[pl.ds(0, amount)], send_sem=send,
            recv_sem=recv, device_id={"row": me_r, "col": me_c}, device_id_type=MESH,
        )

    def exchange(turn, p, src, dst):
        size, axis = sizes[p], axes[p]
        me = lax.axis_index(axis)
        for d in range(1, size):
            target = lax.rem(me + d, size)
            copy = pltpu.make_async_remote_copy(
                src_ref=src.at[target],
                dst_ref=dst.at[me],
                send_sem=sems.at[turn, p, 0],
                recv_sem=sems.at[turn, p, 1],
                device_id={axis: target},
                device_id_type=MESH,
            )
            copy.start()
        dst[me] = src[me]
        return [batch(src, dst, size - 1, sems.at[turn, p, 0], sems.at[turn, p, 1])]

    def swap(p, src, dst):
        for dr in range(rows):
            for dc in range(cols):
                r, c = lax.rem(me_r + dr, rows), lax.rem(me_c + dc, cols)
                if p == 0:
                    there, here = c * rows + r, me_r * cols + me_c
                else:
                    there, here = r * cols + c, me_c * rows + me_r
                if dr == 0 and dc == 0:
                    dst[here] = src[there]
                    continue
                copy = pltpu.make_async_remote_copy(
                    src_ref=src.at[there],
                    dst_ref=dst.at[here],
                    send_sem=ysems.at[p, 0],
                    recv_sem=ysems.at[p, 1],
                    device_id={"row": r, "col": c},
                    device_id_type=MESH,
                )
                copy.start()
        return [batch(src, dst, rows * cols - 1, ysems.at[p, 0], ysems.at[p, 1])]

    def arrived(copies):
        for copy in copies:
            copy.wait_recv()

    def sent(copies):
        for copy in copies:
            copy.wait_send()

    emb_s, emb_r = (emb_s0, emb_s1), (emb_r0, emb_r1)
    cot_s, cot_r = (cot_s0, cot_s1), (cot_r0, cot_r1)
    back_s, back_r = (back_s0, back_s1), (back_r0, back_r1)
    y_s, y_r = (y_s0, y_s1), (y_r0, y_r1)
    spreads = (spread0, spread1)
    pending = []
    half_n, few_n = SUB, SUB // 2
    y_t = dd_t

    def group_tile(p, g, t):
        return tile(g * length[p] + t)

    def added(ref, p, h, b, groups):
        total = ref[h, group_tile(p, 0, b), :]
        for g in range(1, groups):
            total = total + ref[h, group_tile(p, g, b), :]
        return total

    token = lax.broadcasted_iota(jnp.int32, (count, tile_rows), 0)
    lane = lax.broadcasted_iota(jnp.int32, (count, tile_rows), 1)
    of_row = jnp.where(token // tile_cols == lane, 1.0, 0.0).astype(bf16)
    labels = dot(of_row, classes_ref[...].astype(f32).astype(bf16))
    token = lax.broadcasted_iota(jnp.int32, (count, tile_cols), 0)
    lane = lax.broadcasted_iota(jnp.int32, (count, tile_cols), 1)
    labels = jnp.where(lax.rem(token, tile_cols) == lane, labels, 0.0).astype(bf16)
    labels = dot(labels, jnp.ones((tile_cols, LANES), bf16))
    lane = lax.broadcasted_iota(jnp.int32, (count, LANES), 1).astype(f32)
    onehot = jnp.where(labels == lane, 1.0, 0.0).astype(bf16)
    entries = table_ref[...]
    lookup = None
    for i in range(3):
        rounded = entries.astype(bf16).astype(f32)
        rest = jnp.zeros((LANES - entries.shape[0], model), f32)
        term = dot(onehot, jnp.concatenate([rounded, rest], axis=0).astype(bf16))
        lookup = term if lookup is None else lookup + term
        entries = entries - rounded
    home[...] = features_ref[...].astype(f32) + lookup
    pack(home, emb_s1, 1)
    emb1 = exchange(0, 1, emb_s1, emb_r1)
    pack(home, emb_s0, 0)
    emb0 = exchange(0, 0, emb_s0, emb_r0)
    home[...] = upstream_ref[...].astype(f32)
    pack(home, cot_s0, 0)
    cot0 = exchange(1, 0, cot_s0, cot_r0)
    pack(home, cot_s1, 1)
    cot1 = exchange(1, 1, cot_s1, cot_r1)
    pending += emb1 + emb0 + cot0 + cot1

    key_row = lax.broadcasted_iota(jnp.int32, (LANES, 2 * LANES), 0)
    lane_tile = lax.broadcasted_iota(jnp.int32, (LANES, 2 * LANES), 1) // LANES
    for p in range(2):
        which = lax.rem(key_row, 2 * states) // states
        key = which * per_n[p] + lax.rem(key_row, per_n[p])
        key = jnp.where(key_row < 4 * states, key - lane_tile, -8 * states)
        for q in range(per_n[p]):
            spreads[p][:, 2 * q * LANES : 2 * (q + 1) * LANES] = jnp.where(
                key == 2 * q, 1.0, 0.0
            ).astype(bf16)
    sw32 = sw_ref[...].astype(f32)
    for d in range(4):
        off = d * group
        low_w = sw32[off : off + rank]
        wpk[d] = jnp.concatenate(
            [sw32[off + rank : off + group], low_w,
             jnp.zeros((LANES - group, inner), f32)], axis=0
        ).astype(bf16)
        step_w = step_weight_ref[d]
        w1, w2 = split2(step_w)
        w3 = (step_w - w1.astype(f32) - w2.astype(f32)).astype(bf16)
        blank = jnp.zeros((rank, inner), f32)
        left = jnp.concatenate([low_w, low_w, low_w, blank], axis=0).astype(bf16)
        right = jnp.concatenate(
            [w1.astype(f32), w2.astype(f32), w3.astype(f32), blank], axis=0
        ).astype(bf16)
        c_high, c_low = split2(cross(left, right))
        cmat[d, 0] = c_high
        cmat[d, 1] = c_low
        for i, w in enumerate((w1, w2)):
            swp[d, i] = jnp.concatenate(
                [jnp.zeros((2 * states, inner), f32), w.astype(f32),
                 jnp.zeros((LANES - group, inner), f32)], axis=0
            ).astype(bf16)
        rate = -jnp.exp(decay_ref[d]) * LOG2E
        p, k = d // 2, d % 2
        for n in range(states):
            m, n1 = n // per_n[p], n % per_n[p]
            for h in range(eh):
                row = jnp.broadcast_to(rate[n : n + 1, part(h)], (SUB, LANES))
                if p == 0:
                    mask = lax.rem(sub, 2) == k
                else:
                    mask = pos == 2 * m + k
                at = slice(n1 * SUB, (n1 + 1) * SUB)
                if k == 0 and m == 0:
                    rate_s[p, h, at, :] = row
                else:
                    rate_s[p, h, at, :] = jnp.where(mask, row, rate_s[p, h, at, :])

    def to_scan(p, *moves):
        def one(b, carry):
            for move in moves:
                one_of(b, *move)
            return carry

        def one_of(b, first, second, store):
            mirror = blocks - 1 - b
            x0, x1 = first(tile(b)), second(tile(mirror))
            if p == 0:
                z = jnp.where(even, x1, x0)
                store(2 * b, jnp.where(even, x0, x1))
                store(
                    2 * b + 1,
                    jnp.where(even, pltpu.roll(z, SUB - 1, 0), pltpu.roll(z, 1, 0)),
                )
            else:
                u = jnp.where(pos_even, x0, x1)
                v = pltpu.roll(u, 4, 0)
                u2 = pltpu.roll(jnp.where(pos_even, x1, x0), 2, 0)
                v2 = pltpu.roll(u2, 4, 0)
                store(4 * b, jnp.where(pos_edge, u, v))
                store(4 * b + 1, jnp.where(low_half, v2, u2))
                store(4 * b + 2, jnp.where(pos_edge, v, u))
                store(4 * b + 3, jnp.where(low_half, u2, v2))

        lax.fori_loop(0, blocks, one, 0, unroll=max(2, 4 // len(moves)))

    def from_scan(p, *moves):
        def one(b, carry):
            for move in moves:
                one_of(b, *move)
            return carry

        def one_of(b, load, store):
            mirror = blocks - 1 - b
            if p == 0:
                s0, s1 = load(2 * b), load(2 * b + 1)
                store(0, tile(b), jnp.where(even, s0, pltpu.roll(s1, 1, 0)))
                store(1, tile(mirror), jnp.where(even, pltpu.roll(s1, SUB - 1, 0), s0))
            else:
                a = []
                for i in range(4):
                    s = load(4 * b + i)
                    s = s + pltpu.roll(s, 4, 0)
                    a.append(pltpu.roll(s, 2, 0) if i % 2 else s)
                store(
                    0, tile(b),
                    jnp.where(low_half, jnp.where(pos == 0, a[0], a[1]), jnp.where(pos == 2, a[2], a[3])),
                )
                store(
                    1, tile(mirror),
                    jnp.where(low_half, jnp.where(pos == 0, a[3], a[2]), jnp.where(pos == 2, a[1], a[0])),
                )

        lax.fori_loop(0, blocks, one, 0, unroll=max(2, 4 // len(moves)))

    def put_step(ref, p, b, x):
        ref[step_tile(p, b), :] = x

    def put_at(ref, b, x):
        ref[tile(b), :] = x

    def put_probe(b, x):
        probe_t[tile(b), :] = x

    def prologue(p):
        embedded = emb_r[p][...].reshape(count, model)
        normed = layer_norm(embedded, norm_gain_ref[...]).astype(bf16)
        normed_s[p] = normed
        mixed_s[p] = dot(normed, in_weight_ref[...])
        value = jax.nn.silu(mixed_s[p, :, :inner]).astype(bf16)
        value_s[p] = value
        value32 = value.astype(f32)
        for k in range(2):
            d = 2 * p + k
            proj_s[p, k] = back(value, wpk[d])
            before = dot(value, cmat[d, 0]) + dot(value, cmat[d, 1]) + step_bias_ref[d : d + 1, :]
            slope[p, k] = jax.nn.sigmoid(before)
            pace = softplus(before)
            for h in range(eh):
                tok[p, k, h] = pace[:, part(h)]
        moves = [(lambda at: proj_s[p, 0, at, :], lambda at: proj_s[p, 1, at, :], put_probe)]
        for h in range(eh):
            bufs_tok[0, 0, h] = value32[:, part(h)]
            moves.append(
                (lambda at, h=h: tok[p, 0, h, at, :], lambda at, h=h: tok[p, 1, h, at, :],
                 functools.partial(put_step, pace_t.at[h], p))
            )
            moves.append(
                (lambda at, h=h: tok[p, 0, h, at, :] * bufs_tok[0, 0, h, at, :],
                 lambda at, h=h: tok[p, 1, h, at, :] * bufs_tok[0, 0, h, at, :],
                 functools.partial(put_step, drive_t.at[h], p))
            )
        to_scan(p, *moves)
        size_of = tall[p]
        x = jnp.where(keep_lanes(p, size_of), probe_t[:size_of, :], 0.0)
        high = x.astype(bf16).astype(f32)
        lhs[:size_of, :] = (high + pltpu.roll(x - high, 2 * states, 1)).astype(bf16)
        if copies_m[p] > 1:
            row = lax.broadcasted_iota(jnp.int32, (size_of, LANES), 0)
            x = jnp.where(lax.rem(row, SUB) < 4, x, pltpu.roll(x, LANES - per_n[p], 1))
        probe_t[:size_of, :] = x
        chunk = count
        for q in range(per_n[p]):
            w, n1 = 2 * q // per_n[p], 2 * q % per_n[p]
            for s in range(size_of // chunk):
                if q % 3 == 2:
                    for j in range(2):
                        at = (n1 + j) * size_of + s * chunk
                        col = w * states + n1 + j
                        wide[p, w, at : at + chunk, :] = jnp.broadcast_to(
                            probe_t[s * chunk : (s + 1) * chunk, col : col + 1], (chunk, LANES)
                        )
                    continue
                out = dot(
                    lhs[s * chunk : (s + 1) * chunk, :],
                    spreads[p][:, 2 * q * LANES : 2 * (q + 1) * LANES],
                )
                for j in range(2):
                    at = (n1 + j) * size_of + s * chunk
                    wide[p, w, at : at + chunk, :] = out[:, part(j)]

    def keep_lanes(p, height):
        lane = lax.broadcasted_iota(jnp.int32, (height, LANES), 1)
        keep = lane < 2 * states
        if copies_m[p] > 1:
            row = lax.broadcasted_iota(jnp.int32, (height, LANES), 0)
            m = lax.rem(row, SUB) // (SUB // copies_m[p])
            keep = keep & (lax.rem(lane, states) // per_n[p] == m)
        return keep

    def forward(p):
        high, stride = tall[p], tall[p] + SUB
        for h in range(eh):
            for n in range(per_n[p]):
                hist[p, h, n * stride : n * stride + SUB, :] = zero
        for g in range(per_n[p] // half_n):
            ns = range(g * half_n, (g + 1) * half_n)

            def step(t, carry, g=g, ns=ns):
                at = tile(t)
                pace = [pace_t[h, step_tile(p, t), :] for h in range(eh)]
                drive = [drive_t[h, step_tile(p, t), :] for h in range(eh)]
                y = [None] * eh
                new = []
                for i, n in enumerate(ns):
                    row = tile(n * (high // SUB) + t)
                    slot = tile(n * (stride // SUB) + t + 1)
                    source, probe = wide[p, 0, row, :], wide[p, 1, row, :]
                    for h in range(eh):
                        a = jnp.exp2(pace[h] * rate_s[p, h, n * SUB : (n + 1) * SUB, :])
                        state = a * carry[i * eh + h] + source * drive[h]
                        hist[p, h, slot, :] = state
                        new.append(state)
                        term = probe * state
                        y[h] = term if y[h] is None else y[h] + term
                for h in range(eh):
                    y_t[h, group_tile(p, g, t), :] = y[h]
                return tuple(new)

            lax.fori_loop(0, length[p], step, (zero,) * (half_n * eh), unroll=8)
        moves = []
        for h in range(eh):

            def put_y(k, at, x, h=h):
                bufs_tok[k, 0, h, at, :] = x

            moves.append((lambda b, h=h: added(y_t, p, h, b, per_n[p] // half_n), put_y))
        from_scan(p, *moves)
        for h in range(eh):
            y_s[p][:, :, part(h)] = (bufs_tok[0, 0, h] + bufs_tok[1, 0, h]).reshape(blocks, SUB, LANES)

    def gate(p):
        value = value_s[p].astype(f32)
        skips = jnp.sum(skip_ref[...], axis=0, keepdims=True)
        total = (
            y_s[p][...].reshape(count, inner) + y_r[p][...].reshape(count, inner) + skips * value
        )
        upstream = cot_r[p][...].reshape(count, model).astype(bf16)
        d_gated = back(upstream, output_weight_ref[...])
        gated, pull = jax.vjp(gate_output, total, mixed_s[p, :, inner:], output_gain_ref[...])
        d_total, d_gate_in, gain_grad = pull(d_gated)
        dval[p] = d_total
        if p == 0:
            put(0, pad_rows(*[gain_grad[:, part(h)] for h in range(eh)]))
            put_wide(0, cross(gated.astype(bf16), upstream))
            d_gate = d_gate_in.astype(bf16)
            gate16 = d_gate
            put_wide(0, cross(normed_s[p], d_gate))
        else:
            gate16 = None

        moves = []
        for h in range(eh):
            load = lambda at, h=h: dval[p, at, part(h)]
            moves.append((load, load, functools.partial(put_at, g_t.at[h])))
        to_scan(p, *moves)
        return gate16

    sums = (
        (mine0, from0, side0, full0), (mine1, from1, side1, full1),
        (mine2, from2, side2, full2), (mine3, from3, side3, full3),
    )
    fill = [0] * 4

    def put(lot, x):
        mine = sums[lot][0]
        per = mine.shape[1] // SUB
        for i in range(x.shape[0] // SUB):
            n = fill[lot]
            at = (n % per) * SUB
            mine[n // per, at : at + SUB, :] = x[i * SUB : (i + 1) * SUB]
            fill[lot] += 1

    def put_wide(lot, x):
        for h in range(x.shape[1] // LANES):
            put(lot, x[:, h * LANES : (h + 1) * LANES])

    def pad_rows(*rows_in):
        missing = -len(rows_in) % SUB
        return jnp.concatenate(list(rows_in) + [jnp.zeros((missing, LANES), f32)], axis=0)

    def pad_lot(lot):
        mine = sums[lot][0]
        while fill[lot] < rows * mine.shape[1] // SUB:
            put(lot, zero)

    def spread(lot, phase, axis, source, result, whole):
        size = lax.axis_size(axis)
        me = lax.axis_index(axis)
        for d in range(1, size):
            target = lax.rem(me + d, size)
            copy = pltpu.make_async_remote_copy(
                src_ref=source(target),
                dst_ref=result(me, d),
                send_sem=sumsems.at[lot, phase, 0],
                recv_sem=sumsems.at[lot, phase, 1],
                device_id={axis: target},
                device_id_type=MESH,
            )
            copy.start()
        out = [batch(whole, whole, size - 1, sumsems.at[lot, phase, 0], sumsems.at[lot, phase, 1])]
        pending.extend(out)
        return out

    def sum_scatter(lot):
        mine, other, side, full = sums[lot]
        pad_lot(lot)
        return spread(lot, 0, "row", lambda t: mine.at[t], lambda me, d: other.at[d - 1], other)

    def sum_across(lot, copies):
        mine, other, side, full = sums[lot]
        arrived(copies)
        acc = mine[me_r]
        for d in range(rows - 1):
            acc = acc + other[d]
        side[me_c] = acc
        return spread(lot, 1, "col", lambda t: side.at[me_c], lambda m, d: side.at[m], side)

    def sum_gather(lot, copies):
        mine, other, side, full = sums[lot]
        arrived(copies)
        acc = side[0]
        for d in range(1, cols):
            acc = acc + side[d]
        full[me_r] = acc
        return spread(lot, 2, "row", lambda t: full.at[me_r], lambda m, d: full.at[m], full)

    def backward(p):
        high, stride = tall[p], tall[p] + SUB
        for g in range(per_n[p] // few_n):
            ns = range(g * few_n, (g + 1) * few_n)

            def step(i, carry, g=g, ns=ns):
                grads, rates, t = carry
                at = tile(t)
                pace = [pace_t[h, step_tile(p, t), :] for h in range(eh)]
                drive = [drive_t[h, step_tile(p, t), :] for h in range(eh)]
                gs = [g_t[h, at, :] for h in range(eh)]
                dd, dp = [None] * eh, [None] * eh
                new, new_rates = [], []
                for i, n in enumerate(ns):
                    row = tile(n * (high // SUB) + t)
                    earlier = tile(n * (stride // SUB) + t)
                    current = tile(n * (stride // SUB) + t + 1)
                    source, probe = wide[p, 0, row, :], wide[p, 1, row, :]
                    flow = read = None
                    for h in range(eh):
                        j = i * eh + h
                        rate = rate_s[p, h, n * SUB : (n + 1) * SUB, :]
                        grad = grads[j] + probe * gs[h]
                        term = grad * drive[h]
                        flow = term if flow is None else flow + term
                        term = gs[h] * hist[p, h, current, :]
                        read = term if read is None else read + term
                        term = grad * source
                        dd[h] = term if dd[h] is None else dd[h] + term
                        carried = jnp.exp2(pace[h] * rate) * grad
                        q = carried * hist[p, h, earlier, :]
                        term = q * rate
                        dp[h] = term if dp[h] is None else dp[h] + term
                        new_rates.append(rates[j] + q * pace[h])
                        new.append(carried)
                    if n % 2 == 0:
                        kept = (flow, read)
                        continue
                    place = tile2((n // 2) * (high // SUB) + t)
                    for w, x in enumerate((flow, read)):
                        both = jnp.concatenate([kept[w], x], axis=0)
                        flows[w, place, :] = both.astype(bf16)
                for h in range(eh):
                    dd_t[h, group_tile(p, g, t), :] = dd[h]
                    dp_t[h, group_tile(p, g, t), :] = dp[h]
                return tuple(new), tuple(new_rates), t - 1

            chains = (zero,) * (few_n * eh)
            unused, rates, end = lax.fori_loop(
                0, length[p], step, (chains, chains, jnp.int32(length[p] - 1)), unroll=4
            )
            for i, n in enumerate(ns):
                for h in range(eh):
                    place = slice(n * SUB, (n + 1) * SUB)
                    dr_s[h, place, :] = rates[i * eh + h] * rate_s[p, h, place, :] * (1.0 / LOG2E)

    def finish_pair(p, gate16):
        lot = p + 1
        high = tall[p]
        chunk = count
        wide_high = 2 * chunk
        lane = lax.broadcasted_iota(jnp.int32, (wide_high, LANES), 1)
        row = lax.broadcasted_iota(jnp.int32, (wide_high, LANES), 0)
        mine = lax.rem(lane, 2) == lax.rem(row // SUB, 2)
        keep = keep_lanes(p, wide_high) & mine

        def ones_of(w, a):
            at = (w * per_n[p] + 2 * a) * LANES
            return spreads[p][:, at : at + LANES] + spreads[p][:, at + LANES : at + 2 * LANES]

        for s in range(high // chunk):
            flow = None
            for w in range(2):
                for a in range(0, per_n[p] // 2, 2):
                    at = [(a + i) * 2 * high + s * wide_high for i in range(2)]
                    left = jnp.concatenate([flows[w, i : i + wide_high, :] for i in at], axis=1)
                    right = jnp.concatenate([ones_of(w, a), ones_of(w, a + 1)], axis=1)
                    term = back(left, right)
                    flow = term if flow is None else flow + term
            flow = jnp.where(keep, flow, 0.0).reshape(chunk // SUB, 2, SUB, LANES)
            probe_t[s * chunk : (s + 1) * chunk, :] = (flow[:, 0] + flow[:, 1]).reshape(chunk, LANES)

        def put_flow(k, at, x):
            bufs[k, at, :] = x

        moves = [(lambda b: probe_t[tile(b), :], put_flow)]
        value16 = value_s[p]
        value = value16.astype(f32)
        d_total = dval[p]
        direct = jnp.sum(d_total * value, axis=0, keepdims=True)
        small = [direct[:, part(h)] for h in range(eh)]
        skip = skip_ref[2 * p : 2 * p + 1, :] + skip_ref[2 * p + 1 : 2 * p + 2, :]
        dv = skip * d_total
        for h in range(eh):
            for which, source in enumerate((dd_t, dp_t)):

                def put_tok(k, at, x, which=which, h=h):
                    bufs_tok[k, which, h, at, :] = x

                moves.append(
                    (lambda b, source=source, h=h: added(source, p, h, b, per_n[p] // few_n), put_tok)
                )
        from_scan(p, *moves)
        for k in range(2):
            d = 2 * p + k
            drive = jnp.concatenate([bufs_tok[k, 0, h] for h in range(eh)], axis=1)
            pull = jnp.concatenate([bufs_tok[k, 1, h] for h in range(eh)], axis=1)
            pace = jnp.concatenate([tok[p, k, h] for h in range(eh)], axis=1)
            dv = dv + drive * pace
            d_before = (drive * value + pull * (1.0 / LOG2E)) * slope[p, k]
            b_high, b_low = split2(d_before)
            bias_sum = jnp.sum(d_before, axis=0, keepdims=True)
            small += [bias_sum[:, part(h)] for h in range(eh)]
            d_proj = (
                bufs[k, :count, :] + back(b_high, swp[d, 0]) + back(b_low, swp[d, 0])
                + back(b_high, swp[d, 1])
            ).astype(bf16)
            dv = dv + dot(d_proj, wpk[d])
            put_wide(lot, cross(proj_s[p, k].astype(bf16), b_high)[2 * states : group])
            grad = cross(d_proj, value16)
            put_wide(lot, grad[2 * states : group])
            put_wide(lot, grad[: 2 * states])
            for h in range(eh):
                for m in range(copies_m[p]):
                    acc = None
                    for line in range(lines[p]):
                        s = 2 * line + k if p == 0 else 4 * m + 2 * k + line
                        term = dr_s[h, pl.ds(s, per_n[p], stride=SUB), :]
                        acc = term if acc is None else acc + term
                    put(lot, acc)
        put(lot, pad_rows(*small))
        steps = [sum_scatter(lot)]
        d_val = (dv * silu_slope(mixed_s[p, :, :inner])).astype(bf16)
        grad = cross(normed_s[p], d_val)
        if p == 0:
            in_acc[...] = grad
            return steps[0], jnp.concatenate([d_val, gate16], axis=1)
        put_wide(3, in_acc[...] + grad)
        return steps[0], sum_scatter(3), d_val

    def go_home(p, d_mixed):
        d_normed = back(d_mixed, in_weight_ref[:, : d_mixed.shape[1]])
        unused, pull = jax.vjp(
            lambda x: layer_norm(x, norm_gain_ref[...]), emb_r[p][...].reshape(count, model)
        )
        back_s[p][...] = pull(d_normed)[0].reshape(back_s[p].shape)
        out = exchange(2, p, back_s[p], back_r[p])
        pending.extend(out)
        return out

    arrived(emb1)
    prologue(1)
    forward(1)
    y1 = swap(1, y_s1, y_r0)
    pending += y1
    arrived(emb0)
    prologue(0)
    forward(0)
    y0 = swap(0, y_s0, y_r1)
    pending += y0
    arrived(y1)
    arrived(cot0)
    gate16 = gate(0)
    first = sum_scatter(0)
    backward(0)
    second, d_mixed = finish_pair(0, gate16)
    home0 = go_home(0, d_mixed)
    first = sum_across(0, first)
    arrived(y0)
    arrived(cot1)
    gate(1)
    backward(1)
    flying = [sum_across(1, second)]

    third, fourth, d_mixed = finish_pair(1, None)
    home1 = go_home(1, d_mixed)
    first = sum_gather(0, first)
    third = sum_across(2, third)
    flying.append(sum_gather(1, flying[0]))
    sent(pending[:-4])
    del pending[:-4]
    home[...] = upstream_ref[...].astype(f32)
    arrived(home0)
    unpack(back_r0, bufs.at[0], 0)
    home[...] = home[...] + bufs[0, :count, :]
    fourth = sum_across(3, fourth)
    third = sum_gather(2, third)
    arrived(home1)
    unpack(back_r1, bufs.at[1], 1)
    feature_ref[...] = (home[...] + bufs[1, :count, :]).astype(bf16)
    fourth = sum_gather(3, fourth)
    for copies in (first, flying[1], third, fourth):
        arrived(copies)
    sent(pending)


def unpack_kernel(
    states, rank, grad_scale,
    feature_in, full0, full1, full2, full3, in_weight_ref, norm_gain_ref,
    feature_ref, in_grad_ref, scan_grad_ref, stepw_ref, stepb_ref, dr_ref, skip_grad_ref,
    norm_grad_ref, gain_grad_ref, out_grad_ref,
):
    feature_ref[...] = feature_in[...]
    inner = out_grad_ref.shape[0]
    eh = inner // LANES
    group = rank + 2 * states
    taken = [0] * 4
    lots = (full0, full1, full2, full3)

    def take(lot, height):
        at = taken[lot]
        taken[lot] += height
        return lots[lot][at : at + height, :] * grad_scale

    def take_wide(lot, out, at, height, width):
        for h in range(width // LANES):
            out[at : at + height, h * LANES : (h + 1) * LANES] = take(lot, height)

    def part(h):
        return slice(h * LANES, (h + 1) * LANES)

    small = take(0, SUB)
    for h in range(eh):
        gain_grad_ref[:, part(h)] = small[h : h + 1]
    take_wide(0, out_grad_ref, 0, inner, out_grad_ref.shape[1])
    model = in_grad_ref.shape[0]
    for h in range(eh):
        in_grad_ref[:, inner + h * LANES : inner + (h + 1) * LANES] = take(0, model)
    for p in range(2):
        lot = p + 1
        for k in range(2):
            d = 2 * p + k
            take_wide(lot, stepw_ref.at[d], 0, rank, inner)
            take_wide(lot, scan_grad_ref, d * group, rank, inner)
            take_wide(lot, scan_grad_ref, d * group + rank, 2 * states, inner)
            take_wide(lot, dr_ref.at[d], 0, states, inner)
        small = take(lot, -(-3 * eh // SUB) * SUB)
        for h in range(eh):
            for k in range(2):
                d = 2 * p + k
                skip_grad_ref[d : d + 1, part(h)] = small[h : h + 1]
                stepb_ref[d : d + 1, part(h)] = small[(k + 1) * eh + h : (k + 1) * eh + h + 1]
    take_wide(3, in_grad_ref, 0, model, inner)
    weighed = in_grad_ref[...] * in_weight_ref[...].astype(jnp.float32)
    norm_grad_ref[...] = (
        lax.dot_general(
            jnp.ones((SUB, weighed.shape[1]), jnp.float32), weighed, (((1,), (1,)), ((), ())),
            precision=HIGHEST, preferred_element_type=jnp.float32,
        )[0:1]
        / norm_gain_ref[...]
    )


def fast(
    classes, features, cotangent, table, norm_gain, in_weight, scan_weight, step_weight,
    step_bias, decay_log, skip_gain, output_gain, output_weight,
):
    tile_rows, tile_cols, model = features.shape
    inner = output_weight.shape[0]
    count = tile_rows * tile_cols
    rows, cols = lax.axis_size("row"), lax.axis_size("col")
    rank, states = step_weight.shape[1], decay_log.shape[1]
    group = rank + 2 * states
    eh = inner // LANES
    grad_scale = float(count * rows * cols) ** (-0.5)
    f32, bf16 = jnp.float32, jnp.bfloat16
    talls = (SUB * count // (tile_rows // cols), SUB * count // (tile_cols // rows))
    tall, sum_tall = max(talls), sum(talls)
    blocks = count // SUB
    lots = lots_of(rows, inner, model, states, rank, group, eh)
    per_row = ((cols, count // cols, model), (rows, count // rows, model))
    scratch = [((count, model), f32)]
    for name in range(6):
        scratch += [(per_row[0], f32), (per_row[1], f32)]
    scratch += [((blocks, SUB, inner), f32)] * 4
    scratch += [
        ((LANES, 2 * states * LANES), bf16),
        ((LANES, 2 * states * LANES // 2), bf16),
        ((4, LANES, inner), bf16),
        ((4, 2, LANES, inner), bf16),
        ((4, 2, inner, inner), bf16),
        ((2, eh, states * SUB, LANES), f32),
        ((2, count, model), bf16),
        ((2, count, 2 * inner), f32),
        ((2, count, inner), bf16),
        ((2, 2, count, LANES), f32),
        ((2, 2, eh, count, LANES), f32),
        ((2, 2, count, inner), f32),
        ((2, 2, 2 * count * states, LANES), f32),
        ((2, 2 * count * states, LANES), bf16),
        ((2, eh, 2 * count * states + states * SUB, LANES), f32),
        ((eh, sum_tall, LANES), f32),
        ((eh, sum_tall, LANES), f32),
        ((eh, tall, LANES), f32),
        ((eh, 2 * tall, LANES), f32),
        ((eh, 2 * tall, LANES), f32),
        ((2, count, LANES), f32),
        ((2, 2, eh, count, LANES), f32),
        ((tall, LANES), f32),
        ((tall, LANES), bf16),
        ((2, count, inner), f32),
        ((eh, states * SUB, LANES), f32),
        ((model, inner), f32),
    ]
    for lot in lots:
        chunk = (lot // rows, LANES)
        scratch += [((rows,) + chunk, f32), ((rows - 1,) + chunk, f32), ((cols,) + chunk, f32)]
    feature, *full = pl.pallas_call(
        functools.partial(fast_kernel, tile_rows, tile_cols, states, rank),
        out_shape=[
            jax.ShapeDtypeStruct((count, model), bf16),
        ]
        + [jax.ShapeDtypeStruct((rows, lot // rows, LANES), f32) for lot in lots],
        in_specs=[VMEM] * 13,
        out_specs=[VMEM] * 5,
        scratch_shapes=[pltpu.VMEM(*s) for s in scratch]
        + [
            pltpu.SemaphoreType.DMA((3, 2, 2)),
            pltpu.SemaphoreType.DMA((2, 2)),
            pltpu.SemaphoreType.DMA((4, 3, 2)),
        ],
        compiler_params=pltpu.CompilerParams(
            vmem_limit_bytes=BIG + 3 * 1024 * 1024, collective_id=1, has_side_effects=True
        ),
    )(
        features.reshape(count, model), classes, table, cotangent.reshape(count, model),
        norm_gain[None], in_weight, scan_weight.T,
        step_weight, step_bias, decay_log, skip_gain, output_gain[None], output_weight,
    )
    shapes = [
        ((count, model), bf16),
        (in_weight.shape, f32),
        (scan_weight.shape[::-1], f32),
        (step_weight.shape, f32),
        (step_bias.shape, f32),
        (decay_log.shape, f32),
        (skip_gain.shape, f32),
        ((1, model), f32),
        ((1, inner), f32),
        (output_weight.shape, f32),
    ]
    feature_grad, *grads = pl.pallas_call(
        functools.partial(unpack_kernel, states, rank, grad_scale),
        out_shape=[jax.ShapeDtypeStruct(*s) for s in shapes],
        in_specs=[VMEM] * 7,
        out_specs=[VMEM] * 10,
    )(
        feature, *[x.reshape(lot, LANES) for x, lot in zip(full, lots)], in_weight, norm_gain[None]
    )
    feature_grad = feature_grad.reshape(tile_rows, tile_cols, model)
    grads[1] = grads[1].T
    grads[6], grads[7] = grads[6][0], grads[7][0]
    return (feature_grad, *grads)


def local(*args):
    tile_rows, tile_cols, model = args[1].shape
    rows, cols = lax.axis_size("row"), lax.axis_size("col")
    rank, states, inner = args[7].shape[1], args[9].shape[1], args[12].shape[0]
    fits = (
        tile_rows == 4 * cols and tile_cols == 2 * rows and model == LANES and inner == 2 * LANES
        and states == 2 * SUB and rank == SUB and args[3].shape[0] <= LANES
    )
    return (fast if fits else general)(*args)


def solution(mesh):
    in_specs = (P("row", "col"), P("row", "col", None), P("row", "col", None)) + (P(),) * 10
    out_specs = (P("row", "col", None),) + (P(),) * 9
    return jax.shard_map(local, mesh=mesh, in_specs=in_specs, out_specs=out_specs, check_vma=False)
```

```python
import functools
import math

import jax
import jax.numpy as jnp
from jax import lax
from jax.experimental import pallas as pl
from jax.experimental.pallas import tpu as pltpu
from jax.sharding import PartitionSpec as P

EPS = 1e-05
HIGHEST = lax.Precision.HIGHEST
MESH = pl.DeviceIdType.MESH
LANES = 128
SUB = 8
LOG2E = math.log2(math.e)
VMEM = pl.BlockSpec(memory_space=pltpu.VMEM)
BIG = 60 * 1024 * 1024


def layer_norm(rows, gain):
    average = jnp.mean(rows, axis=-1, keepdims=True)
    centred = rows - average
    spread = jnp.mean(centred * centred, axis=-1, keepdims=True)
    return centred * lax.rsqrt(spread + EPS) * gain


def silu_slope(before):
    sigma = jax.nn.sigmoid(before)
    return sigma * (1.0 + before * (1.0 - sigma))


def embed(features, classes, table):
    labels = jnp.arange(table.shape[0], dtype=jnp.int32)
    onehot = (classes[..., None] == labels).astype(jnp.float32)
    lookup = jnp.einsum("hwk,kd->hwd", onehot, table, precision=HIGHEST)
    return features.astype(jnp.float32) + lookup


def gate_output(total, gate_in, output_gain):
    return layer_norm(total, output_gain) * jax.nn.silu(gate_in)


def greet(axes):
    barrier = pltpu.get_barrier_semaphore()
    partners = 0
    for axis in axes:
        count = lax.axis_size(axis)
        me = lax.axis_index(axis)
        for d in range(1, count):
            pl.semaphore_signal(
                barrier, inc=1, device_id={axis: lax.rem(me + d, count)}, device_id_type=MESH
            )
            partners += 1
    pl.semaphore_wait(barrier, partners)


def half(ref, k, h, t):
    return ref[k, h, pl.ds(t, 1), :]


def walk(lines, tile, blocks, group, start, step):
    def outer(b, carry):
        def inner(j, carry):
            time = b * tile + j
            rising = b * (tile * lines) + j
            falling = (blocks - 1 - b) * (tile * lines) + (tile - 1 - j)
            tokens = [[base + line * tile for line in group] for base in (rising, falling)]
            return step(carry, tokens, time)

        return lax.fori_loop(0, tile, inner, carry, unroll=2)

    return lax.fori_loop(0, blocks, outer, start)


def groups_of(lines):
    size = 2 if lines % 2 == 0 else 1
    return [tuple(range(g, g + size)) for g in range(0, lines, size)]


def fold(ref, k, h, count):
    total = ref[k, h, pl.ds(0, count, stride=SUB), :]
    for s in range(1, SUB):
        total = total + ref[k, h, pl.ds(s, count, stride=SUB), :]
    return total


def softplus(x):
    return jnp.maximum(x, 0.0) + jnp.log1p(jnp.exp(-jnp.abs(x)))


def cross(a, b):
    return lax.dot_general(a, b, (((0,), (0,)), ((), ())), preferred_element_type=jnp.float32)


def back(a, b):
    return lax.dot_general(a, b, (((1,), (1,)), ((), ())), preferred_element_type=jnp.float32)


def general_kernel(
    tile_rows, tile_cols, states, rank, grad_scale, tiles,
    embedded_ref, upstream_ref, norm_gain_ref, in_weight_ref, scan_weight_ref, step_weight_ref,
    step_bias_ref, rate_ref, skip_ref, output_gain_ref, output_weight_ref,
    feature_ref, in_grad_ref, scan_grad_ref, stepw_ref, stepb_ref, dr_ref, skip_grad_ref,
    norm_grad_ref, gain_grad_ref, out_grad_ref,
    mixed, gate_grad, turn, along, down, wide, sv, steps, slope, low, hist, eight, pace8, up, dproj, dr_acc,
    mine0, from0, side0, all0, mine1, from1, side1, all1, sems, sumsems,
):
    count, inner = tile_rows * tile_cols, output_weight_ref.shape[0]
    rows, cols = lax.axis_size("row"), lax.axis_size("col")
    eh, nh = inner // LANES, states // SUB
    group = rank + 2 * states
    shapes = ((tile_rows // cols, tile_cols), (tile_cols // rows, tile_rows))
    boxes = (along, down)
    axes = ("col", "row")
    greet(("row", "col"))

    def post(turn_number, pair):
        axis, box = axes[pair], boxes[pair]
        size = lax.axis_size(axis)
        me = lax.axis_index(axis)
        copies = []
        for d in range(1, size):
            target = lax.rem(me + d, size)
            copy = pltpu.make_async_remote_copy(
                src_ref=box.at[2 * turn_number, target],
                dst_ref=box.at[2 * turn_number + 1, me],
                send_sem=sems.at[turn_number, pair, 0, d],
                recv_sem=sems.at[turn_number, pair, 1, d],
                device_id={axis: target},
                device_id_type=MESH,
            )
            copy.start()
            copies.append(copy)
        box[2 * turn_number + 1, me] = box[2 * turn_number, me]
        return copies

    def finish(copies):
        for copy in copies:
            copy.wait()

    def put_home(turn_number, x):
        along[2 * turn_number] = x.reshape(along.shape[1:])
        first = post(turn_number, 0)
        for h in range(eh):
            turn[h] = x[:, h * LANES : (h + 1) * LANES]
        per = tile_cols // rows
        for c in range(tile_cols):
            for h in range(eh):
                down[
                    2 * turn_number, c // per,
                    (c % per) * tile_rows : (c % per + 1) * tile_rows,
                    h * LANES : (h + 1) * LANES,
                ] = turn[h, pl.ds(c, tile_rows, stride=tile_cols), :]
        return first, post(turn_number, 1)

    def take_home(turn_number):
        per = tile_cols // rows
        for c in range(tile_cols):
            for h in range(eh):
                turn[h, pl.ds(c, tile_rows, stride=tile_cols), :] = down[
                    2 * turn_number + 1, c // per,
                    (c % per) * tile_rows : (c % per + 1) * tile_rows,
                    h * LANES : (h + 1) * LANES,
                ]
        here = along[2 * turn_number + 1].reshape(count, inner)
        return here + jnp.concatenate([turn[h] for h in range(eh)], axis=1)

    def lines_in(turn_number, pair):
        return boxes[pair][2 * turn_number + 1].reshape(count, inner)

    def lines_out(turn_number, pair, x):
        boxes[pair][2 * turn_number] = x.reshape(boxes[pair].shape[1:])
        return post(turn_number, pair)

    def rate_of(d, m, h):
        return rate_ref[d, m * SUB : (m + 1) * SUB, h * LANES : (h + 1) * LANES]

    def part(h):
        return slice(h * LANES, (h + 1) * LANES)

    zero = jnp.zeros((SUB, LANES), jnp.float32)

    sums = ((mine0, from0, side0, all0), (mine1, from1, side1, all1))
    fill = [0, 0]

    def put(lot, x):
        mine = sums[lot][0]
        per = mine.shape[1] // SUB
        for i in range(x.shape[0] // SUB):
            tile = fill[lot]
            at = (tile % per) * SUB
            mine[tile // per, at : at + SUB, :] = x[i * SUB : (i + 1) * SUB]
            fill[lot] += 1

    def put_wide(lot, x):
        for h in range(x.shape[1] // LANES):
            put(lot, x[:, h * LANES : (h + 1) * LANES])

    taken = [0, 0]

    def take(lot, height):
        full = sums[lot][3]
        per = full.shape[1] // SUB
        out = []
        for i in range(height // SUB):
            tile = taken[lot]
            at = (tile % per) * SUB
            out.append(full[tile // per, at : at + SUB, :])
            taken[lot] += 1
        return jnp.concatenate(out, axis=0) * grad_scale

    def take_wide(lot, height, width):
        return jnp.concatenate([take(lot, height) for h in range(width // LANES)], axis=1)

    def pad_rows(*rows_in):
        missing = -len(rows_in) % SUB
        return jnp.concatenate(list(rows_in) + [jnp.zeros((missing, LANES), jnp.float32)], axis=0)

    def pad_lot(lot):
        while fill[lot] < tiles[lot]:
            put(lot, zero)

    def spread(lot, phase, axis, source, result):
        size = lax.axis_size(axis)
        me = lax.axis_index(axis)
        copies = []
        for d in range(1, size):
            target = lax.rem(me + d, size)
            copy = pltpu.make_async_remote_copy(
                src_ref=source(target),
                dst_ref=result(me, d),
                send_sem=sumsems.at[lot, phase, 0, d],
                recv_sem=sumsems.at[lot, phase, 1, d],
                device_id={axis: target},
                device_id_type=MESH,
            )
            copy.start()
            copies.append(copy)
        return copies

    def sum_scatter(lot):
        mine, other, side, full = sums[lot]
        pad_lot(lot)
        return spread(lot, 0, "row", lambda t: mine.at[t], lambda me, d: other.at[d - 1])

    def sum_across(lot, copies):
        mine, other, side, full = sums[lot]
        finish(copies)
        acc = mine[lax.axis_index("row")]
        for d in range(rows - 1):
            acc = acc + other[d]
        me = lax.axis_index("col")
        side[me] = acc
        return spread(lot, 1, "col", lambda t: side.at[me], lambda m, d: side.at[m])

    def sum_gather(lot, copies):
        mine, other, side, full = sums[lot]
        finish(copies)
        acc = side[0]
        for d in range(1, cols):
            acc = acc + side[d]
        me = lax.axis_index("row")
        full[me] = acc
        return spread(lot, 2, "row", lambda t: full.at[me], lambda m, d: full.at[m])

    embedded = embedded_ref[...]
    normed = layer_norm(embedded, norm_gain_ref[...]).astype(jnp.bfloat16)
    mixed[...] = jnp.dot(normed, in_weight_ref[...], preferred_element_type=jnp.float32)
    values = jax.nn.silu(mixed[:, :inner]).astype(jnp.bfloat16).astype(jnp.float32)
    arriving = put_home(0, values)

    leaving = []
    for pair in range(2):
        lines, tile = shapes[pair]
        length = count // lines
        blocks = length // tile
        finish(arriving[pair])
        value = lines_in(0, pair)
        wide_p, sv_p, steps_p, hist_p = wide.at[pair], sv.at[pair], steps.at[pair], hist.at[pair]
        weight = scan_weight_ref[:, 2 * pair * group : 2 * (pair + 1) * group]
        projected = jnp.dot(
            value.astype(jnp.bfloat16), weight, preferred_element_type=jnp.float32
        )
        for k in range(2):
            d = 2 * pair + k
            lowrank = projected[:, k * group : k * group + rank]
            low[d] = lowrank
            before = (
                jnp.dot(
                    lowrank, step_weight_ref[d], precision=HIGHEST,
                    preferred_element_type=jnp.float32,
                )
                + step_bias_ref[d : d + 1, :]
            )
            slope[d] = jax.nn.sigmoid(before)
            pace = softplus(before)
            for h in range(eh):
                steps_p[k, h] = pace[:, part(h)]
                sv_p[k, h] = pace[:, part(h)] * value[:, part(h)]
            for which in range(2):
                for n in range(states):
                    col = k * group + rank + which * states + n
                    wide_p[k, which, pl.ds(n, count, stride=states), :] = jnp.broadcast_to(
                        projected[:, col : col + 1], (count, LANES)
                    )
            for h in range(eh):
                for line in range(lines):
                    at = line * (length + 1) * states
                    hist_p[k, h, at : at + states, :] = jnp.zeros((states, LANES), jnp.float32)
        for lot in groups_of(lines):

            def advance(carry, tokens, time):
                new = []
                i = 0
                for k in range(2):
                    for line, t in zip(lot, tokens[k]):
                        drive = [half(sv_p, k, h, t) for h in range(eh)]
                        pace = [half(steps_p, k, h, t) for h in range(eh)]
                        sums = [None] * eh
                        for m in range(nh):
                            at = pl.ds(pl.multiple_of(t * states + m * SUB, SUB), SUB)
                            slot = (line * (length + 1) + time + 1) * states + m * SUB
                            source = wide_p[k, 0, at, :]
                            probe = wide_p[k, 1, at, :]
                            for h in range(eh):
                                a = jnp.exp2(pace[h] * rate_of(2 * pair + k, m, h))
                                state = a * carry[i] + source * drive[h]
                                i += 1
                                hist_p[k, h, pl.ds(pl.multiple_of(slot, SUB), SUB), :] = state
                                new.append(state)
                                term = probe * state
                                sums[h] = term if sums[h] is None else sums[h] + term
                        for h in range(eh):
                            eight[k, h, pl.ds(pl.multiple_of(t * SUB, SUB), SUB), :] = sums[h]
                return tuple(new)

            walk(lines, tile, blocks, lot, (zero,) * (2 * len(lot) * eh * nh), advance)
        skip = skip_ref[2 * pair : 2 * pair + 1, :] + skip_ref[2 * pair + 1 : 2 * pair + 2, :]
        y = skip * value + jnp.concatenate(
            [fold(eight, 0, h, count) + fold(eight, 1, h, count) for h in range(eh)], axis=1
        )
        leaving.append(lines_out(1, pair, y))
    finish(leaving[0])
    finish(leaving[1])
    total = take_home(1)

    upstream = upstream_ref[...]
    gated, gate_pull = jax.vjp(gate_output, total, mixed[:, inner:], output_gain_ref[...])
    d_gated = back(upstream, output_weight_ref[...])
    d_total, d_gate_in, gain_grad = gate_pull(d_gated)
    arriving = put_home(2, d_total)
    gate_grad[...] = d_gate_in
    put(0, pad_rows(*[gain_grad[:, part(h)] for h in range(eh)]))
    put_wide(0, cross(gated.astype(jnp.bfloat16), upstream))

    leaving = []
    for pair in range(2):
        lines, tile = shapes[pair]
        length = count // lines
        blocks = length // tile
        finish(arriving[pair])
        g_all = lines_in(2, pair)
        wide_p, sv_p, steps_p, hist_p = wide.at[pair], sv.at[pair], steps.at[pair], hist.at[pair]
        for h in range(eh):
            up[0, h] = g_all[:, part(h)]
        for lot in groups_of(lines):

            def retreat(carry, tokens, time):
                grads, rates = carry
                rates = list(rates)
                new = []
                i = 0
                for k in range(2):
                    for line, t in zip(lot, tokens[1 - k]):
                        drive = [half(sv_p, k, h, t) for h in range(eh)]
                        pace = [half(steps_p, k, h, t) for h in range(eh)]
                        g = [half(up, 0, h, t) for h in range(eh)]
                        dd = [None] * eh
                        dp = [None] * eh
                        for m in range(nh):
                            at = pl.ds(pl.multiple_of(t * states + m * SUB, SUB), SUB)
                            slot = (line * (length + 1) + length - 1 - time) * states + m * SUB
                            earlier = pl.ds(pl.multiple_of(slot, SUB), SUB)
                            current = pl.ds(pl.multiple_of(slot + states, SUB), SUB)
                            source = wide_p[k, 0, at, :]
                            probe = wide_p[k, 1, at, :]
                            flow = None
                            read = None
                            for h in range(eh):
                                rate = rate_of(2 * pair + k, m, h)
                                grad = grads[i] + probe * g[h]
                                i += 1
                                term = grad * drive[h]
                                flow = term if flow is None else flow + term
                                term = g[h] * hist_p[k, h, current, :]
                                read = term if read is None else read + term
                                term = grad * source
                                dd[h] = term if dd[h] is None else dd[h] + term
                                carried = jnp.exp2(pace[h] * rate) * grad
                                q = carried * hist_p[k, h, earlier, :]
                                term = q * rate
                                dp[h] = term if dp[h] is None else dp[h] + term
                                j = (k * nh + m) * eh + h
                                rates[j] = rates[j] + q * pace[h]
                                new.append(carried)
                            wide_p[k, 0, at, :] = flow
                            wide_p[k, 1, at, :] = read
                        for h in range(eh):
                            at8 = pl.ds(pl.multiple_of(t * SUB, SUB), SUB)
                            eight[k, h, at8, :] = dd[h]
                            pace8[k, h, at8, :] = dp[h]
                return (tuple(new), tuple(rates))

            chains = 2 * len(lot) * eh * nh
            unused, rates = walk(
                lines, tile, blocks, lot, ((zero,) * chains, (zero,) * (2 * eh * nh)), retreat
            )
            for k in range(2):
                for m in range(nh):
                    for h in range(eh):
                        place = (2 * pair + k, slice(m * SUB, (m + 1) * SUB), part(h))
                        add = rates[(k * nh + m) * eh + h] * rate_ref[place] * (1.0 / LOG2E)
                        if lot[0] == 0:
                            dr_acc[place] = add
                        else:
                            dr_acc[place] += add
        value = lines_in(0, pair)
        g_all = lines_in(2, pair)
        skip = skip_ref[2 * pair : 2 * pair + 1, :] + skip_ref[2 * pair + 1 : 2 * pair + 2, :]
        dv = skip * g_all
        direct = jnp.sum(g_all * value, axis=0, keepdims=True)
        small = [direct[:, part(h)] for h in range(eh)]
        for k in range(2):
            d = 2 * pair + k
            drive = jnp.concatenate([fold(eight, k, h, count) for h in range(eh)], axis=1)
            pace = jnp.concatenate([fold(pace8, k, h, count) for h in range(eh)], axis=1)
            dv = dv + drive * jnp.concatenate([steps_p[k, h] for h in range(eh)], axis=1)
            d_before = (drive * value + pace * (1.0 / LOG2E)) * slope[d]
            bias_sum = jnp.sum(d_before, axis=0, keepdims=True)
            small += [bias_sum[:, part(h)] for h in range(eh)]
            put_wide(
                pair,
                lax.dot_general(
                    low[d], d_before, (((0,), (0,)), ((), ())), precision=HIGHEST,
                    preferred_element_type=jnp.float32,
                ),
            )
            put_wide(pair, dr_acc[d])
            dproj[:, k * group : k * group + rank] = lax.dot_general(
                d_before, step_weight_ref[d], (((1,), (1,)), ((), ())), precision=HIGHEST,
                preferred_element_type=jnp.float32,
            )
            lane = lax.broadcasted_iota(jnp.int32, (LANES, 2 * states), 1)
            flow = None
            for j in range(2 * states):
                x = wide_p[k, j // states, pl.ds(j % states, count, stride=states), :]
                pick = (lane == j).astype(jnp.bfloat16)
                term = jnp.dot(x.astype(jnp.bfloat16), pick, preferred_element_type=jnp.float32)
                flow = term if flow is None else flow + term
            dproj[:, k * group + rank : (k + 1) * group] = flow
        d_projected = dproj[...].astype(jnp.bfloat16)
        span = slice(2 * pair * group, 2 * (pair + 1) * group)
        leaving.append(lines_out(3, pair, back(d_projected, scan_weight_ref[:, span]) + dv))
        put(pair, pad_rows(*small))
        put_wide(pair, cross(d_projected, value.astype(jnp.bfloat16)))
        if pair == 0:
            early = sum_scatter(0)
        else:
            early = sum_across(0, early)
    finish(leaving[0])
    finish(leaving[1])
    d_values = take_home(3)
    early = sum_gather(0, early)

    d_mixed = jnp.concatenate(
        [d_values * silu_slope(mixed[:, :inner]), gate_grad[...]], axis=1
    ).astype(jnp.bfloat16)
    normed, norm_pull = jax.vjp(layer_norm, embedded_ref[...], norm_gain_ref[...])
    put_wide(1, cross(normed.astype(jnp.bfloat16), d_mixed))
    d_embedded, norm_grad = norm_pull(back(d_mixed, in_weight_ref[...]))
    put(1, pad_rows(norm_grad))
    late = sum_scatter(1)
    feature_ref[...] = (upstream_ref[...].astype(jnp.float32) + d_embedded).astype(jnp.bfloat16)
    late = sum_across(1, late)
    finish(early)
    late = sum_gather(1, late)

    def take_pair(pair):
        for d in (2 * pair, 2 * pair + 1):
            stepw_ref[d] = take_wide(pair, rank, inner)
            dr_ref[d] = take_wide(pair, states, inner)
        small = take(pair, -(-3 * eh // SUB) * SUB)
        for h in range(eh):
            for k in range(2):
                d = 2 * pair + k
                skip_grad_ref[d : d + 1, part(h)] = small[h : h + 1]
                stepb_ref[d : d + 1, part(h)] = small[(k + 1) * eh + h : (k + 1) * eh + h + 1]
        span = slice(2 * pair * group, 2 * (pair + 1) * group)
        scan_grad_ref[:, span] = take_wide(pair, 2 * group, inner).T

    small = take(0, SUB)
    for h in range(eh):
        gain_grad_ref[:, part(h)] = small[h : h + 1]
    out_grad_ref[...] = take_wide(0, inner, out_grad_ref.shape[1])
    take_pair(0)
    finish(late)
    take_pair(1)
    in_grad_ref[...] = take_wide(1, in_grad_ref.shape[0], in_grad_ref.shape[1])
    norm_grad_ref[...] = take(1, SUB)[0:1]


def general(
    classes, features, cotangent, table, norm_gain, in_weight, scan_weight, step_weight,
    step_bias, decay_log, skip_gain, output_gain, output_weight,
):
    tile_rows, tile_cols, model_width = features.shape
    inner = output_weight.shape[0]
    count = tile_rows * tile_cols
    rows, cols = lax.axis_size("row"), lax.axis_size("col")
    rank = step_weight.shape[1]
    states = decay_log.shape[1]
    group = rank + 2 * states
    eh = inner // LANES
    lines = max(tile_rows // cols, tile_cols // rows)
    grad_scale = float(count * rows * cols) ** (-0.5)
    rate2 = -jnp.exp(decay_log) * LOG2E
    embedded = embed(features, classes, table).reshape(count, model_width)
    f32 = jnp.float32
    shapes = [
        ((count, model_width), jnp.bfloat16),
        (in_weight.shape, f32),
        (scan_weight.shape, f32),
        (step_weight.shape, f32),
        (step_bias.shape, f32),
        (decay_log.shape, f32),
        (skip_gain.shape, f32),
        ((1, model_width), f32),
        ((1, inner), f32),
        (output_weight.shape, f32),
    ]
    scratch = [
        ((count, 2 * inner), f32),
        ((count, inner), f32),
        ((eh, count, LANES), f32),
        ((8, cols, count // cols, inner), f32),
        ((8, rows, count // rows, inner), f32),
        ((2, 2, 2, count * states, LANES), f32),
        ((2, 2, eh, count, LANES), f32),
        ((2, 2, eh, count, LANES), f32),
        ((4, count, inner), f32),
        ((4, count, rank), f32),
        ((2, 2, eh, (count + lines) * states, LANES), f32),
        ((2, eh, count * SUB, LANES), f32),
        ((2, eh, count * SUB, LANES), f32),
        ((1, eh, count, LANES), f32),
        ((count, 2 * group), f32),
        (decay_log.shape, f32),
    ]
    pair_tiles = eh * (2 * rank + 2 * states + 2 * group) // SUB + -(-3 * eh // SUB)
    least = (
        1 + inner * model_width // (LANES * SUB) + pair_tiles,
        1 + in_weight.size // (LANES * SUB) + pair_tiles,
    )
    tiles = tuple(-(-t // rows) * rows for t in least)
    for lot in range(2):
        chunk = (tiles[lot] // rows * SUB, LANES)
        scratch += [((rows,) + chunk, f32), ((rows - 1,) + chunk, f32), ((cols,) + chunk, f32), ((rows,) + chunk, f32)]
    feature_grad, *grads = pl.pallas_call(
        functools.partial(general_kernel, tile_rows, tile_cols, states, rank, grad_scale, tiles),
        out_shape=[jax.ShapeDtypeStruct(*s) for s in shapes],
        in_specs=[VMEM] * 11,
        out_specs=[VMEM] * 10,
        scratch_shapes=[pltpu.VMEM(*s) for s in scratch]
        + [
            pltpu.SemaphoreType.DMA((4, 2, 2, max(rows, cols))),
            pltpu.SemaphoreType.DMA((2, 3, 2, max(rows, cols))),
        ],
        compiler_params=pltpu.CompilerParams(
            vmem_limit_bytes=BIG, collective_id=1, has_side_effects=True
        ),
    )(
        embedded, cotangent.reshape(count, model_width), norm_gain[None], in_weight, scan_weight,
        step_weight, step_bias, rate2, skip_gain, output_gain[None], output_weight,
    )
    feature_grad = feature_grad.reshape(tile_rows, tile_cols, model_width)
    grads[6], grads[7] = grads[6][0], grads[7][0]
    return (feature_grad, *grads)


def split2(x):
    high = x.astype(jnp.bfloat16)
    return high, (x - high.astype(jnp.float32)).astype(jnp.bfloat16)


def dot(a, b):
    return jnp.dot(a, b, preferred_element_type=jnp.float32)


def greet_all():
    barrier = pltpu.get_barrier_semaphore()
    rows, cols = lax.axis_size("row"), lax.axis_size("col")
    r, c = lax.axis_index("row"), lax.axis_index("col")
    for dr in range(rows):
        for dc in range(cols):
            if dr or dc:
                there = {"row": lax.rem(r + dr, rows), "col": lax.rem(c + dc, cols)}
                pl.semaphore_signal(barrier, inc=1, device_id=there, device_id_type=MESH)
    pl.semaphore_wait(barrier, rows * cols - 1)


def lots_of(rows, inner, model_width, states, rank, group, eh):
    pair = (rank + states + group) * 2 * eh + -(-3 * eh // SUB) * SUB
    gated = SUB + inner * model_width // LANES + model_width * eh
    per = SUB * rows
    return tuple(-(-n // per) * per for n in (gated, pair, pair, model_width * eh))


def fast_kernel(
    tile_rows, tile_cols, states, rank,
    features_ref, classes_ref, table_ref, upstream_ref, norm_gain_ref, in_weight_ref, sw_ref,
    step_weight_ref, step_bias_ref, decay_ref, skip_ref, output_gain_ref, output_weight_ref,
    feature_ref, full0, full1, full2, full3,
    home, emb_s0, emb_s1, emb_r0, emb_r1, cot_s0, cot_s1, cot_r0, cot_r1,
    back_s0, back_s1, back_r0, back_r1, y_s0, y_s1, y_r0, y_r1,
    spread0, spread1, wpk, swp, cmat, rate_s, normed_s, mixed_s, value_s, proj_s, tok, slope,
    wide, flows, hist, pace_t, drive_t, g_t, dd_t, dp_t, bufs, bufs_tok, probe_t, lhs, dval, dr_s, in_acc,
    mine0, from0, side0, mine1, from1, side1, mine2, from2, side2, mine3, from3, side3,
    sems, ysems, sumsems,
):
    f32, bf16 = jnp.float32, jnp.bfloat16
    count, inner = tile_rows * tile_cols, output_weight_ref.shape[0]
    model = features_ref.shape[1]
    rows, cols = lax.axis_size("row"), lax.axis_size("col")
    me_r, me_c = lax.axis_index("row"), lax.axis_index("col")
    eh = inner // LANES
    group = rank + 2 * states
    lines = (tile_rows // cols, tile_cols // rows)
    length = (count // lines[0], count // lines[1])
    copies_m = tuple(SUB // (2 * n) for n in lines)
    per_n = tuple(states // m for m in copies_m)
    tall = tuple(SUB * n for n in length)
    blocks = count // SUB
    axes = ("col", "row")
    sizes = (cols, rows)
    zero = jnp.zeros((SUB, LANES), f32)
    sub = lax.broadcasted_iota(jnp.int32, (SUB, LANES), 0)
    even = lax.rem(sub, 2) == 0
    pos = sub // 2
    pos_even = lax.rem(pos, 2) == 0
    pos_edge = (pos == 0) | (pos == 3)
    low_half = sub < 4

    def part(h):
        return slice(h * LANES, (h + 1) * LANES)

    def tile(b):
        return pl.ds(pl.multiple_of(b * SUB, SUB), SUB)

    def step_tile(p, b):
        return tile(b + (length[0] if p else 0))

    def tile2(b):
        return pl.ds(pl.multiple_of(b * 2 * SUB, 2 * SUB), 2 * SUB)

    greet_all()

    def pack(src, dst, p):
        if p == 0:
            for rho in range(tile_rows):
                c, i = rho // lines[0], rho % lines[0]
                for j in range(2):
                    dst[c, pl.ds(2 * i + j, tile_cols // 2, stride=SUB), :] = src[
                        pl.ds(rho * tile_cols + j, tile_cols // 2, stride=2), :
                    ]
        else:
            for r in range(rows):
                for j in range(2):
                    dst[r, pl.ds(j, tile_rows, stride=2), :] = src[
                        pl.ds(2 * r + j, tile_rows, stride=tile_cols), :
                    ]

    def unpack(src, dst, p):
        if p == 0:
            for rho in range(tile_rows):
                c, i = rho // lines[0], rho % lines[0]
                for j in range(2):
                    dst[pl.ds(rho * tile_cols + j, tile_cols // 2, stride=2), :] = src[
                        c, pl.ds(2 * i + j, tile_cols // 2, stride=SUB), :
                    ]
        else:
            for r in range(rows):
                for j in range(2):
                    dst[pl.ds(2 * r + j, tile_rows, stride=tile_cols), :] = src[
                        r, pl.ds(j, tile_rows, stride=2), :
                    ]

    def batch(src, dst, amount, send, recv):
        return pltpu.make_async_remote_copy(
            src_ref=src.at[pl.ds(0, amount)], dst_ref=dst.at[pl.ds(0, amount)], send_sem=send,
            recv_sem=recv, device_id={"row": me_r, "col": me_c}, device_id_type=MESH,
        )

    def exchange(turn, p, src, dst):
        size, axis = sizes[p], axes[p]
        me = lax.axis_index(axis)
        for d in range(1, size):
            target = lax.rem(me + d, size)
            copy = pltpu.make_async_remote_copy(
                src_ref=src.at[target],
                dst_ref=dst.at[me],
                send_sem=sems.at[turn, p, 0],
                recv_sem=sems.at[turn, p, 1],
                device_id={axis: target},
                device_id_type=MESH,
            )
            copy.start()
        dst[me] = src[me]
        return [batch(src, dst, size - 1, sems.at[turn, p, 0], sems.at[turn, p, 1])]

    def swap(p, src, dst):
        for dr in range(rows):
            for dc in range(cols):
                r, c = lax.rem(me_r + dr, rows), lax.rem(me_c + dc, cols)
                if p == 0:
                    there, here = c * rows + r, me_r * cols + me_c
                else:
                    there, here = r * cols + c, me_c * rows + me_r
                if dr == 0 and dc == 0:
                    dst[here] = src[there]
                    continue
                copy = pltpu.make_async_remote_copy(
                    src_ref=src.at[there],
                    dst_ref=dst.at[here],
                    send_sem=ysems.at[p, 0],
                    recv_sem=ysems.at[p, 1],
                    device_id={"row": r, "col": c},
                    device_id_type=MESH,
                )
                copy.start()
        return [batch(src, dst, rows * cols - 1, ysems.at[p, 0], ysems.at[p, 1])]

    def arrived(copies):
        for copy in copies:
            copy.wait_recv()

    def sent(copies):
        for copy in copies:
            copy.wait_send()

    emb_s, emb_r = (emb_s0, emb_s1), (emb_r0, emb_r1)
    cot_s, cot_r = (cot_s0, cot_s1), (cot_r0, cot_r1)
    back_s, back_r = (back_s0, back_s1), (back_r0, back_r1)
    y_s, y_r = (y_s0, y_s1), (y_r0, y_r1)
    spreads = (spread0, spread1)
    pending = []
    half_n, few_n = SUB, SUB // 2
    y_t = dd_t

    def group_tile(p, g, t):
        return tile(g * length[p] + t)

    def added(ref, p, h, b, groups):
        total = ref[h, group_tile(p, 0, b), :]
        for g in range(1, groups):
            total = total + ref[h, group_tile(p, g, b), :]
        return total

    token = lax.broadcasted_iota(jnp.int32, (count, tile_rows), 0)
    lane = lax.broadcasted_iota(jnp.int32, (count, tile_rows), 1)
    of_row = jnp.where(token // tile_cols == lane, 1.0, 0.0).astype(bf16)
    labels = dot(of_row, classes_ref[...].astype(f32).astype(bf16))
    token = lax.broadcasted_iota(jnp.int32, (count, tile_cols), 0)
    lane = lax.broadcasted_iota(jnp.int32, (count, tile_cols), 1)
    labels = jnp.where(lax.rem(token, tile_cols) == lane, labels, 0.0).astype(bf16)
    labels = dot(labels, jnp.ones((tile_cols, LANES), bf16))
    lane = lax.broadcasted_iota(jnp.int32, (count, LANES), 1).astype(f32)
    onehot = jnp.where(labels == lane, 1.0, 0.0).astype(bf16)
    entries = table_ref[...]
    lookup = None
    for i in range(3):
        rounded = entries.astype(bf16).astype(f32)
        rest = jnp.zeros((LANES - entries.shape[0], model), f32)
        term = dot(onehot, jnp.concatenate([rounded, rest], axis=0).astype(bf16))
        lookup = term if lookup is None else lookup + term
        entries = entries - rounded
    home[...] = features_ref[...].astype(f32) + lookup
    pack(home, emb_s1, 1)
    emb1 = exchange(0, 1, emb_s1, emb_r1)
    pack(home, emb_s0, 0)
    emb0 = exchange(0, 0, emb_s0, emb_r0)
    home[...] = upstream_ref[...].astype(f32)
    pack(home, cot_s0, 0)
    cot0 = exchange(1, 0, cot_s0, cot_r0)
    pack(home, cot_s1, 1)
    cot1 = exchange(1, 1, cot_s1, cot_r1)
    pending += emb1 + emb0 + cot0 + cot1

    key_row = lax.broadcasted_iota(jnp.int32, (LANES, 2 * LANES), 0)
    lane_tile = lax.broadcasted_iota(jnp.int32, (LANES, 2 * LANES), 1) // LANES
    for p in range(2):
        which = lax.rem(key_row, 2 * states) // states
        key = which * per_n[p] + lax.rem(key_row, per_n[p])
        key = jnp.where(key_row < 4 * states, key - lane_tile, -8 * states)
        for q in range(per_n[p]):
            spreads[p][:, 2 * q * LANES : 2 * (q + 1) * LANES] = jnp.where(
                key == 2 * q, 1.0, 0.0
            ).astype(bf16)
    sw32 = sw_ref[...].astype(f32)
    for d in range(4):
        off = d * group
        low_w = sw32[off : off + rank]
        wpk[d] = jnp.concatenate(
            [sw32[off + rank : off + group], low_w,
             jnp.zeros((LANES - group, inner), f32)], axis=0
        ).astype(bf16)
        step_w = step_weight_ref[d]
        w1, w2 = split2(step_w)
        w3 = (step_w - w1.astype(f32) - w2.astype(f32)).astype(bf16)
        blank = jnp.zeros((rank, inner), f32)
        left = jnp.concatenate([low_w, low_w, low_w, blank], axis=0).astype(bf16)
        right = jnp.concatenate(
            [w1.astype(f32), w2.astype(f32), w3.astype(f32), blank], axis=0
        ).astype(bf16)
        c_high, c_low = split2(cross(left, right))
        cmat[d, 0] = c_high
        cmat[d, 1] = c_low
        for i, w in enumerate((w1, w2)):
            swp[d, i] = jnp.concatenate(
                [jnp.zeros((2 * states, inner), f32), w.astype(f32),
                 jnp.zeros((LANES - group, inner), f32)], axis=0
            ).astype(bf16)
        rate = -jnp.exp(decay_ref[d]) * LOG2E
        p, k = d // 2, d % 2
        for n in range(states):
            m, n1 = n // per_n[p], n % per_n[p]
            for h in range(eh):
                row = jnp.broadcast_to(rate[n : n + 1, part(h)], (SUB, LANES))
                if p == 0:
                    mask = lax.rem(sub, 2) == k
                else:
                    mask = pos == 2 * m + k
                at = slice(n1 * SUB, (n1 + 1) * SUB)
                if k == 0 and m == 0:
                    rate_s[p, h, at, :] = row
                else:
                    rate_s[p, h, at, :] = jnp.where(mask, row, rate_s[p, h, at, :])

    def to_scan(p, *moves):
        def one(b, carry):
            for move in moves:
                one_of(b, *move)
            return carry

        def one_of(b, first, second, store):
            mirror = blocks - 1 - b
            x0, x1 = first(tile(b)), second(tile(mirror))
            if p == 0:
                z = jnp.where(even, x1, x0)
                store(2 * b, jnp.where(even, x0, x1))
                store(
                    2 * b + 1,
                    jnp.where(even, pltpu.roll(z, SUB - 1, 0), pltpu.roll(z, 1, 0)),
                )
            else:
                u = jnp.where(pos_even, x0, x1)
                v = pltpu.roll(u, 4, 0)
                u2 = pltpu.roll(jnp.where(pos_even, x1, x0), 2, 0)
                v2 = pltpu.roll(u2, 4, 0)
                store(4 * b, jnp.where(pos_edge, u, v))
                store(4 * b + 1, jnp.where(low_half, v2, u2))
                store(4 * b + 2, jnp.where(pos_edge, v, u))
                store(4 * b + 3, jnp.where(low_half, u2, v2))

        lax.fori_loop(0, blocks, one, 0, unroll=max(2, 4 // len(moves)))

    def from_scan(p, *moves):
        def one(b, carry):
            for move in moves:
                one_of(b, *move)
            return carry

        def one_of(b, load, store):
            mirror = blocks - 1 - b
            if p == 0:
                s0, s1 = load(2 * b), load(2 * b + 1)
                store(0, tile(b), jnp.where(even, s0, pltpu.roll(s1, 1, 0)))
                store(1, tile(mirror), jnp.where(even, pltpu.roll(s1, SUB - 1, 0), s0))
            else:
                a = []
                for i in range(4):
                    s = load(4 * b + i)
                    s = s + pltpu.roll(s, 4, 0)
                    a.append(pltpu.roll(s, 2, 0) if i % 2 else s)
                store(
                    0, tile(b),
                    jnp.where(low_half, jnp.where(pos == 0, a[0], a[1]), jnp.where(pos == 2, a[2], a[3])),
                )
                store(
                    1, tile(mirror),
                    jnp.where(low_half, jnp.where(pos == 0, a[3], a[2]), jnp.where(pos == 2, a[1], a[0])),
                )

        lax.fori_loop(0, blocks, one, 0, unroll=max(2, 4 // len(moves)))

    def put_step(ref, p, b, x):
        ref[step_tile(p, b), :] = x

    def put_at(ref, b, x):
        ref[tile(b), :] = x

    def put_probe(b, x):
        probe_t[tile(b), :] = x

    def prologue(p):
        embedded = emb_r[p][...].reshape(count, model)
        normed = layer_norm(embedded, norm_gain_ref[...]).astype(bf16)
        normed_s[p] = normed
        mixed_s[p] = dot(normed, in_weight_ref[...])
        value = jax.nn.silu(mixed_s[p, :, :inner]).astype(bf16)
        value_s[p] = value
        value32 = value.astype(f32)
        for k in range(2):
            d = 2 * p + k
            proj_s[p, k] = back(value, wpk[d])
            before = dot(value, cmat[d, 0]) + dot(value, cmat[d, 1]) + step_bias_ref[d : d + 1, :]
            slope[p, k] = jax.nn.sigmoid(before)
            pace = softplus(before)
            for h in range(eh):
                tok[p, k, h] = pace[:, part(h)]
        moves = [(lambda at: proj_s[p, 0, at, :], lambda at: proj_s[p, 1, at, :], put_probe)]
        for h in range(eh):
            bufs_tok[0, 0, h] = value32[:, part(h)]
            moves.append(
                (lambda at, h=h: tok[p, 0, h, at, :], lambda at, h=h: tok[p, 1, h, at, :],
                 functools.partial(put_step, pace_t.at[h], p))
            )
            moves.append(
                (lambda at, h=h: tok[p, 0, h, at, :] * bufs_tok[0, 0, h, at, :],
                 lambda at, h=h: tok[p, 1, h, at, :] * bufs_tok[0, 0, h, at, :],
                 functools.partial(put_step, drive_t.at[h], p))
            )
        to_scan(p, *moves)
        size_of = tall[p]
        x = jnp.where(keep_lanes(p, size_of), probe_t[:size_of, :], 0.0)
        high = x.astype(bf16).astype(f32)
        lhs[:size_of, :] = (high + pltpu.roll(x - high, 2 * states, 1)).astype(bf16)
        if copies_m[p] > 1:
            row = lax.broadcasted_iota(jnp.int32, (size_of, LANES), 0)
            x = jnp.where(lax.rem(row, SUB) < 4, x, pltpu.roll(x, LANES - per_n[p], 1))
        probe_t[:size_of, :] = x
        chunk = count
        for q in range(per_n[p]):
            w, n1 = 2 * q // per_n[p], 2 * q % per_n[p]
            for s in range(size_of // chunk):
                if q % 3 == 2:
                    for j in range(2):
                        at = (n1 + j) * size_of + s * chunk
                        col = w * states + n1 + j
                        wide[p, w, at : at + chunk, :] = jnp.broadcast_to(
                            probe_t[s * chunk : (s + 1) * chunk, col : col + 1], (chunk, LANES)
                        )
                    continue
                out = dot(
                    lhs[s * chunk : (s + 1) * chunk, :],
                    spreads[p][:, 2 * q * LANES : 2 * (q + 1) * LANES],
                )
                for j in range(2):
                    at = (n1 + j) * size_of + s * chunk
                    wide[p, w, at : at + chunk, :] = out[:, part(j)]

    def keep_lanes(p, height):
        lane = lax.broadcasted_iota(jnp.int32, (height, LANES), 1)
        keep = lane < 2 * states
        if copies_m[p] > 1:
            row = lax.broadcasted_iota(jnp.int32, (height, LANES), 0)
            m = lax.rem(row, SUB) // (SUB // copies_m[p])
            keep = keep & (lax.rem(lane, states) // per_n[p] == m)
        return keep

    def forward(p):
        high, stride = tall[p], tall[p] + SUB
        for h in range(eh):
            for n in range(per_n[p]):
                hist[p, h, n * stride : n * stride + SUB, :] = zero
        for g in range(per_n[p] // half_n):
            ns = range(g * half_n, (g + 1) * half_n)

            def step(t, carry, g=g, ns=ns):
                at = tile(t)
                pace = [pace_t[h, step_tile(p, t), :] for h in range(eh)]
                drive = [drive_t[h, step_tile(p, t), :] for h in range(eh)]
                y = [None] * eh
                new = []
                for i, n in enumerate(ns):
                    row = tile(n * (high // SUB) + t)
                    slot = tile(n * (stride // SUB) + t + 1)
                    source, probe = wide[p, 0, row, :], wide[p, 1, row, :]
                    for h in range(eh):
                        a = jnp.exp2(pace[h] * rate_s[p, h, n * SUB : (n + 1) * SUB, :])
                        state = a * carry[i * eh + h] + source * drive[h]
                        hist[p, h, slot, :] = state
                        new.append(state)
                        term = probe * state
                        y[h] = term if y[h] is None else y[h] + term
                for h in range(eh):
                    y_t[h, group_tile(p, g, t), :] = y[h]
                return tuple(new)

            lax.fori_loop(0, length[p], step, (zero,) * (half_n * eh), unroll=8)
        moves = []
        for h in range(eh):

            def put_y(k, at, x, h=h):
                bufs_tok[k, 0, h, at, :] = x

            moves.append((lambda b, h=h: added(y_t, p, h, b, per_n[p] // half_n), put_y))
        from_scan(p, *moves)
        for h in range(eh):
            y_s[p][:, :, part(h)] = (bufs_tok[0, 0, h] + bufs_tok[1, 0, h]).reshape(blocks, SUB, LANES)

    def gate(p):
        value = value_s[p].astype(f32)
        skips = jnp.sum(skip_ref[...], axis=0, keepdims=True)
        total = (
            y_s[p][...].reshape(count, inner) + y_r[p][...].reshape(count, inner) + skips * value
        )
        upstream = cot_r[p][...].reshape(count, model).astype(bf16)
        d_gated = back(upstream, output_weight_ref[...])
        gated, pull = jax.vjp(gate_output, total, mixed_s[p, :, inner:], output_gain_ref[...])
        d_total, d_gate_in, gain_grad = pull(d_gated)
        dval[p] = d_total
        if p == 0:
            put(0, pad_rows(*[gain_grad[:, part(h)] for h in range(eh)]))
            put_wide(0, cross(gated.astype(bf16), upstream))
            d_gate = d_gate_in.astype(bf16)
            gate16 = d_gate
            put_wide(0, cross(normed_s[p], d_gate))
        else:
            gate16 = None

        moves = []
        for h in range(eh):
            load = lambda at, h=h: dval[p, at, part(h)]
            moves.append((load, load, functools.partial(put_at, g_t.at[h])))
        to_scan(p, *moves)
        return gate16

    sums = (
        (mine0, from0, side0, full0), (mine1, from1, side1, full1),
        (mine2, from2, side2, full2), (mine3, from3, side3, full3),
    )
    fill = [0] * 4

    def put(lot, x):
        mine = sums[lot][0]
        per = mine.shape[1] // SUB
        for i in range(x.shape[0] // SUB):
            n = fill[lot]
            at = (n % per) * SUB
            mine[n // per, at : at + SUB, :] = x[i * SUB : (i + 1) * SUB]
            fill[lot] += 1

    def put_wide(lot, x):
        for h in range(x.shape[1] // LANES):
            put(lot, x[:, h * LANES : (h + 1) * LANES])

    def pad_rows(*rows_in):
        missing = -len(rows_in) % SUB
        return jnp.concatenate(list(rows_in) + [jnp.zeros((missing, LANES), f32)], axis=0)

    def pad_lot(lot):
        mine = sums[lot][0]
        while fill[lot] < rows * mine.shape[1] // SUB:
            put(lot, zero)

    def spread(lot, phase, axis, source, result, whole):
        size = lax.axis_size(axis)
        me = lax.axis_index(axis)
        for d in range(1, size):
            target = lax.rem(me + d, size)
            copy = pltpu.make_async_remote_copy(
                src_ref=source(target),
                dst_ref=result(me, d),
                send_sem=sumsems.at[lot, phase, 0],
                recv_sem=sumsems.at[lot, phase, 1],
                device_id={axis: target},
                device_id_type=MESH,
            )
            copy.start()
        out = [batch(whole, whole, size - 1, sumsems.at[lot, phase, 0], sumsems.at[lot, phase, 1])]
        pending.extend(out)
        return out

    def sum_scatter(lot):
        mine, other, side, full = sums[lot]
        pad_lot(lot)
        return spread(lot, 0, "row", lambda t: mine.at[t], lambda me, d: other.at[d - 1], other)

    def sum_across(lot, copies):
        mine, other, side, full = sums[lot]
        arrived(copies)
        acc = mine[me_r]
        for d in range(rows - 1):
            acc = acc + other[d]
        side[me_c] = acc
        return spread(lot, 1, "col", lambda t: side.at[me_c], lambda m, d: side.at[m], side)

    def sum_gather(lot, copies):
        mine, other, side, full = sums[lot]
        arrived(copies)
        acc = side[0]
        for d in range(1, cols):
            acc = acc + side[d]
        full[me_r] = acc
        return spread(lot, 2, "row", lambda t: full.at[me_r], lambda m, d: full.at[m], full)

    def backward(p, hook=None):
        high, stride = tall[p], tall[p] + SUB
        for g in range(per_n[p] // few_n):
            if hook is not None and g == 1:
                hook()
            ns = range(g * few_n, (g + 1) * few_n)

            def step(i, carry, g=g, ns=ns):
                grads, rates, t = carry
                at = tile(t)
                pace = [pace_t[h, step_tile(p, t), :] for h in range(eh)]
                drive = [drive_t[h, step_tile(p, t), :] for h in range(eh)]
                gs = [g_t[h, at, :] for h in range(eh)]
                dd, dp = [None] * eh, [None] * eh
                new, new_rates = [], []
                for i, n in enumerate(ns):
                    row = tile(n * (high // SUB) + t)
                    earlier = tile(n * (stride // SUB) + t)
                    current = tile(n * (stride // SUB) + t + 1)
                    source, probe = wide[p, 0, row, :], wide[p, 1, row, :]
                    flow = read = None
                    for h in range(eh):
                        j = i * eh + h
                        rate = rate_s[p, h, n * SUB : (n + 1) * SUB, :]
                        grad = grads[j] + probe * gs[h]
                        term = grad * drive[h]
                        flow = term if flow is None else flow + term
                        term = gs[h] * hist[p, h, current, :]
                        read = term if read is None else read + term
                        term = grad * source
                        dd[h] = term if dd[h] is None else dd[h] + term
                        carried = jnp.exp2(pace[h] * rate) * grad
                        q = carried * hist[p, h, earlier, :]
                        term = q * rate
                        dp[h] = term if dp[h] is None else dp[h] + term
                        new_rates.append(rates[j] + q * pace[h])
                        new.append(carried)
                    if n % 2 == 0:
                        kept = (flow, read)
                        continue
                    place = tile2((n // 2) * (high // SUB) + t)
                    for w, x in enumerate((flow, read)):
                        both = jnp.concatenate([kept[w], x], axis=0)
                        flows[w, place, :] = both.astype(bf16)
                for h in range(eh):
                    dd_t[h, group_tile(p, g, t), :] = dd[h]
                    dp_t[h, group_tile(p, g, t), :] = dp[h]
                return tuple(new), tuple(new_rates), t - 1

            chains = (zero,) * (few_n * eh)
            unused, rates, end = lax.fori_loop(
                0, length[p], step, (chains, chains, jnp.int32(length[p] - 1)), unroll=4
            )
            for i, n in enumerate(ns):
                for h in range(eh):
                    place = slice(n * SUB, (n + 1) * SUB)
                    dr_s[h, place, :] = rates[i * eh + h] * rate_s[p, h, place, :] * (1.0 / LOG2E)

    def finish_pair(p, gate16):
        lot = p + 1
        high = tall[p]
        chunk = count
        wide_high = 2 * chunk
        lane = lax.broadcasted_iota(jnp.int32, (wide_high, LANES), 1)
        row = lax.broadcasted_iota(jnp.int32, (wide_high, LANES), 0)
        mine = lax.rem(lane, 2) == lax.rem(row // SUB, 2)
        keep = keep_lanes(p, wide_high) & mine

        def ones_of(w, a):
            at = (w * per_n[p] + 2 * a) * LANES
            return spreads[p][:, at : at + LANES] + spreads[p][:, at + LANES : at + 2 * LANES]

        for s in range(high // chunk):
            flow = None
            for w in range(2):
                for a in range(0, per_n[p] // 2, 2):
                    at = [(a + i) * 2 * high + s * wide_high for i in range(2)]
                    left = jnp.concatenate([flows[w, i : i + wide_high, :] for i in at], axis=1)
                    right = jnp.concatenate([ones_of(w, a), ones_of(w, a + 1)], axis=1)
                    term = back(left, right)
                    flow = term if flow is None else flow + term
            flow = jnp.where(keep, flow, 0.0).reshape(chunk // SUB, 2, SUB, LANES)
            probe_t[s * chunk : (s + 1) * chunk, :] = (flow[:, 0] + flow[:, 1]).reshape(chunk, LANES)

        def put_flow(k, at, x):
            bufs[k, at, :] = x

        moves = [(lambda b: probe_t[tile(b), :], put_flow)]
        value16 = value_s[p]
        value = value16.astype(f32)
        d_total = dval[p]
        direct = jnp.sum(d_total * value, axis=0, keepdims=True)
        small = [direct[:, part(h)] for h in range(eh)]
        skip = skip_ref[2 * p : 2 * p + 1, :] + skip_ref[2 * p + 1 : 2 * p + 2, :]
        dv = skip * d_total
        for h in range(eh):
            for which, source in enumerate((dd_t, dp_t)):

                def put_tok(k, at, x, which=which, h=h):
                    bufs_tok[k, which, h, at, :] = x

                moves.append(
                    (lambda b, source=source, h=h: added(source, p, h, b, per_n[p] // few_n), put_tok)
                )
        from_scan(p, *moves)
        for k in range(2):
            d = 2 * p + k
            drive = jnp.concatenate([bufs_tok[k, 0, h] for h in range(eh)], axis=1)
            pull = jnp.concatenate([bufs_tok[k, 1, h] for h in range(eh)], axis=1)
            pace = jnp.concatenate([tok[p, k, h] for h in range(eh)], axis=1)
            dv = dv + drive * pace
            d_before = (drive * value + pull * (1.0 / LOG2E)) * slope[p, k]
            b_high, b_low = split2(d_before)
            bias_sum = jnp.sum(d_before, axis=0, keepdims=True)
            small += [bias_sum[:, part(h)] for h in range(eh)]
            d_proj = (
                bufs[k, :count, :] + back(b_high, swp[d, 0]) + back(b_low, swp[d, 0])
                + back(b_high, swp[d, 1])
            ).astype(bf16)
            dv = dv + dot(d_proj, wpk[d])
            put_wide(lot, cross(proj_s[p, k].astype(bf16), b_high)[2 * states : group])
            grad = cross(d_proj, value16)
            put_wide(lot, grad[2 * states : group])
            put_wide(lot, grad[: 2 * states])
            for h in range(eh):
                for m in range(copies_m[p]):
                    acc = None
                    for line in range(lines[p]):
                        s = 2 * line + k if p == 0 else 4 * m + 2 * k + line
                        term = dr_s[h, pl.ds(s, per_n[p], stride=SUB), :]
                        acc = term if acc is None else acc + term
                    put(lot, acc)
        put(lot, pad_rows(*small))
        steps = [sum_scatter(lot)]
        d_val = (dv * silu_slope(mixed_s[p, :, :inner])).astype(bf16)
        grad = cross(normed_s[p], d_val)
        if p == 0:
            in_acc[...] = grad
            return steps[0], jnp.concatenate([d_val, gate16], axis=1)
        put_wide(3, in_acc[...] + grad)
        return steps[0], sum_scatter(3), d_val

    def go_home(p, d_mixed):
        d_normed = back(d_mixed, in_weight_ref[:, : d_mixed.shape[1]])
        unused, pull = jax.vjp(
            lambda x: layer_norm(x, norm_gain_ref[...]), emb_r[p][...].reshape(count, model)
        )
        back_s[p][...] = pull(d_normed)[0].reshape(back_s[p].shape)

    def send_home(p):
        out = exchange(2, p, back_s[p], back_r[p])
        pending.extend(out)
        return out

    arrived(emb1)
    prologue(1)
    forward(1)
    y1 = swap(1, y_s1, y_r0)
    pending += y1
    arrived(emb0)
    prologue(0)
    forward(0)
    arrived(y1)
    arrived(cot0)
    y0 = swap(0, y_s0, y_r1)
    pending += y0
    gate16 = gate(0)
    first = sum_scatter(0)
    backward(0)
    second, d_mixed = finish_pair(0, gate16)
    go_home(0, d_mixed)
    first = sum_across(0, first)
    home0 = send_home(0)
    arrived(y0)
    arrived(cot1)
    gate(1)
    backward(1)
    first = sum_gather(0, first)
    flying = [sum_across(1, second)]

    third, fourth, d_mixed = finish_pair(1, None)
    third = sum_across(2, third)
    go_home(1, d_mixed)
    home1 = send_home(1)
    flying.append(sum_gather(1, flying[0]))
    sent(pending[:-4])
    del pending[:-4]
    home[...] = upstream_ref[...].astype(f32)
    arrived(home0)
    unpack(back_r0, bufs.at[0], 0)
    home[...] = home[...] + bufs[0, :count, :]
    fourth = sum_across(3, fourth)
    third = sum_gather(2, third)
    arrived(home1)
    unpack(back_r1, bufs.at[1], 1)
    feature_ref[...] = (home[...] + bufs[1, :count, :]).astype(bf16)
    fourth = sum_gather(3, fourth)
    for copies in (first, flying[1], third, fourth):
        arrived(copies)
    sent(pending)


def unpack_kernel(
    states, rank, grad_scale,
    feature_in, full0, full1, full2, full3, in_weight_ref, norm_gain_ref,
    feature_ref, in_grad_ref, scan_grad_ref, stepw_ref, stepb_ref, dr_ref, skip_grad_ref,
    norm_grad_ref, gain_grad_ref, out_grad_ref,
):
    feature_ref[...] = feature_in[...]
    inner = out_grad_ref.shape[0]
    eh = inner // LANES
    group = rank + 2 * states
    taken = [0] * 4
    lots = (full0, full1, full2, full3)

    def take(lot, height):
        at = taken[lot]
        taken[lot] += height
        return lots[lot][at : at + height, :] * grad_scale

    def take_wide(lot, out, at, height, width):
        for h in range(width // LANES):
            out[at : at + height, h * LANES : (h + 1) * LANES] = take(lot, height)

    def part(h):
        return slice(h * LANES, (h + 1) * LANES)

    small = take(0, SUB)
    for h in range(eh):
        gain_grad_ref[:, part(h)] = small[h : h + 1]
    take_wide(0, out_grad_ref, 0, inner, out_grad_ref.shape[1])
    model = in_grad_ref.shape[0]
    for h in range(eh):
        in_grad_ref[:, inner + h * LANES : inner + (h + 1) * LANES] = take(0, model)
    for p in range(2):
        lot = p + 1
        for k in range(2):
            d = 2 * p + k
            take_wide(lot, stepw_ref.at[d], 0, rank, inner)
            take_wide(lot, scan_grad_ref, d * group, rank, inner)
            take_wide(lot, scan_grad_ref, d * group + rank, 2 * states, inner)
            take_wide(lot, dr_ref.at[d], 0, states, inner)
        small = take(lot, -(-3 * eh // SUB) * SUB)
        for h in range(eh):
            for k in range(2):
                d = 2 * p + k
                skip_grad_ref[d : d + 1, part(h)] = small[h : h + 1]
                stepb_ref[d : d + 1, part(h)] = small[(k + 1) * eh + h : (k + 1) * eh + h + 1]
    take_wide(3, in_grad_ref, 0, model, inner)
    weighed = in_grad_ref[...] * in_weight_ref[...].astype(jnp.float32)
    norm_grad_ref[...] = (
        lax.dot_general(
            jnp.ones((SUB, weighed.shape[1]), jnp.float32), weighed, (((1,), (1,)), ((), ())),
            precision=HIGHEST, preferred_element_type=jnp.float32,
        )[0:1]
        / norm_gain_ref[...]
    )


def fast(
    classes, features, cotangent, table, norm_gain, in_weight, scan_weight, step_weight,
    step_bias, decay_log, skip_gain, output_gain, output_weight,
):
    tile_rows, tile_cols, model = features.shape
    inner = output_weight.shape[0]
    count = tile_rows * tile_cols
    rows, cols = lax.axis_size("row"), lax.axis_size("col")
    rank, states = step_weight.shape[1], decay_log.shape[1]
    group = rank + 2 * states
    eh = inner // LANES
    grad_scale = float(count * rows * cols) ** (-0.5)
    f32, bf16 = jnp.float32, jnp.bfloat16
    talls = (SUB * count // (tile_rows // cols), SUB * count // (tile_cols // rows))
    tall, sum_tall = max(talls), sum(talls)
    blocks = count // SUB
    lots = lots_of(rows, inner, model, states, rank, group, eh)
    per_row = ((cols, count // cols, model), (rows, count // rows, model))
    scratch = [((count, model), f32)]
    for name in range(6):
        scratch += [(per_row[0], f32), (per_row[1], f32)]
    scratch += [((blocks, SUB, inner), f32)] * 4
    scratch += [
        ((LANES, 2 * states * LANES), bf16),
        ((LANES, 2 * states * LANES // 2), bf16),
        ((4, LANES, inner), bf16),
        ((4, 2, LANES, inner), bf16),
        ((4, 2, inner, inner), bf16),
        ((2, eh, states * SUB, LANES), f32),
        ((2, count, model), bf16),
        ((2, count, 2 * inner), f32),
        ((2, count, inner), bf16),
        ((2, 2, count, LANES), f32),
        ((2, 2, eh, count, LANES), f32),
        ((2, 2, count, inner), f32),
        ((2, 2, 2 * count * states, LANES), f32),
        ((2, 2 * count * states, LANES), bf16),
        ((2, eh, 2 * count * states + states * SUB, LANES), f32),
        ((eh, sum_tall, LANES), f32),
        ((eh, sum_tall, LANES), f32),
        ((eh, tall, LANES), f32),
        ((eh, 2 * tall, LANES), f32),
        ((eh, 2 * tall, LANES), f32),
        ((2, count, LANES), f32),
        ((2, 2, eh, count, LANES), f32),
        ((tall, LANES), f32),
        ((tall, LANES), bf16),
        ((2, count, inner), f32),
        ((eh, states * SUB, LANES), f32),
        ((model, inner), f32),
    ]
    for lot in lots:
        chunk = (lot // rows, LANES)
        scratch += [((rows,) + chunk, f32), ((rows - 1,) + chunk, f32), ((cols,) + chunk, f32)]
    feature, *full = pl.pallas_call(
        functools.partial(fast_kernel, tile_rows, tile_cols, states, rank),
        out_shape=[
            jax.ShapeDtypeStruct((count, model), bf16),
        ]
        + [jax.ShapeDtypeStruct((rows, lot // rows, LANES), f32) for lot in lots],
        in_specs=[VMEM] * 13,
        out_specs=[VMEM] * 5,
        scratch_shapes=[pltpu.VMEM(*s) for s in scratch]
        + [
            pltpu.SemaphoreType.DMA((3, 2, 2)),
            pltpu.SemaphoreType.DMA((2, 2)),
            pltpu.SemaphoreType.DMA((4, 3, 2)),
        ],
        compiler_params=pltpu.CompilerParams(
            vmem_limit_bytes=BIG + 3 * 1024 * 1024, collective_id=1, has_side_effects=True
        ),
    )(
        features.reshape(count, model), classes, table, cotangent.reshape(count, model),
        norm_gain[None], in_weight, scan_weight.T,
        step_weight, step_bias, decay_log, skip_gain, output_gain[None], output_weight,
    )
    shapes = [
        ((count, model), bf16),
        (in_weight.shape, f32),
        (scan_weight.shape[::-1], f32),
        (step_weight.shape, f32),
        (step_bias.shape, f32),
        (decay_log.shape, f32),
        (skip_gain.shape, f32),
        ((1, model), f32),
        ((1, inner), f32),
        (output_weight.shape, f32),
    ]
    feature_grad, *grads = pl.pallas_call(
        functools.partial(unpack_kernel, states, rank, grad_scale),
        out_shape=[jax.ShapeDtypeStruct(*s) for s in shapes],
        in_specs=[VMEM] * 7,
        out_specs=[VMEM] * 10,
    )(
        feature, *[x.reshape(lot, LANES) for x, lot in zip(full, lots)], in_weight, norm_gain[None]
    )
    feature_grad = feature_grad.reshape(tile_rows, tile_cols, model)
    grads[1] = grads[1].T
    grads[6], grads[7] = grads[6][0], grads[7][0]
    return (feature_grad, *grads)


def local(*args):
    tile_rows, tile_cols, model = args[1].shape
    rows, cols = lax.axis_size("row"), lax.axis_size("col")
    rank, states, inner = args[7].shape[1], args[9].shape[1], args[12].shape[0]
    fits = (
        tile_rows == 4 * cols and tile_cols == 2 * rows and model == LANES and inner == 2 * LANES
        and states == 2 * SUB and rank == SUB and args[3].shape[0] <= LANES
    )
    return (fast if fits else general)(*args)


def solution(mesh):
    in_specs = (P("row", "col"), P("row", "col", None), P("row", "col", None)) + (P(),) * 10
    out_specs = (P("row", "col", None),) + (P(),) * 9
    return jax.shard_map(local, mesh=mesh, in_specs=in_specs, out_specs=out_specs, check_vma=False)
```

```python
import functools
import math

import jax
import jax.numpy as jnp
from jax import lax
from jax.experimental import pallas as pl
from jax.experimental.pallas import tpu as pltpu
from jax.sharding import PartitionSpec as P

EPS = 1e-05
HIGHEST = lax.Precision.HIGHEST
MESH = pl.DeviceIdType.MESH
LANES = 128
SUB = 8
LOG2E = math.log2(math.e)
VMEM = pl.BlockSpec(memory_space=pltpu.VMEM)
BIG = 60 * 1024 * 1024


def layer_norm(rows, gain):
    average = jnp.mean(rows, axis=-1, keepdims=True)
    centred = rows - average
    spread = jnp.mean(centred * centred, axis=-1, keepdims=True)
    return centred * lax.rsqrt(spread + EPS) * gain


def silu_slope(before):
    sigma = jax.nn.sigmoid(before)
    return sigma * (1.0 + before * (1.0 - sigma))


def embed(features, classes, table):
    labels = jnp.arange(table.shape[0], dtype=jnp.int32)
    onehot = (classes[..., None] == labels).astype(jnp.float32)
    lookup = jnp.einsum("hwk,kd->hwd", onehot, table, precision=HIGHEST)
    return features.astype(jnp.float32) + lookup


def gate_output(total, gate_in, output_gain):
    return layer_norm(total, output_gain) * jax.nn.silu(gate_in)


def greet(axes):
    barrier = pltpu.get_barrier_semaphore()
    partners = 0
    for axis in axes:
        count = lax.axis_size(axis)
        me = lax.axis_index(axis)
        for d in range(1, count):
            pl.semaphore_signal(
                barrier, inc=1, device_id={axis: lax.rem(me + d, count)}, device_id_type=MESH
            )
            partners += 1
    pl.semaphore_wait(barrier, partners)


def half(ref, k, h, t):
    return ref[k, h, pl.ds(t, 1), :]


def walk(lines, tile, blocks, group, start, step):
    def outer(b, carry):
        def inner(j, carry):
            time = b * tile + j
            rising = b * (tile * lines) + j
            falling = (blocks - 1 - b) * (tile * lines) + (tile - 1 - j)
            tokens = [[base + line * tile for line in group] for base in (rising, falling)]
            return step(carry, tokens, time)

        return lax.fori_loop(0, tile, inner, carry, unroll=2)

    return lax.fori_loop(0, blocks, outer, start)


def groups_of(lines):
    size = 2 if lines % 2 == 0 else 1
    return [tuple(range(g, g + size)) for g in range(0, lines, size)]


def fold(ref, k, h, count):
    total = ref[k, h, pl.ds(0, count, stride=SUB), :]
    for s in range(1, SUB):
        total = total + ref[k, h, pl.ds(s, count, stride=SUB), :]
    return total


def softplus(x):
    return jnp.maximum(x, 0.0) + jnp.log1p(jnp.exp(-jnp.abs(x)))


def cross(a, b):
    return lax.dot_general(a, b, (((0,), (0,)), ((), ())), preferred_element_type=jnp.float32)


def back(a, b):
    return lax.dot_general(a, b, (((1,), (1,)), ((), ())), preferred_element_type=jnp.float32)


def general_kernel(
    tile_rows, tile_cols, states, rank, grad_scale, tiles,
    embedded_ref, upstream_ref, norm_gain_ref, in_weight_ref, scan_weight_ref, step_weight_ref,
    step_bias_ref, rate_ref, skip_ref, output_gain_ref, output_weight_ref,
    feature_ref, in_grad_ref, scan_grad_ref, stepw_ref, stepb_ref, dr_ref, skip_grad_ref,
    norm_grad_ref, gain_grad_ref, out_grad_ref,
    mixed, gate_grad, turn, along, down, wide, sv, steps, slope, low, hist, eight, pace8, up, dproj, dr_acc,
    mine0, from0, side0, all0, mine1, from1, side1, all1, sems, sumsems,
):
    count, inner = tile_rows * tile_cols, output_weight_ref.shape[0]
    rows, cols = lax.axis_size("row"), lax.axis_size("col")
    eh, nh = inner // LANES, states // SUB
    group = rank + 2 * states
    shapes = ((tile_rows // cols, tile_cols), (tile_cols // rows, tile_rows))
    boxes = (along, down)
    axes = ("col", "row")
    greet(("row", "col"))

    def post(turn_number, pair):
        axis, box = axes[pair], boxes[pair]
        size = lax.axis_size(axis)
        me = lax.axis_index(axis)
        copies = []
        for d in range(1, size):
            target = lax.rem(me + d, size)
            copy = pltpu.make_async_remote_copy(
                src_ref=box.at[2 * turn_number, target],
                dst_ref=box.at[2 * turn_number + 1, me],
                send_sem=sems.at[turn_number, pair, 0, d],
                recv_sem=sems.at[turn_number, pair, 1, d],
                device_id={axis: target},
                device_id_type=MESH,
            )
            copy.start()
            copies.append(copy)
        box[2 * turn_number + 1, me] = box[2 * turn_number, me]
        return copies

    def finish(copies):
        for copy in copies:
            copy.wait()

    def put_home(turn_number, x):
        along[2 * turn_number] = x.reshape(along.shape[1:])
        first = post(turn_number, 0)
        for h in range(eh):
            turn[h] = x[:, h * LANES : (h + 1) * LANES]
        per = tile_cols // rows
        for c in range(tile_cols):
            for h in range(eh):
                down[
                    2 * turn_number, c // per,
                    (c % per) * tile_rows : (c % per + 1) * tile_rows,
                    h * LANES : (h + 1) * LANES,
                ] = turn[h, pl.ds(c, tile_rows, stride=tile_cols), :]
        return first, post(turn_number, 1)

    def take_home(turn_number):
        per = tile_cols // rows
        for c in range(tile_cols):
            for h in range(eh):
                turn[h, pl.ds(c, tile_rows, stride=tile_cols), :] = down[
                    2 * turn_number + 1, c // per,
                    (c % per) * tile_rows : (c % per + 1) * tile_rows,
                    h * LANES : (h + 1) * LANES,
                ]
        here = along[2 * turn_number + 1].reshape(count, inner)
        return here + jnp.concatenate([turn[h] for h in range(eh)], axis=1)

    def lines_in(turn_number, pair):
        return boxes[pair][2 * turn_number + 1].reshape(count, inner)

    def lines_out(turn_number, pair, x):
        boxes[pair][2 * turn_number] = x.reshape(boxes[pair].shape[1:])
        return post(turn_number, pair)

    def rate_of(d, m, h):
        return rate_ref[d, m * SUB : (m + 1) * SUB, h * LANES : (h + 1) * LANES]

    def part(h):
        return slice(h * LANES, (h + 1) * LANES)

    zero = jnp.zeros((SUB, LANES), jnp.float32)

    sums = ((mine0, from0, side0, all0), (mine1, from1, side1, all1))
    fill = [0, 0]

    def put(lot, x):
        mine = sums[lot][0]
        per = mine.shape[1] // SUB
        for i in range(x.shape[0] // SUB):
            tile = fill[lot]
            at = (tile % per) * SUB
            mine[tile // per, at : at + SUB, :] = x[i * SUB : (i + 1) * SUB]
            fill[lot] += 1

    def put_wide(lot, x):
        for h in range(x.shape[1] // LANES):
            put(lot, x[:, h * LANES : (h + 1) * LANES])

    taken = [0, 0]

    def take(lot, height):
        full = sums[lot][3]
        per = full.shape[1] // SUB
        out = []
        for i in range(height // SUB):
            tile = taken[lot]
            at = (tile % per) * SUB
            out.append(full[tile // per, at : at + SUB, :])
            taken[lot] += 1
        return jnp.concatenate(out, axis=0) * grad_scale

    def take_wide(lot, height, width):
        return jnp.concatenate([take(lot, height) for h in range(width // LANES)], axis=1)

    def pad_rows(*rows_in):
        missing = -len(rows_in) % SUB
        return jnp.concatenate(list(rows_in) + [jnp.zeros((missing, LANES), jnp.float32)], axis=0)

    def pad_lot(lot):
        while fill[lot] < tiles[lot]:
            put(lot, zero)

    def spread(lot, phase, axis, source, result):
        size = lax.axis_size(axis)
        me = lax.axis_index(axis)
        copies = []
        for d in range(1, size):
            target = lax.rem(me + d, size)
            copy = pltpu.make_async_remote_copy(
                src_ref=source(target),
                dst_ref=result(me, d),
                send_sem=sumsems.at[lot, phase, 0, d],
                recv_sem=sumsems.at[lot, phase, 1, d],
                device_id={axis: target},
                device_id_type=MESH,
            )
            copy.start()
            copies.append(copy)
        return copies

    def sum_scatter(lot):
        mine, other, side, full = sums[lot]
        pad_lot(lot)
        return spread(lot, 0, "row", lambda t: mine.at[t], lambda me, d: other.at[d - 1])

    def sum_across(lot, copies):
        mine, other, side, full = sums[lot]
        finish(copies)
        acc = mine[lax.axis_index("row")]
        for d in range(rows - 1):
            acc = acc + other[d]
        me = lax.axis_index("col")
        side[me] = acc
        return spread(lot, 1, "col", lambda t: side.at[me], lambda m, d: side.at[m])

    def sum_gather(lot, copies):
        mine, other, side, full = sums[lot]
        finish(copies)
        acc = side[0]
        for d in range(1, cols):
            acc = acc + side[d]
        me = lax.axis_index("row")
        full[me] = acc
        return spread(lot, 2, "row", lambda t: full.at[me], lambda m, d: full.at[m])

    embedded = embedded_ref[...]
    normed = layer_norm(embedded, norm_gain_ref[...]).astype(jnp.bfloat16)
    mixed[...] = jnp.dot(normed, in_weight_ref[...], preferred_element_type=jnp.float32)
    values = jax.nn.silu(mixed[:, :inner]).astype(jnp.bfloat16).astype(jnp.float32)
    arriving = put_home(0, values)

    leaving = []
    for pair in range(2):
        lines, tile = shapes[pair]
        length = count // lines
        blocks = length // tile
        finish(arriving[pair])
        value = lines_in(0, pair)
        wide_p, sv_p, steps_p, hist_p = wide.at[pair], sv.at[pair], steps.at[pair], hist.at[pair]
        weight = scan_weight_ref[:, 2 * pair * group : 2 * (pair + 1) * group]
        projected = jnp.dot(
            value.astype(jnp.bfloat16), weight, preferred_element_type=jnp.float32
        )
        for k in range(2):
            d = 2 * pair + k
            lowrank = projected[:, k * group : k * group + rank]
            low[d] = lowrank
            before = (
                jnp.dot(
                    lowrank, step_weight_ref[d], precision=HIGHEST,
                    preferred_element_type=jnp.float32,
                )
                + step_bias_ref[d : d + 1, :]
            )
            slope[d] = jax.nn.sigmoid(before)
            pace = softplus(before)
            for h in range(eh):
                steps_p[k, h] = pace[:, part(h)]
                sv_p[k, h] = pace[:, part(h)] * value[:, part(h)]
            for which in range(2):
                for n in range(states):
                    col = k * group + rank + which * states + n
                    wide_p[k, which, pl.ds(n, count, stride=states), :] = jnp.broadcast_to(
                        projected[:, col : col + 1], (count, LANES)
                    )
            for h in range(eh):
                for line in range(lines):
                    at = line * (length + 1) * states
                    hist_p[k, h, at : at + states, :] = jnp.zeros((states, LANES), jnp.float32)
        for lot in groups_of(lines):

            def advance(carry, tokens, time):
                new = []
                i = 0
                for k in range(2):
                    for line, t in zip(lot, tokens[k]):
                        drive = [half(sv_p, k, h, t) for h in range(eh)]
                        pace = [half(steps_p, k, h, t) for h in range(eh)]
                        sums = [None] * eh
                        for m in range(nh):
                            at = pl.ds(pl.multiple_of(t * states + m * SUB, SUB), SUB)
                            slot = (line * (length + 1) + time + 1) * states + m * SUB
                            source = wide_p[k, 0, at, :]
                            probe = wide_p[k, 1, at, :]
                            for h in range(eh):
                                a = jnp.exp2(pace[h] * rate_of(2 * pair + k, m, h))
                                state = a * carry[i] + source * drive[h]
                                i += 1
                                hist_p[k, h, pl.ds(pl.multiple_of(slot, SUB), SUB), :] = state
                                new.append(state)
                                term = probe * state
                                sums[h] = term if sums[h] is None else sums[h] + term
                        for h in range(eh):
                            eight[k, h, pl.ds(pl.multiple_of(t * SUB, SUB), SUB), :] = sums[h]
                return tuple(new)

            walk(lines, tile, blocks, lot, (zero,) * (2 * len(lot) * eh * nh), advance)
        skip = skip_ref[2 * pair : 2 * pair + 1, :] + skip_ref[2 * pair + 1 : 2 * pair + 2, :]
        y = skip * value + jnp.concatenate(
            [fold(eight, 0, h, count) + fold(eight, 1, h, count) for h in range(eh)], axis=1
        )
        leaving.append(lines_out(1, pair, y))
    finish(leaving[0])
    finish(leaving[1])
    total = take_home(1)

    upstream = upstream_ref[...]
    gated, gate_pull = jax.vjp(gate_output, total, mixed[:, inner:], output_gain_ref[...])
    d_gated = back(upstream, output_weight_ref[...])
    d_total, d_gate_in, gain_grad = gate_pull(d_gated)
    arriving = put_home(2, d_total)
    gate_grad[...] = d_gate_in
    put(0, pad_rows(*[gain_grad[:, part(h)] for h in range(eh)]))
    put_wide(0, cross(gated.astype(jnp.bfloat16), upstream))

    leaving = []
    for pair in range(2):
        lines, tile = shapes[pair]
        length = count // lines
        blocks = length // tile
        finish(arriving[pair])
        g_all = lines_in(2, pair)
        wide_p, sv_p, steps_p, hist_p = wide.at[pair], sv.at[pair], steps.at[pair], hist.at[pair]
        for h in range(eh):
            up[0, h] = g_all[:, part(h)]
        for lot in groups_of(lines):

            def retreat(carry, tokens, time):
                grads, rates = carry
                rates = list(rates)
                new = []
                i = 0
                for k in range(2):
                    for line, t in zip(lot, tokens[1 - k]):
                        drive = [half(sv_p, k, h, t) for h in range(eh)]
                        pace = [half(steps_p, k, h, t) for h in range(eh)]
                        g = [half(up, 0, h, t) for h in range(eh)]
                        dd = [None] * eh
                        dp = [None] * eh
                        for m in range(nh):
                            at = pl.ds(pl.multiple_of(t * states + m * SUB, SUB), SUB)
                            slot = (line * (length + 1) + length - 1 - time) * states + m * SUB
                            earlier = pl.ds(pl.multiple_of(slot, SUB), SUB)
                            current = pl.ds(pl.multiple_of(slot + states, SUB), SUB)
                            source = wide_p[k, 0, at, :]
                            probe = wide_p[k, 1, at, :]
                            flow = None
                            read = None
                            for h in range(eh):
                                rate = rate_of(2 * pair + k, m, h)
                                grad = grads[i] + probe * g[h]
                                i += 1
                                term = grad * drive[h]
                                flow = term if flow is None else flow + term
                                term = g[h] * hist_p[k, h, current, :]
                                read = term if read is None else read + term
                                term = grad * source
                                dd[h] = term if dd[h] is None else dd[h] + term
                                carried = jnp.exp2(pace[h] * rate) * grad
                                q = carried * hist_p[k, h, earlier, :]
                                term = q * rate
                                dp[h] = term if dp[h] is None else dp[h] + term
                                j = (k * nh + m) * eh + h
                                rates[j] = rates[j] + q * pace[h]
                                new.append(carried)
                            wide_p[k, 0, at, :] = flow
                            wide_p[k, 1, at, :] = read
                        for h in range(eh):
                            at8 = pl.ds(pl.multiple_of(t * SUB, SUB), SUB)
                            eight[k, h, at8, :] = dd[h]
                            pace8[k, h, at8, :] = dp[h]
                return (tuple(new), tuple(rates))

            chains = 2 * len(lot) * eh * nh
            unused, rates = walk(
                lines, tile, blocks, lot, ((zero,) * chains, (zero,) * (2 * eh * nh)), retreat
            )
            for k in range(2):
                for m in range(nh):
                    for h in range(eh):
                        place = (2 * pair + k, slice(m * SUB, (m + 1) * SUB), part(h))
                        add = rates[(k * nh + m) * eh + h] * rate_ref[place] * (1.0 / LOG2E)
                        if lot[0] == 0:
                            dr_acc[place] = add
                        else:
                            dr_acc[place] += add
        value = lines_in(0, pair)
        g_all = lines_in(2, pair)
        skip = skip_ref[2 * pair : 2 * pair + 1, :] + skip_ref[2 * pair + 1 : 2 * pair + 2, :]
        dv = skip * g_all
        direct = jnp.sum(g_all * value, axis=0, keepdims=True)
        small = [direct[:, part(h)] for h in range(eh)]
        for k in range(2):
            d = 2 * pair + k
            drive = jnp.concatenate([fold(eight, k, h, count) for h in range(eh)], axis=1)
            pace = jnp.concatenate([fold(pace8, k, h, count) for h in range(eh)], axis=1)
            dv = dv + drive * jnp.concatenate([steps_p[k, h] for h in range(eh)], axis=1)
            d_before = (drive * value + pace * (1.0 / LOG2E)) * slope[d]
            bias_sum = jnp.sum(d_before, axis=0, keepdims=True)
            small += [bias_sum[:, part(h)] for h in range(eh)]
            put_wide(
                pair,
                lax.dot_general(
                    low[d], d_before, (((0,), (0,)), ((), ())), precision=HIGHEST,
                    preferred_element_type=jnp.float32,
                ),
            )
            put_wide(pair, dr_acc[d])
            dproj[:, k * group : k * group + rank] = lax.dot_general(
                d_before, step_weight_ref[d], (((1,), (1,)), ((), ())), precision=HIGHEST,
                preferred_element_type=jnp.float32,
            )
            lane = lax.broadcasted_iota(jnp.int32, (LANES, 2 * states), 1)
            flow = None
            for j in range(2 * states):
                x = wide_p[k, j // states, pl.ds(j % states, count, stride=states), :]
                pick = (lane == j).astype(jnp.bfloat16)
                term = jnp.dot(x.astype(jnp.bfloat16), pick, preferred_element_type=jnp.float32)
                flow = term if flow is None else flow + term
            dproj[:, k * group + rank : (k + 1) * group] = flow
        d_projected = dproj[...].astype(jnp.bfloat16)
        span = slice(2 * pair * group, 2 * (pair + 1) * group)
        leaving.append(lines_out(3, pair, back(d_projected, scan_weight_ref[:, span]) + dv))
        put(pair, pad_rows(*small))
        put_wide(pair, cross(d_projected, value.astype(jnp.bfloat16)))
        if pair == 0:
            early = sum_scatter(0)
        else:
            early = sum_across(0, early)
    finish(leaving[0])
    finish(leaving[1])
    d_values = take_home(3)
    early = sum_gather(0, early)

    d_mixed = jnp.concatenate(
        [d_values * silu_slope(mixed[:, :inner]), gate_grad[...]], axis=1
    ).astype(jnp.bfloat16)
    normed, norm_pull = jax.vjp(layer_norm, embedded_ref[...], norm_gain_ref[...])
    put_wide(1, cross(normed.astype(jnp.bfloat16), d_mixed))
    d_embedded, norm_grad = norm_pull(back(d_mixed, in_weight_ref[...]))
    put(1, pad_rows(norm_grad))
    late = sum_scatter(1)
    feature_ref[...] = (upstream_ref[...].astype(jnp.float32) + d_embedded).astype(jnp.bfloat16)
    late = sum_across(1, late)
    finish(early)
    late = sum_gather(1, late)

    def take_pair(pair):
        for d in (2 * pair, 2 * pair + 1):
            stepw_ref[d] = take_wide(pair, rank, inner)
            dr_ref[d] = take_wide(pair, states, inner)
        small = take(pair, -(-3 * eh // SUB) * SUB)
        for h in range(eh):
            for k in range(2):
                d = 2 * pair + k
                skip_grad_ref[d : d + 1, part(h)] = small[h : h + 1]
                stepb_ref[d : d + 1, part(h)] = small[(k + 1) * eh + h : (k + 1) * eh + h + 1]
        span = slice(2 * pair * group, 2 * (pair + 1) * group)
        scan_grad_ref[:, span] = take_wide(pair, 2 * group, inner).T

    small = take(0, SUB)
    for h in range(eh):
        gain_grad_ref[:, part(h)] = small[h : h + 1]
    out_grad_ref[...] = take_wide(0, inner, out_grad_ref.shape[1])
    take_pair(0)
    finish(late)
    take_pair(1)
    in_grad_ref[...] = take_wide(1, in_grad_ref.shape[0], in_grad_ref.shape[1])
    norm_grad_ref[...] = take(1, SUB)[0:1]


def general(
    classes, features, cotangent, table, norm_gain, in_weight, scan_weight, step_weight,
    step_bias, decay_log, skip_gain, output_gain, output_weight,
):
    tile_rows, tile_cols, model_width = features.shape
    inner = output_weight.shape[0]
    count = tile_rows * tile_cols
    rows, cols = lax.axis_size("row"), lax.axis_size("col")
    rank = step_weight.shape[1]
    states = decay_log.shape[1]
    group = rank + 2 * states
    eh = inner // LANES
    lines = max(tile_rows // cols, tile_cols // rows)
    grad_scale = float(count * rows * cols) ** (-0.5)
    rate2 = -jnp.exp(decay_log) * LOG2E
    embedded = embed(features, classes, table).reshape(count, model_width)
    f32 = jnp.float32
    shapes = [
        ((count, model_width), jnp.bfloat16),
        (in_weight.shape, f32),
        (scan_weight.shape, f32),
        (step_weight.shape, f32),
        (step_bias.shape, f32),
        (decay_log.shape, f32),
        (skip_gain.shape, f32),
        ((1, model_width), f32),
        ((1, inner), f32),
        (output_weight.shape, f32),
    ]
    scratch = [
        ((count, 2 * inner), f32),
        ((count, inner), f32),
        ((eh, count, LANES), f32),
        ((8, cols, count // cols, inner), f32),
        ((8, rows, count // rows, inner), f32),
        ((2, 2, 2, count * states, LANES), f32),
        ((2, 2, eh, count, LANES), f32),
        ((2, 2, eh, count, LANES), f32),
        ((4, count, inner), f32),
        ((4, count, rank), f32),
        ((2, 2, eh, (count + lines) * states, LANES), f32),
        ((2, eh, count * SUB, LANES), f32),
        ((2, eh, count * SUB, LANES), f32),
        ((1, eh, count, LANES), f32),
        ((count, 2 * group), f32),
        (decay_log.shape, f32),
    ]
    pair_tiles = eh * (2 * rank + 2 * states + 2 * group) // SUB + -(-3 * eh // SUB)
    least = (
        1 + inner * model_width // (LANES * SUB) + pair_tiles,
        1 + in_weight.size // (LANES * SUB) + pair_tiles,
    )
    tiles = tuple(-(-t // rows) * rows for t in least)
    for lot in range(2):
        chunk = (tiles[lot] // rows * SUB, LANES)
        scratch += [((rows,) + chunk, f32), ((rows - 1,) + chunk, f32), ((cols,) + chunk, f32), ((rows,) + chunk, f32)]
    feature_grad, *grads = pl.pallas_call(
        functools.partial(general_kernel, tile_rows, tile_cols, states, rank, grad_scale, tiles),
        out_shape=[jax.ShapeDtypeStruct(*s) for s in shapes],
        in_specs=[VMEM] * 11,
        out_specs=[VMEM] * 10,
        scratch_shapes=[pltpu.VMEM(*s) for s in scratch]
        + [
            pltpu.SemaphoreType.DMA((4, 2, 2, max(rows, cols))),
            pltpu.SemaphoreType.DMA((2, 3, 2, max(rows, cols))),
        ],
        compiler_params=pltpu.CompilerParams(
            vmem_limit_bytes=BIG, collective_id=1, has_side_effects=True
        ),
    )(
        embedded, cotangent.reshape(count, model_width), norm_gain[None], in_weight, scan_weight,
        step_weight, step_bias, rate2, skip_gain, output_gain[None], output_weight,
    )
    feature_grad = feature_grad.reshape(tile_rows, tile_cols, model_width)
    grads[6], grads[7] = grads[6][0], grads[7][0]
    return (feature_grad, *grads)


def split2(x):
    high = x.astype(jnp.bfloat16)
    return high, (x - high.astype(jnp.float32)).astype(jnp.bfloat16)


def dot(a, b):
    return jnp.dot(a, b, preferred_element_type=jnp.float32)


def greet_all():
    barrier = pltpu.get_barrier_semaphore()
    rows, cols = lax.axis_size("row"), lax.axis_size("col")
    r, c = lax.axis_index("row"), lax.axis_index("col")
    for dr in range(rows):
        for dc in range(cols):
            if dr or dc:
                there = {"row": lax.rem(r + dr, rows), "col": lax.rem(c + dc, cols)}
                pl.semaphore_signal(barrier, inc=1, device_id=there, device_id_type=MESH)
    pl.semaphore_wait(barrier, rows * cols - 1)


def lots_of(rows, inner, model_width, states, rank, group, eh):
    pair = (rank + states + group) * 2 * eh + -(-3 * eh // SUB) * SUB
    gated = SUB + inner * model_width // LANES + model_width * eh
    per = SUB * rows
    return tuple(-(-n // per) * per for n in (gated, pair, pair, model_width * eh))


def fast_kernel(
    tile_rows, tile_cols, states, rank,
    features_ref, classes_ref, table_ref, upstream_ref, norm_gain_ref, in_weight_ref, sw_ref,
    step_weight_ref, step_bias_ref, decay_ref, skip_ref, output_gain_ref, output_weight_ref,
    feature_ref, full0, full1, full2, full3,
    home, emb_s0, emb_s1, emb_r0, emb_r1, cot_s0, cot_s1, cot_r0, cot_r1,
    back_s0, back_s1, back_r0, back_r1, y_s0, y_s1, y_r0, y_r1,
    spread0, spread1, wpk, swp, cmat, rate_s, normed_s, mixed_s, value_s, proj_s, tok, slope,
    wide, flows, hist, pace_t, drive_t, g_t, dd_t, dp_t, bufs, bufs_tok, probe_t, lhs, dval, dr_s, in_acc,
    mine0, from0, side0, mine1, from1, side1, mine2, from2, side2, mine3, from3, side3,
    sems, ysems, sumsems,
):
    f32, bf16 = jnp.float32, jnp.bfloat16
    count, inner = tile_rows * tile_cols, output_weight_ref.shape[0]
    model = features_ref.shape[1]
    rows, cols = lax.axis_size("row"), lax.axis_size("col")
    me_r, me_c = lax.axis_index("row"), lax.axis_index("col")
    eh = inner // LANES
    group = rank + 2 * states
    lines = (tile_rows // cols, tile_cols // rows)
    length = (count // lines[0], count // lines[1])
    copies_m = tuple(SUB // (2 * n) for n in lines)
    per_n = tuple(states // m for m in copies_m)
    tall = tuple(SUB * n for n in length)
    blocks = count // SUB
    axes = ("col", "row")
    sizes = (cols, rows)
    zero = jnp.zeros((SUB, LANES), f32)
    sub = lax.broadcasted_iota(jnp.int32, (SUB, LANES), 0)
    even = lax.rem(sub, 2) == 0
    pos = sub // 2
    pos_even = lax.rem(pos, 2) == 0
    pos_edge = (pos == 0) | (pos == 3)
    low_half = sub < 4

    def part(h):
        return slice(h * LANES, (h + 1) * LANES)

    def tile(b):
        return pl.ds(pl.multiple_of(b * SUB, SUB), SUB)

    def step_tile(p, b):
        return tile(b + (length[0] if p else 0))

    def tile2(b):
        return pl.ds(pl.multiple_of(b * 2 * SUB, 2 * SUB), 2 * SUB)

    greet_all()

    def pack(src, dst, p):
        if p == 0:
            for rho in range(tile_rows):
                c, i = rho // lines[0], rho % lines[0]
                for j in range(2):
                    dst[c, pl.ds(2 * i + j, tile_cols // 2, stride=SUB), :] = src[
                        pl.ds(rho * tile_cols + j, tile_cols // 2, stride=2), :
                    ]
        else:
            for r in range(rows):
                for j in range(2):
                    dst[r, pl.ds(j, tile_rows, stride=2), :] = src[
                        pl.ds(2 * r + j, tile_rows, stride=tile_cols), :
                    ]

    def unpack(src, dst, p):
        if p == 0:
            for rho in range(tile_rows):
                c, i = rho // lines[0], rho % lines[0]
                for j in range(2):
                    dst[pl.ds(rho * tile_cols + j, tile_cols // 2, stride=2), :] = src[
                        c, pl.ds(2 * i + j, tile_cols // 2, stride=SUB), :
                    ]
        else:
            for r in range(rows):
                for j in range(2):
                    dst[pl.ds(2 * r + j, tile_rows, stride=tile_cols), :] = src[
                        r, pl.ds(j, tile_rows, stride=2), :
                    ]

    def batch(src, dst, amount, send, recv):
        return pltpu.make_async_remote_copy(
            src_ref=src.at[pl.ds(0, amount)], dst_ref=dst.at[pl.ds(0, amount)], send_sem=send,
            recv_sem=recv, device_id={"row": me_r, "col": me_c}, device_id_type=MESH,
        )

    def exchange(turn, p, src, dst):
        size, axis = sizes[p], axes[p]
        me = lax.axis_index(axis)
        for d in range(1, size):
            target = lax.rem(me + d, size)
            copy = pltpu.make_async_remote_copy(
                src_ref=src.at[target],
                dst_ref=dst.at[me],
                send_sem=sems.at[turn, p, 0],
                recv_sem=sems.at[turn, p, 1],
                device_id={axis: target},
                device_id_type=MESH,
            )
            copy.start()
        dst[me] = src[me]
        return [batch(src, dst, size - 1, sems.at[turn, p, 0], sems.at[turn, p, 1])]

    def swap(p, src, dst):
        for dr in range(rows):
            for dc in range(cols):
                r, c = lax.rem(me_r + dr, rows), lax.rem(me_c + dc, cols)
                if p == 0:
                    there, here = c * rows + r, me_r * cols + me_c
                else:
                    there, here = r * cols + c, me_c * rows + me_r
                if dr == 0 and dc == 0:
                    dst[here] = src[there]
                    continue
                copy = pltpu.make_async_remote_copy(
                    src_ref=src.at[there],
                    dst_ref=dst.at[here],
                    send_sem=ysems.at[p, 0],
                    recv_sem=ysems.at[p, 1],
                    device_id={"row": r, "col": c},
                    device_id_type=MESH,
                )
                copy.start()
        return [batch(src, dst, rows * cols - 1, ysems.at[p, 0], ysems.at[p, 1])]

    def arrived(copies):
        for copy in copies:
            copy.wait_recv()

    def sent(copies):
        for copy in copies:
            copy.wait_send()

    emb_s, emb_r = (emb_s0, emb_s1), (emb_r0, emb_r1)
    cot_s, cot_r = (cot_s0, cot_s1), (cot_r0, cot_r1)
    back_s, back_r = (back_s0, back_s1), (back_r0, back_r1)
    y_s, y_r = (y_s0, y_s1), (y_r0, y_r1)
    spreads = (spread0, spread1)
    pending = []
    half_n, few_n = SUB, SUB // 2
    y_t = dd_t

    def group_tile(p, g, t):
        return tile(g * length[p] + t)

    def added(ref, p, h, b, groups):
        total = ref[h, group_tile(p, 0, b), :]
        for g in range(1, groups):
            total = total + ref[h, group_tile(p, g, b), :]
        return total

    token = lax.broadcasted_iota(jnp.int32, (count, tile_rows), 0)
    lane = lax.broadcasted_iota(jnp.int32, (count, tile_rows), 1)
    of_row = jnp.where(token // tile_cols == lane, 1.0, 0.0).astype(bf16)
    labels = dot(of_row, classes_ref[...].astype(f32).astype(bf16))
    token = lax.broadcasted_iota(jnp.int32, (count, tile_cols), 0)
    lane = lax.broadcasted_iota(jnp.int32, (count, tile_cols), 1)
    labels = jnp.where(lax.rem(token, tile_cols) == lane, labels, 0.0).astype(bf16)
    labels = dot(labels, jnp.ones((tile_cols, LANES), bf16))
    lane = lax.broadcasted_iota(jnp.int32, (count, LANES), 1).astype(f32)
    onehot = jnp.where(labels == lane, 1.0, 0.0).astype(bf16)
    entries = table_ref[...]
    lookup = None
    for i in range(3):
        rounded = entries.astype(bf16).astype(f32)
        rest = jnp.zeros((LANES - entries.shape[0], model), f32)
        term = dot(onehot, jnp.concatenate([rounded, rest], axis=0).astype(bf16))
        lookup = term if lookup is None else lookup + term
        entries = entries - rounded
    home[...] = features_ref[...].astype(f32) + lookup
    pack(home, emb_s1, 1)
    emb1 = exchange(0, 1, emb_s1, emb_r1)
    pack(home, emb_s0, 0)
    emb0 = exchange(0, 0, emb_s0, emb_r0)
    home[...] = upstream_ref[...].astype(f32)
    pack(home, cot_s0, 0)
    cot0 = exchange(1, 0, cot_s0, cot_r0)
    pack(home, cot_s1, 1)
    cot1 = exchange(1, 1, cot_s1, cot_r1)
    pending += emb1 + emb0 + cot0 + cot1

    key_row = lax.broadcasted_iota(jnp.int32, (LANES, 2 * LANES), 0)
    lane_tile = lax.broadcasted_iota(jnp.int32, (LANES, 2 * LANES), 1) // LANES
    for p in range(2):
        which = lax.rem(key_row, 2 * states) // states
        key = which * per_n[p] + lax.rem(key_row, per_n[p])
        key = jnp.where(key_row < 4 * states, key - lane_tile, -8 * states)
        for q in range(per_n[p]):
            spreads[p][:, 2 * q * LANES : 2 * (q + 1) * LANES] = jnp.where(
                key == 2 * q, 1.0, 0.0
            ).astype(bf16)
    sw32 = sw_ref[...].astype(f32)
    for d in range(4):
        off = d * group
        low_w = sw32[off : off + rank]
        wpk[d] = jnp.concatenate(
            [sw32[off + rank : off + group], low_w,
             jnp.zeros((LANES - group, inner), f32)], axis=0
        ).astype(bf16)
        step_w = step_weight_ref[d]
        w1, w2 = split2(step_w)
        w3 = (step_w - w1.astype(f32) - w2.astype(f32)).astype(bf16)
        blank = jnp.zeros((rank, inner), f32)
        left = jnp.concatenate([low_w, low_w, low_w, blank], axis=0).astype(bf16)
        right = jnp.concatenate(
            [w1.astype(f32), w2.astype(f32), w3.astype(f32), blank], axis=0
        ).astype(bf16)
        c_high, c_low = split2(cross(left, right))
        cmat[d, 0] = c_high
        cmat[d, 1] = c_low
        for i, w in enumerate((w1, w2)):
            swp[d, i] = jnp.concatenate(
                [jnp.zeros((2 * states, inner), f32), w.astype(f32),
                 jnp.zeros((LANES - group, inner), f32)], axis=0
            ).astype(bf16)
        rate = -jnp.exp(decay_ref[d]) * LOG2E
        p, k = d // 2, d % 2
        for n in range(states):
            m, n1 = n // per_n[p], n % per_n[p]
            for h in range(eh):
                row = jnp.broadcast_to(rate[n : n + 1, part(h)], (SUB, LANES))
                if p == 0:
                    mask = lax.rem(sub, 2) == k
                else:
                    mask = pos == 2 * m + k
                at = slice(n1 * SUB, (n1 + 1) * SUB)
                if k == 0 and m == 0:
                    rate_s[p, h, at, :] = row
                else:
                    rate_s[p, h, at, :] = jnp.where(mask, row, rate_s[p, h, at, :])

    def to_scan(p, *moves):
        def one(b, carry):
            for move in moves:
                one_of(b, *move)
            return carry

        def one_of(b, first, second, store):
            mirror = blocks - 1 - b
            x0, x1 = first(tile(b)), second(tile(mirror))
            if p == 0:
                z = jnp.where(even, x1, x0)
                store(2 * b, jnp.where(even, x0, x1))
                store(
                    2 * b + 1,
                    jnp.where(even, pltpu.roll(z, SUB - 1, 0), pltpu.roll(z, 1, 0)),
                )
            else:
                u = jnp.where(pos_even, x0, x1)
                v = pltpu.roll(u, 4, 0)
                u2 = pltpu.roll(jnp.where(pos_even, x1, x0), 2, 0)
                v2 = pltpu.roll(u2, 4, 0)
                store(4 * b, jnp.where(pos_edge, u, v))
                store(4 * b + 1, jnp.where(low_half, v2, u2))
                store(4 * b + 2, jnp.where(pos_edge, v, u))
                store(4 * b + 3, jnp.where(low_half, u2, v2))

        lax.fori_loop(0, blocks, one, 0, unroll=4)

    def from_scan(p, *moves):
        def one(b, carry):
            for move in moves:
                one_of(b, *move)
            return carry

        def one_of(b, load, store):
            mirror = blocks - 1 - b
            if p == 0:
                s0, s1 = load(2 * b), load(2 * b + 1)
                store(0, tile(b), jnp.where(even, s0, pltpu.roll(s1, 1, 0)))
                store(1, tile(mirror), jnp.where(even, pltpu.roll(s1, SUB - 1, 0), s0))
            else:
                a = []
                for i in range(4):
                    s = load(4 * b + i)
                    s = s + pltpu.roll(s, 4, 0)
                    a.append(pltpu.roll(s, 2, 0) if i % 2 else s)
                store(
                    0, tile(b),
                    jnp.where(low_half, jnp.where(pos == 0, a[0], a[1]), jnp.where(pos == 2, a[2], a[3])),
                )
                store(
                    1, tile(mirror),
                    jnp.where(low_half, jnp.where(pos == 0, a[3], a[2]), jnp.where(pos == 2, a[1], a[0])),
                )

        lax.fori_loop(0, blocks, one, 0, unroll=4)

    def put_step(ref, p, b, x):
        ref[step_tile(p, b), :] = x

    def put_at(ref, b, x):
        ref[tile(b), :] = x

    def put_probe(b, x):
        probe_t[tile(b), :] = x

    def prologue(p):
        embedded = emb_r[p][...].reshape(count, model)
        normed = layer_norm(embedded, norm_gain_ref[...]).astype(bf16)
        normed_s[p] = normed
        mixed_s[p] = dot(normed, in_weight_ref[...])
        value = jax.nn.silu(mixed_s[p, :, :inner]).astype(bf16)
        value_s[p] = value
        value32 = value.astype(f32)
        for k in range(2):
            d = 2 * p + k
            proj_s[p, k] = back(value, wpk[d])
            before = dot(value, cmat[d, 0]) + dot(value, cmat[d, 1]) + step_bias_ref[d : d + 1, :]
            slope[p, k] = jax.nn.sigmoid(before)
            pace = softplus(before)
            for h in range(eh):
                tok[p, k, h] = pace[:, part(h)]
        moves = [(lambda at: proj_s[p, 0, at, :], lambda at: proj_s[p, 1, at, :], put_probe)]
        for h in range(eh):
            bufs_tok[0, 0, h] = value32[:, part(h)]
            moves.append(
                (lambda at, h=h: tok[p, 0, h, at, :], lambda at, h=h: tok[p, 1, h, at, :],
                 functools.partial(put_step, pace_t.at[h], p))
            )
            moves.append(
                (lambda at, h=h: tok[p, 0, h, at, :] * bufs_tok[0, 0, h, at, :],
                 lambda at, h=h: tok[p, 1, h, at, :] * bufs_tok[0, 0, h, at, :],
                 functools.partial(put_step, drive_t.at[h], p))
            )
        to_scan(p, *moves)
        size_of = tall[p]
        x = jnp.where(keep_lanes(p, size_of), probe_t[:size_of, :], 0.0)
        high = x.astype(bf16).astype(f32)
        lhs[:size_of, :] = (high + pltpu.roll(x - high, 2 * states, 1)).astype(bf16)
        if copies_m[p] > 1:
            row = lax.broadcasted_iota(jnp.int32, (size_of, LANES), 0)
            x = jnp.where(lax.rem(row, SUB) < 4, x, pltpu.roll(x, LANES - per_n[p], 1))
        probe_t[:size_of, :] = x
        chunk = count
        for q in range(per_n[p]):
            w, n1 = 2 * q // per_n[p], 2 * q % per_n[p]
            for s in range(size_of // chunk):
                if q % 3 == 2:
                    for j in range(2):
                        at = (n1 + j) * size_of + s * chunk
                        col = w * states + n1 + j
                        wide[p, w, at : at + chunk, :] = jnp.broadcast_to(
                            probe_t[s * chunk : (s + 1) * chunk, col : col + 1], (chunk, LANES)
                        )
                    continue
                out = dot(
                    lhs[s * chunk : (s + 1) * chunk, :],
                    spreads[p][:, 2 * q * LANES : 2 * (q + 1) * LANES],
                )
                for j in range(2):
                    at = (n1 + j) * size_of + s * chunk
                    wide[p, w, at : at + chunk, :] = out[:, part(j)]

    def keep_lanes(p, height):
        lane = lax.broadcasted_iota(jnp.int32, (height, LANES), 1)
        keep = lane < 2 * states
        if copies_m[p] > 1:
            row = lax.broadcasted_iota(jnp.int32, (height, LANES), 0)
            m = lax.rem(row, SUB) // (SUB // copies_m[p])
            keep = keep & (lax.rem(lane, states) // per_n[p] == m)
        return keep

    def forward(p):
        high, stride = tall[p], tall[p] + SUB
        for h in range(eh):
            for n in range(per_n[p]):
                hist[p, h, n * stride : n * stride + SUB, :] = zero
        for g in range(per_n[p] // half_n):
            ns = range(g * half_n, (g + 1) * half_n)

            def step(t, carry, g=g, ns=ns):
                at = tile(t)
                pace = [pace_t[h, step_tile(p, t), :] for h in range(eh)]
                drive = [drive_t[h, step_tile(p, t), :] for h in range(eh)]
                y = [None] * eh
                new = []
                for i, n in enumerate(ns):
                    row = tile(n * (high // SUB) + t)
                    slot = tile(n * (stride // SUB) + t + 1)
                    source, probe = wide[p, 0, row, :], wide[p, 1, row, :]
                    for h in range(eh):
                        a = jnp.exp2(pace[h] * rate_s[p, h, n * SUB : (n + 1) * SUB, :])
                        state = a * carry[i * eh + h] + source * drive[h]
                        hist[p, h, slot, :] = state
                        new.append(state)
                        term = probe * state
                        y[h] = term if y[h] is None else y[h] + term
                for h in range(eh):
                    y_t[h, group_tile(p, g, t), :] = y[h]
                return tuple(new)

            lax.fori_loop(0, length[p], step, (zero,) * (half_n * eh), unroll=8)
        moves = []
        for h in range(eh):

            def put_y(k, at, x, h=h):
                bufs_tok[k, 0, h, at, :] = x

            moves.append((lambda b, h=h: added(y_t, p, h, b, per_n[p] // half_n), put_y))
        from_scan(p, *moves)
        for h in range(eh):
            y_s[p][:, :, part(h)] = (bufs_tok[0, 0, h] + bufs_tok[1, 0, h]).reshape(blocks, SUB, LANES)

    def gate(p):
        value = value_s[p].astype(f32)
        skips = jnp.sum(skip_ref[...], axis=0, keepdims=True)
        total = (
            y_s[p][...].reshape(count, inner) + y_r[p][...].reshape(count, inner) + skips * value
        )
        upstream = cot_r[p][...].reshape(count, model).astype(bf16)
        d_gated = back(upstream, output_weight_ref[...])
        gated, pull = jax.vjp(gate_output, total, mixed_s[p, :, inner:], output_gain_ref[...])
        d_total, d_gate_in, gain_grad = pull(d_gated)
        dval[p] = d_total
        if p == 0:
            put(0, pad_rows(*[gain_grad[:, part(h)] for h in range(eh)]))
            put_wide(0, cross(gated.astype(bf16), upstream))
            d_gate = d_gate_in.astype(bf16)
            gate16 = d_gate
            put_wide(0, cross(normed_s[p], d_gate))
        else:
            gate16 = None

        moves = []
        for h in range(eh):
            load = lambda at, h=h: dval[p, at, part(h)]
            moves.append((load, load, functools.partial(put_at, g_t.at[h])))
        to_scan(p, *moves)
        return gate16

    sums = (
        (mine0, from0, side0, full0), (mine1, from1, side1, full1),
        (mine2, from2, side2, full2), (mine3, from3, side3, full3),
    )
    fill = [0] * 4

    def put(lot, x):
        mine = sums[lot][0]
        per = mine.shape[1] // SUB
        for i in range(x.shape[0] // SUB):
            n = fill[lot]
            at = (n % per) * SUB
            mine[n // per, at : at + SUB, :] = x[i * SUB : (i + 1) * SUB]
            fill[lot] += 1

    def put_wide(lot, x):
        for h in range(x.shape[1] // LANES):
            put(lot, x[:, h * LANES : (h + 1) * LANES])

    def pad_rows(*rows_in):
        missing = -len(rows_in) % SUB
        return jnp.concatenate(list(rows_in) + [jnp.zeros((missing, LANES), f32)], axis=0)

    def pad_lot(lot):
        mine = sums[lot][0]
        while fill[lot] < rows * mine.shape[1] // SUB:
            put(lot, zero)

    def spread(lot, phase, axis, source, result, whole):
        size = lax.axis_size(axis)
        me = lax.axis_index(axis)
        for d in range(1, size):
            target = lax.rem(me + d, size)
            copy = pltpu.make_async_remote_copy(
                src_ref=source(target),
                dst_ref=result(me, d),
                send_sem=sumsems.at[lot, phase, 0],
                recv_sem=sumsems.at[lot, phase, 1],
                device_id={axis: target},
                device_id_type=MESH,
            )
            copy.start()
        out = [batch(whole, whole, size - 1, sumsems.at[lot, phase, 0], sumsems.at[lot, phase, 1])]
        pending.extend(out)
        return out

    def sum_scatter(lot):
        mine, other, side, full = sums[lot]
        pad_lot(lot)
        return spread(lot, 0, "row", lambda t: mine.at[t], lambda me, d: other.at[d - 1], other)

    def sum_across(lot, copies):
        mine, other, side, full = sums[lot]
        arrived(copies)
        acc = mine[me_r]
        for d in range(rows - 1):
            acc = acc + other[d]
        side[me_c] = acc
        return spread(lot, 1, "col", lambda t: side.at[me_c], lambda m, d: side.at[m], side)

    def sum_gather(lot, copies):
        mine, other, side, full = sums[lot]
        arrived(copies)
        acc = side[0]
        for d in range(1, cols):
            acc = acc + side[d]
        full[me_r] = acc
        return spread(lot, 2, "row", lambda t: full.at[me_r], lambda m, d: full.at[m], full)

    def backward(p, hook=None):
        high, stride = tall[p], tall[p] + SUB
        for g in range(per_n[p] // few_n):
            if hook is not None and g == 1:
                hook()
            ns = range(g * few_n, (g + 1) * few_n)

            def step(i, carry, g=g, ns=ns):
                grads, rates, t = carry
                at = tile(t)
                pace = [pace_t[h, step_tile(p, t), :] for h in range(eh)]
                drive = [drive_t[h, step_tile(p, t), :] for h in range(eh)]
                gs = [g_t[h, at, :] for h in range(eh)]
                dd, dp = [None] * eh, [None] * eh
                new, new_rates = [], []
                for i, n in enumerate(ns):
                    row = tile(n * (high // SUB) + t)
                    earlier = tile(n * (stride // SUB) + t)
                    current = tile(n * (stride // SUB) + t + 1)
                    source, probe = wide[p, 0, row, :], wide[p, 1, row, :]
                    flow = read = None
                    for h in range(eh):
                        j = i * eh + h
                        rate = rate_s[p, h, n * SUB : (n + 1) * SUB, :]
                        grad = grads[j] + probe * gs[h]
                        term = grad * drive[h]
                        flow = term if flow is None else flow + term
                        term = gs[h] * hist[p, h, current, :]
                        read = term if read is None else read + term
                        term = grad * source
                        dd[h] = term if dd[h] is None else dd[h] + term
                        carried = jnp.exp2(pace[h] * rate) * grad
                        q = carried * hist[p, h, earlier, :]
                        term = q * rate
                        dp[h] = term if dp[h] is None else dp[h] + term
                        new_rates.append(rates[j] + q * pace[h])
                        new.append(carried)
                    if n % 2 == 0:
                        kept = (flow, read)
                        continue
                    place = tile2((n // 2) * (high // SUB) + t)
                    for w, x in enumerate((flow, read)):
                        both = jnp.concatenate([kept[w], x], axis=0)
                        flows[w, place, :] = both.astype(bf16)
                for h in range(eh):
                    dd_t[h, group_tile(p, g, t), :] = dd[h]
                    dp_t[h, group_tile(p, g, t), :] = dp[h]
                return tuple(new), tuple(new_rates), t - 1

            chains = (zero,) * (few_n * eh)
            unused, rates, end = lax.fori_loop(
                0, length[p], step, (chains, chains, jnp.int32(length[p] - 1)), unroll=4
            )
            for i, n in enumerate(ns):
                for h in range(eh):
                    place = slice(n * SUB, (n + 1) * SUB)
                    dr_s[h, place, :] = rates[i * eh + h] * rate_s[p, h, place, :] * (1.0 / LOG2E)

    def finish_pair(p, gate16):
        lot = p + 1
        high = tall[p]
        chunk = count
        wide_high = 2 * chunk
        lane = lax.broadcasted_iota(jnp.int32, (wide_high, LANES), 1)
        row = lax.broadcasted_iota(jnp.int32, (wide_high, LANES), 0)
        mine = lax.rem(lane, 2) == lax.rem(row // SUB, 2)
        keep = keep_lanes(p, wide_high) & mine

        def ones_of(w, a):
            at = (w * per_n[p] + 2 * a) * LANES
            return spreads[p][:, at : at + LANES] + spreads[p][:, at + LANES : at + 2 * LANES]

        for s in range(high // chunk):
            flow = None
            for w in range(2):
                for a in range(0, per_n[p] // 2, 2):
                    at = [(a + i) * 2 * high + s * wide_high for i in range(2)]
                    left = jnp.concatenate([flows[w, i : i + wide_high, :] for i in at], axis=1)
                    right = jnp.concatenate([ones_of(w, a), ones_of(w, a + 1)], axis=1)
                    term = back(left, right)
                    flow = term if flow is None else flow + term
            flow = jnp.where(keep, flow, 0.0).reshape(chunk // SUB, 2, SUB, LANES)
            probe_t[s * chunk : (s + 1) * chunk, :] = (flow[:, 0] + flow[:, 1]).reshape(chunk, LANES)

        def put_flow(k, at, x):
            bufs[k, at, :] = x

        moves = [(lambda b: probe_t[tile(b), :], put_flow)]
        value16 = value_s[p]
        value = value16.astype(f32)
        d_total = dval[p]
        direct = jnp.sum(d_total * value, axis=0, keepdims=True)
        small = [direct[:, part(h)] for h in range(eh)]
        skip = skip_ref[2 * p : 2 * p + 1, :] + skip_ref[2 * p + 1 : 2 * p + 2, :]
        dv = skip * d_total
        for h in range(eh):
            for which, source in enumerate((dd_t, dp_t)):

                def put_tok(k, at, x, which=which, h=h):
                    bufs_tok[k, which, h, at, :] = x

                moves.append(
                    (lambda b, source=source, h=h: added(source, p, h, b, per_n[p] // few_n), put_tok)
                )
        from_scan(p, *moves)
        for k in range(2):
            d = 2 * p + k
            drive = jnp.concatenate([bufs_tok[k, 0, h] for h in range(eh)], axis=1)
            pull = jnp.concatenate([bufs_tok[k, 1, h] for h in range(eh)], axis=1)
            pace = jnp.concatenate([tok[p, k, h] for h in range(eh)], axis=1)
            dv = dv + drive * pace
            d_before = (drive * value + pull * (1.0 / LOG2E)) * slope[p, k]
            b_high, b_low = split2(d_before)
            bias_sum = jnp.sum(d_before, axis=0, keepdims=True)
            small += [bias_sum[:, part(h)] for h in range(eh)]
            d_proj = (
                bufs[k, :count, :] + back(b_high, swp[d, 0]) + back(b_low, swp[d, 0])
                + back(b_high, swp[d, 1])
            ).astype(bf16)
            dv = dv + dot(d_proj, wpk[d])
            put_wide(lot, cross(proj_s[p, k].astype(bf16), b_high)[2 * states : group])
            grad = cross(d_proj, value16)
            put_wide(lot, grad[2 * states : group])
            put_wide(lot, grad[: 2 * states])
            for h in range(eh):
                for m in range(copies_m[p]):
                    acc = None
                    for line in range(lines[p]):
                        s = 2 * line + k if p == 0 else 4 * m + 2 * k + line
                        term = dr_s[h, pl.ds(s, per_n[p], stride=SUB), :]
                        acc = term if acc is None else acc + term
                    put(lot, acc)
        put(lot, pad_rows(*small))
        steps = [sum_scatter(lot)]
        d_val = (dv * silu_slope(mixed_s[p, :, :inner])).astype(bf16)
        grad = cross(normed_s[p], d_val)
        if p == 0:
            in_acc[...] = grad
            return steps[0], jnp.concatenate([d_val, gate16], axis=1)
        put_wide(3, in_acc[...] + grad)
        return steps[0], sum_scatter(3), d_val

    def go_home(p, d_mixed):
        d_normed = back(d_mixed, in_weight_ref[:, : d_mixed.shape[1]])
        unused, pull = jax.vjp(
            lambda x: layer_norm(x, norm_gain_ref[...]), emb_r[p][...].reshape(count, model)
        )
        back_s[p][...] = pull(d_normed)[0].reshape(back_s[p].shape)

    def send_home(p):
        out = exchange(2, p, back_s[p], back_r[p])
        pending.extend(out)
        return out

    arrived(emb1)
    prologue(1)
    forward(1)
    y1 = swap(1, y_s1, y_r0)
    pending += y1
    arrived(emb0)
    prologue(0)
    forward(0)
    arrived(y1)
    arrived(cot0)
    y0 = swap(0, y_s0, y_r1)
    pending += y0
    gate16 = gate(0)
    first = sum_scatter(0)
    backward(0)
    second, d_mixed = finish_pair(0, gate16)
    go_home(0, d_mixed)
    first = sum_across(0, first)
    home0 = send_home(0)
    arrived(y0)
    arrived(cot1)
    gate(1)
    backward(1)
    first = sum_gather(0, first)
    flying = [sum_across(1, second)]

    third, fourth, d_mixed = finish_pair(1, None)
    third = sum_across(2, third)
    go_home(1, d_mixed)
    home1 = send_home(1)
    flying.append(sum_gather(1, flying[0]))
    sent(pending[:-4])
    del pending[:-4]
    home[...] = upstream_ref[...].astype(f32)
    arrived(home0)
    unpack(back_r0, bufs.at[0], 0)
    home[...] = home[...] + bufs[0, :count, :]
    fourth = sum_across(3, fourth)
    third = sum_gather(2, third)
    arrived(home1)
    unpack(back_r1, bufs.at[1], 1)
    feature_ref[...] = (home[...] + bufs[1, :count, :]).astype(bf16)
    fourth = sum_gather(3, fourth)
    for copies in (first, flying[1], third, fourth):
        arrived(copies)
    sent(pending)


def unpack_kernel(
    states, rank, grad_scale,
    feature_in, full0, full1, full2, full3, in_weight_ref, norm_gain_ref,
    feature_ref, in_grad_ref, scan_grad_ref, stepw_ref, stepb_ref, dr_ref, skip_grad_ref,
    norm_grad_ref, gain_grad_ref, out_grad_ref,
):
    feature_ref[...] = feature_in[...]
    inner = out_grad_ref.shape[0]
    eh = inner // LANES
    group = rank + 2 * states
    taken = [0] * 4
    lots = (full0, full1, full2, full3)

    def take(lot, height):
        at = taken[lot]
        taken[lot] += height
        return lots[lot][at : at + height, :] * grad_scale

    def take_wide(lot, out, at, height, width):
        for h in range(width // LANES):
            out[at : at + height, h * LANES : (h + 1) * LANES] = take(lot, height)

    def part(h):
        return slice(h * LANES, (h + 1) * LANES)

    small = take(0, SUB)
    for h in range(eh):
        gain_grad_ref[:, part(h)] = small[h : h + 1]
    take_wide(0, out_grad_ref, 0, inner, out_grad_ref.shape[1])
    model = in_grad_ref.shape[0]
    for h in range(eh):
        in_grad_ref[:, inner + h * LANES : inner + (h + 1) * LANES] = take(0, model)
    for p in range(2):
        lot = p + 1
        for k in range(2):
            d = 2 * p + k
            take_wide(lot, stepw_ref.at[d], 0, rank, inner)
            take_wide(lot, scan_grad_ref, d * group, rank, inner)
            take_wide(lot, scan_grad_ref, d * group + rank, 2 * states, inner)
            take_wide(lot, dr_ref.at[d], 0, states, inner)
        small = take(lot, -(-3 * eh // SUB) * SUB)
        for h in range(eh):
            for k in range(2):
                d = 2 * p + k
                skip_grad_ref[d : d + 1, part(h)] = small[h : h + 1]
                stepb_ref[d : d + 1, part(h)] = small[(k + 1) * eh + h : (k + 1) * eh + h + 1]
    take_wide(3, in_grad_ref, 0, model, inner)
    weighed = in_grad_ref[...] * in_weight_ref[...].astype(jnp.float32)
    norm_grad_ref[...] = (
        lax.dot_general(
            jnp.ones((SUB, weighed.shape[1]), jnp.float32), weighed, (((1,), (1,)), ((), ())),
            precision=HIGHEST, preferred_element_type=jnp.float32,
        )[0:1]
        / norm_gain_ref[...]
    )


def fast(
    classes, features, cotangent, table, norm_gain, in_weight, scan_weight, step_weight,
    step_bias, decay_log, skip_gain, output_gain, output_weight,
):
    tile_rows, tile_cols, model = features.shape
    inner = output_weight.shape[0]
    count = tile_rows * tile_cols
    rows, cols = lax.axis_size("row"), lax.axis_size("col")
    rank, states = step_weight.shape[1], decay_log.shape[1]
    group = rank + 2 * states
    eh = inner // LANES
    grad_scale = float(count * rows * cols) ** (-0.5)
    f32, bf16 = jnp.float32, jnp.bfloat16
    talls = (SUB * count // (tile_rows // cols), SUB * count // (tile_cols // rows))
    tall, sum_tall = max(talls), sum(talls)
    blocks = count // SUB
    lots = lots_of(rows, inner, model, states, rank, group, eh)
    per_row = ((cols, count // cols, model), (rows, count // rows, model))
    scratch = [((count, model), f32)]
    for name in range(6):
        scratch += [(per_row[0], f32), (per_row[1], f32)]
    scratch += [((blocks, SUB, inner), f32)] * 4
    scratch += [
        ((LANES, 2 * states * LANES), bf16),
        ((LANES, 2 * states * LANES // 2), bf16),
        ((4, LANES, inner), bf16),
        ((4, 2, LANES, inner), bf16),
        ((4, 2, inner, inner), bf16),
        ((2, eh, states * SUB, LANES), f32),
        ((2, count, model), bf16),
        ((2, count, 2 * inner), f32),
        ((2, count, inner), bf16),
        ((2, 2, count, LANES), f32),
        ((2, 2, eh, count, LANES), f32),
        ((2, 2, count, inner), f32),
        ((2, 2, 2 * count * states, LANES), f32),
        ((2, 2 * count * states, LANES), bf16),
        ((2, eh, 2 * count * states + states * SUB, LANES), f32),
        ((eh, sum_tall, LANES), f32),
        ((eh, sum_tall, LANES), f32),
        ((eh, tall, LANES), f32),
        ((eh, 2 * tall, LANES), f32),
        ((eh, 2 * tall, LANES), f32),
        ((2, count, LANES), f32),
        ((2, 2, eh, count, LANES), f32),
        ((tall, LANES), f32),
        ((tall, LANES), bf16),
        ((2, count, inner), f32),
        ((eh, states * SUB, LANES), f32),
        ((model, inner), f32),
    ]
    for lot in lots:
        chunk = (lot // rows, LANES)
        scratch += [((rows,) + chunk, f32), ((rows - 1,) + chunk, f32), ((cols,) + chunk, f32)]
    feature, *full = pl.pallas_call(
        functools.partial(fast_kernel, tile_rows, tile_cols, states, rank),
        out_shape=[
            jax.ShapeDtypeStruct((count, model), bf16),
        ]
        + [jax.ShapeDtypeStruct((rows, lot // rows, LANES), f32) for lot in lots],
        in_specs=[VMEM] * 13,
        out_specs=[VMEM] * 5,
        scratch_shapes=[pltpu.VMEM(*s) for s in scratch]
        + [
            pltpu.SemaphoreType.DMA((3, 2, 2)),
            pltpu.SemaphoreType.DMA((2, 2)),
            pltpu.SemaphoreType.DMA((4, 3, 2)),
        ],
        compiler_params=pltpu.CompilerParams(
            vmem_limit_bytes=BIG + 3 * 1024 * 1024, collective_id=1, has_side_effects=True
        ),
    )(
        features.reshape(count, model), classes, table, cotangent.reshape(count, model),
        norm_gain[None], in_weight, scan_weight.T,
        step_weight, step_bias, decay_log, skip_gain, output_gain[None], output_weight,
    )
    shapes = [
        ((count, model), bf16),
        (in_weight.shape, f32),
        (scan_weight.shape[::-1], f32),
        (step_weight.shape, f32),
        (step_bias.shape, f32),
        (decay_log.shape, f32),
        (skip_gain.shape, f32),
        ((1, model), f32),
        ((1, inner), f32),
        (output_weight.shape, f32),
    ]
    feature_grad, *grads = pl.pallas_call(
        functools.partial(unpack_kernel, states, rank, grad_scale),
        out_shape=[jax.ShapeDtypeStruct(*s) for s in shapes],
        in_specs=[VMEM] * 7,
        out_specs=[VMEM] * 10,
    )(
        feature, *[x.reshape(lot, LANES) for x, lot in zip(full, lots)], in_weight, norm_gain[None]
    )
    feature_grad = feature_grad.reshape(tile_rows, tile_cols, model)
    grads[1] = grads[1].T
    grads[6], grads[7] = grads[6][0], grads[7][0]
    return (feature_grad, *grads)


def local(*args):
    tile_rows, tile_cols, model = args[1].shape
    rows, cols = lax.axis_size("row"), lax.axis_size("col")
    rank, states, inner = args[7].shape[1], args[9].shape[1], args[12].shape[0]
    fits = (
        tile_rows == 4 * cols and tile_cols == 2 * rows and model == LANES and inner == 2 * LANES
        and states == 2 * SUB and rank == SUB and args[3].shape[0] <= LANES
    )
    return (fast if fits else general)(*args)


def solution(mesh):
    in_specs = (P("row", "col"), P("row", "col", None), P("row", "col", None)) + (P(),) * 10
    out_specs = (P("row", "col", None),) + (P(),) * 9
    return jax.shard_map(local, mesh=mesh, in_specs=in_specs, out_specs=out_specs, check_vma=False)
```
